32 devices in a mesh: segment: 4 (over x, core), mp: 8 (over z, y).
Axes of the slice: x: 2, y: 2, z: 4, core: 2. Of those that a mesh axis runs over, the one named last changes fastest.
Arguments:
- frames_in: bfloat16 [1024, 1536], P('mp'), may hold values from -6 to 6
- section_weights: bfloat16 [4, 1536, 1536], P('segment', 'mp'), may hold values from -0.15625 to 0.15625
- conv_kernels: bfloat16 [4, 31, 1536], P('segment'), may hold values from -1 to 1
- valid_length: int32 [1], replicated, may hold values from 512 to 1024
- out_cotangent: bfloat16 [1024, 1536], P('mp'), may hold values from -6 to 6
Outputs:
- section_outputs: bfloat16 [4, 1024, 1536], P('segment', 'mp')
- input_grads: bfloat16 [4, 1024, 1536], P('segment', 'mp')
- kernel_grads: float32 [4, 31, 1536], P('segment', None, 'mp')
The draws below stay inside these ranges and needn't reach their ends.
All inputs are finite; a program needn't handle non-finite values.
Results may differ from the reference program's by a relative error of at most 0.012.
Values may be sent and summed in bfloat16 or wider, within the bound.
A program may use at most 128 MiB of HBM per device.

```python
import jax
import jax.numpy as jnp
from jax import lax

D = 1536
KW = 31
TOKENS = 1024
N_SEGMENT = 4


def steps_of(own_key, shape, split, low, high):
    gain, own = 1.0, jax.random.fold_in(own_key, 6)
    for position, shards_of in split:
        draws = jnp.exp(jax.random.uniform(jax.random.fold_in(own, position), (shards_of,), jnp.float32, low / len(split), high / len(split)))
        gain = gain * jnp.repeat(draws, shape[position] // shards_of).reshape([-1 if axis == position else 1 for axis in range(len(shape))])
    return gain


def scatter_about(key, dims, spread, limit, cuts=(), kind=jnp.bfloat16):
    entries = jax.random.normal(key, dims, jnp.float32) * spread
    if len(cuts) > 0:
        entries = steps_of(key, dims, cuts, -0.22, 0.18) * entries
    return jnp.clip(entries, min=-limit, max=limit).astype(kind)


def setup_inputs(seed: int = 0) -> dict:
    seeds = jax.random.split(jax.random.key(seed), 6)
    frames_in = scatter_about(seeds[0], (TOKENS, D), 1.0, 6.0, ((0, 8),))
    section_weights = scatter_about(seeds[1], (N_SEGMENT, D, D), D ** -0.5, 0.15625, ((0, 4), (1, 8)))
    conv_kernels = scatter_about(seeds[2], (N_SEGMENT, KW, D), KW ** -0.5, 1.0, ((0, 4),))
    valid_length = jax.random.randint(seeds[3], (1,), TOKENS // 2, TOKENS + 1).astype(jnp.int32)
    out_cotangent = scatter_about(seeds[4], (TOKENS, D), 1.0, 6.0, ((0, 8),))
    return {"frames_in": frames_in, "section_weights": section_weights, "conv_kernels": conv_kernels, "valid_length": valid_length, "out_cotangent": out_cotangent}


EPSILON = 1e-05

def normalize(values):
    center = values - lax.optimization_barrier(jnp.mean(values, axis=-1, keepdims=True))
    inverse = lax.rsqrt(lax.optimization_barrier(jnp.mean(center * center, axis=-1, keepdims=True)) + EPSILON)
    return (center * inverse, inverse)

def tap_sum(kernel32, padded, length, forward):
    tap_count = kernel32.shape[0]
    running = jnp.zeros((length, kernel32.shape[1]), jnp.float32)
    for tap_index in range(tap_count):
        offset = tap_index if forward else tap_count - 1 - tap_index
        running = running + kernel32[tap_index] * padded[offset:offset + length].astype(jnp.float32)
    return running

def tap_grads(grad32, padded, length):
    rows_list = []
    for tap_index in range(KW):
        rows_list.append(lax.optimization_barrier(jnp.sum(grad32 * padded[tap_index:tap_index + length].astype(jnp.float32), axis=0)))
    return jnp.stack(rows_list)

def reference(frames_in, section_weights, conv_kernels, valid_length, out_cotangent):
    half_width = KW // 2
    valid_mask = (jnp.arange(TOKENS, dtype=jnp.int32) < valid_length[0]).astype(jnp.float32)[:, None]
    current = frames_in
    stored = []
    outputs = []
    for section in range(N_SEGMENT):
        kernel32 = conv_kernels[section].astype(jnp.float32)
        normed, inverse = normalize(current.astype(jnp.float32))
        masked = (normed * valid_mask).astype(jnp.bfloat16)
        padded = jnp.pad(masked, ((half_width, half_width), (0, 0)))
        conv_out = tap_sum(kernel32, padded, TOKENS, True)
        activated = (conv_out * jax.nn.sigmoid(conv_out)).astype(jnp.bfloat16)
        product = jnp.dot(activated, section_weights[section], preferred_element_type=jnp.float32)
        current = (current.astype(jnp.float32) + product).astype(jnp.bfloat16)
        stored.append((normed, inverse, padded, conv_out))
        outputs.append(current)
    upstream = out_cotangent
    input_list = [None] * N_SEGMENT
    kernel_list = [None] * N_SEGMENT
    for section in reversed(range(N_SEGMENT)):
        normed, inverse, padded, conv_out = stored[section]
        kernel32 = conv_kernels[section].astype(jnp.float32)
        grad_swish = lax.dot_general(upstream, section_weights[section], (((1,), (1,)), ((), ())), preferred_element_type=jnp.float32)
        gate_value = jax.nn.sigmoid(conv_out)
        grad_conv = (grad_swish * gate_value * (1.0 + conv_out * (1.0 - gate_value))).astype(jnp.bfloat16)
        grad_padded = jnp.pad(grad_conv, ((half_width, half_width), (0, 0)))
        grad_masked = tap_sum(kernel32, grad_padded, TOKENS, False) * valid_mask
        grad_input = inverse * (grad_masked - lax.optimization_barrier(jnp.mean(grad_masked, axis=-1, keepdims=True)) - normed * lax.optimization_barrier(jnp.mean(grad_masked * normed, axis=-1, keepdims=True)))
        upstream = (upstream.astype(jnp.float32) + grad_input).astype(jnp.bfloat16)
        input_list[section] = upstream
        kernel_list[section] = tap_grads(grad_conv.astype(jnp.float32), padded, TOKENS) * TOKENS ** (-0.5)
    return (jnp.stack(outputs), jnp.stack(input_list), jnp.stack(kernel_list))
```

```python
import functools

import jax
import jax.numpy as jnp
from jax import lax
from jax.experimental import pallas as pl
from jax.experimental.pallas import tpu as pltpu
from jax.sharding import PartitionSpec as P

EPSILON = 1e-05
PAD = 16
LANES = 128
ROWS = 16
WIDE = 256
MESH = pl.DeviceIdType.MESH
NORM_ROWS = 32
BF = jnp.bfloat16
F32 = jnp.float32

STAGES = ((0, 0), (1, 0), (2, 0), (0, 1), (1, 1), (2, 1), (0, 2), (1, 2), (2, 2), (0, 3), (1, 3),)
INNER_0 = (
    (12, 9, 10,),
    (76, 73, 74, 47, 23, 143,),
    (6, 16, 17, 111, 87, 207, 36, 81, 55, 31, 151, 70, 48, 25, 119, 215, 134, 40, 145, 95, 63, 175, 166, 80, 209, 159, 183, 231,),
    (),
    (198,),
    (112, 89, 191, 239, 247, 103, 226, 223, 127,),
    (),
    (),
    (),
    (),
    (255,),
    (),
)
INNER_1 = (
    (140, 138, 137,),
    (204, 202, 15, 151, 199,),
    (201, 175, 144, 194, 79, 135, 215, 73, 239, 130, 208, 7, 23, 221, 111, 2, 168, 39, 159, 231, 153, 255, 34, 224, 55, 31, 103, 145, 191, 98, 232, 47, 63, 71,),
    (),
    (209, 183,),
    (66, 87, 127, 167, 247, 119, 95,),
    (),
    (),
    (),
    (),
    (),
    (),
)
CORNER_0 = (4, 1, 2, 68, 65, 39, 199, 34, 103, 135, 96, 66, 167, 130, 162, 194, 98,)
CORNER_1 = (133, 196, 194, 128, 130, 193, 7, 167, 2, 160, 71, 230, 102, 66, 162,)
SENDS = 24


def decode(event):
    return event // 64, event // 32 % 2, event // 8 % 4, event // 4 % 2, event % 4


def spread(
    x_any, w_any, k_any, vl_ref, cot_any,
    out_whole, gin_whole, kg_out,
    w, a, up, norm, inv, pm, pg, act, slope, gs, k_bf, k_ref, kg, kg_land,
    local_sem, x_send, x_recv, k_send, k_recv, own_send, rel_send, rel_recv, sib_send, sib_recv,
    halo_send, halo_recv, out_send, out_recv, gin_send, gin_recv, kg_send, kg_recv,
):
    n_sec, rows_in, width = w.shape
    part = a.shape[1]
    taps = k_ref.shape[1]
    seg, mp = lax.axis_index("segment"), lax.axis_index("mp")
    n_seg, n_mp = lax.axis_size("segment"), lax.axis_size("mp")
    own = rows_in // n_mp
    half = own // 2
    chunks = width // LANES
    tiles = width // WIDE
    x, c = lax.div(seg, 2), lax.rem(seg, 2)
    z, y = lax.div(mp, 2), lax.rem(mp, 2)
    inner = (z == 1) | (z == 2)
    block = jnp.where(z == 1, jnp.where(x == 0, y, 3 - y), jnp.where(x == 1, 4 + y, 7 - y))
    chunk_id = 2 * block + c

    def place(number):
        far = ((number >= 2) & (number < 6)) * 1
        side = ((number == 1) | (number == 2) | (number == 5) | (number == 6)) * 1
        return far, (number >= 4) * 2 + 2 + side

    def device_of(number, core):
        far, to = place(number)
        return 2 * far + core, to

    barrier = pltpu.get_barrier_semaphore()
    me = seg * n_mp + mp
    total = n_seg * n_mp

    @pl.loop(1, total)
    def _(by):
        other = lax.rem(me + by, total)
        pl.semaphore_signal(
            barrier, inc=1, device_id=(lax.div(other, n_mp), lax.rem(other, n_mp)), device_id_type=MESH
        )

    w_copy = pltpu.make_async_copy(
        w_any, w.at[seg, pl.ds(pl.multiple_of(own * mp, own), own)], local_sem.at[0]
    )
    k_copy = pltpu.make_async_copy(k_any, k_bf.at[seg], local_sem.at[1])
    w_copy.start()

    @pl.when(inner)
    def _():
        k_copy.start()

    pl.semaphore_wait(barrier, total - 1)

    def half_ref(section, shard, core):
        return w.at[section, pl.ds(pl.multiple_of(own * shard + half * core, half), half)]

    def own_copy(kind):
        core = c if kind else 1 - c
        return pltpu.make_async_remote_copy(
            src_ref=half_ref(seg, mp, core), dst_ref=half_ref(seg, mp, core),
            send_sem=own_send.at[kind],
            recv_sem=(sib_recv if kind else rel_recv).at[seg * n_mp + mp],
            device_id={"segment": seg + 1 - 2 * c}, device_id_type=MESH,
        )

    def relay_copy(section, shard, way, slot):
        target = (
            {"segment": seg + 2 - 4 * x}, {"mp": mp + 1 - 2 * y}, {"mp": mp + jnp.where(z < 2, 2, -2)}
        )[way]
        return pltpu.make_async_remote_copy(
            src_ref=half_ref(section, shard, c), dst_ref=half_ref(section, shard, c),
            send_sem=rel_send.at[slot], recv_sem=rel_recv.at[section * n_mp + shard],
            device_id=target, device_id_type=MESH,
        )

    def sib_copy(section, shard, core):
        return pltpu.make_async_remote_copy(
            src_ref=half_ref(section, shard, core), dst_ref=half_ref(section, shard, core),
            send_sem=sib_send.at[section * n_mp + shard], recv_sem=sib_recv.at[section * n_mp + shard],
            device_id={"segment": seg + 1 - 2 * c}, device_id_type=MESH,
        )

    def shard_of(across, depth):
        from_y = 1 - y if across else y
        return 2 * jnp.where(z < 2, depth, 3 - depth) + from_y

    def is_home(section, across, depth, plane, corner):
        return section // 2 == plane and across == 0 and depth == (0 if corner else 1)

    def run_events(events, plane, corner, slot):
        for event in events:
            section, across, depth, first, way = decode(event)
            shard = shard_of(across, depth)
            if first and is_home(section, across, depth, plane, corner):
                pl.when(c != section % 2)(
                    lambda: relay_copy(section, shard, 0, 0).wait_recv()
                )
            elif first:
                relay_copy(section, shard, 0, 0).wait_recv()
                if not corner:
                    sib_copy(section, shard, c).start()
            if way < 3:
                relay_copy(section, shard, way, slot).start()
                slot += 1
        return slot

    def finish_events(groups, plane, corner):
        slot = 0
        for events in groups:
            for event in events:
                section, across, depth, first, way = decode(event)
                shard = shard_of(across, depth)
                if first and not corner and not is_home(section, across, depth, plane, corner):
                    sib_copy(section, shard, c).wait_send()
                if way < 3:
                    relay_copy(section, shard, way, slot).wait_send()
                    slot += 1

    def siblings(section, plane):
        for across in range(2):
            for depth in range(4):
                shard = shard_of(across, depth)
                wait = sib_copy(section, shard, 1 - c).wait_recv
                if is_home(section, across, depth, plane, False):
                    pl.when(c != section % 2)(wait)
                else:
                    wait()

    far_of_block, to_mp = place(mp)
    sends_x = x == far_of_block
    stays = to_mp == mp

    def x_move(index, remote):
        rows = pl.ds(pl.multiple_of(part * c, part), part)
        source, target = ((x_any, a.at[0]), (cot_any, up.at[n_sec]))[index]
        if not remote:
            return pltpu.make_async_copy(source.at[rows], target, x_recv.at[index])
        return pltpu.make_async_remote_copy(
            src_ref=source.at[rows], dst_ref=target, send_sem=x_send.at[index], recv_sem=x_recv.at[index],
            device_id={"mp": to_mp}, device_id_type=MESH,
        )

    def x_start(index):
        pl.when(sends_x & stays)(lambda: x_move(index, False).start())
        pl.when(sends_x & (to_mp != mp))(lambda: x_move(index, True).start())

    def x_wait(index):
        here = (block == mp) & sends_x
        pl.when(here)(lambda: x_move(index, False).wait())
        pl.when(jnp.logical_not(here))(lambda: x_move(index, True).wait_recv())

    def k_move(by, sender):
        return pltpu.make_async_remote_copy(
            src_ref=k_any, dst_ref=k_bf.at[sender], send_sem=k_send.at[by - 1], recv_sem=k_recv.at[sender],
            device_id={"segment": lax.rem(seg + by, n_seg)}, device_id_type=MESH,
        )

    w_copy.wait()
    own_copy(0).start()
    pl.when(inner)(lambda: own_copy(1).start())

    @pl.when(inner)
    def _():
        for by in range(1, n_sec):
            k_move(by, seg).start()

    x_start(0)

    corner = jnp.logical_not(inner)
    for plane, table in ((0, CORNER_0), (1, CORNER_1)):

        @pl.when(corner & (x == plane))
        def _():
            run_events(table, plane, True, 0)

    x_start(1)

    def mask_rows(start, count):
        position = chunk_id * part + start + lax.broadcasted_iota(jnp.int32, (count, LANES), 0)
        return (position < vl_ref[0]).astype(F32)

    def halo_copy(pad_ref, section, slot, to_next):
        rows_from = pl.ds(part, PAD) if to_next else pl.ds(PAD, PAD)
        rows_to = pl.ds(0, PAD) if to_next else pl.ds(part + PAD, PAD)
        if to_next:
            away_seg, away_mp = device_of(block + 1, 0)
            target = (jnp.where(c == 0, seg + 1, away_seg), jnp.where(c == 0, mp, away_mp))
        else:
            away_seg, away_mp = device_of(block - 1, 1)
            target = (jnp.where(c == 1, seg - 1, away_seg), jnp.where(c == 1, mp, away_mp))
        sem = 4 * section + slot + (0 if to_next else 1)
        return pltpu.make_async_remote_copy(
            src_ref=pad_ref.at[section, rows_from], dst_ref=pad_ref.at[section, rows_to],
            send_sem=halo_send.at[sem], recv_sem=halo_recv.at[sem],
            device_id=target, device_id_type=MESH,
        )

    last = 2 * n_mp - 1

    def halo_start(pad_ref, section, slot):
        pl.when(chunk_id < last)(lambda: halo_copy(pad_ref, section, slot, True).start())
        pl.when(chunk_id > 0)(lambda: halo_copy(pad_ref, section, slot, False).start())

    def halo_wait(pad_ref, section, slot):
        pl.when(chunk_id > 0)(lambda: halo_copy(pad_ref, section, slot, True).wait_recv())
        pl.when(chunk_id < last)(lambda: halo_copy(pad_ref, section, slot, False).wait_recv())

    def halo_sent(pad_ref, section, slot):
        pl.when(chunk_id < last)(lambda: halo_copy(pad_ref, section, slot, True).wait_send())
        pl.when(chunk_id > 0)(lambda: halo_copy(pad_ref, section, slot, False).wait_send())

    def tap_sum(padded, section, columns, forward):
        rows = padded.shape[0]
        running = jnp.zeros((part, LANES), F32)
        for r in range(8):
            moved = padded if r == 0 else pltpu.roll(padded, rows - r, 0)
            for base in range(0, 2 * PAD, 8):
                offset = base + r
                if 1 <= offset <= taps:
                    tap = offset - 1 if forward else taps - offset
                    running = running + k_ref[section, tap : tap + 1, columns] * moved[base : base + part]
        return running

    def normalize(section):
        for start in range(0, part, NORM_ROWS):
            rows = slice(start, start + NORM_ROWS)
            values = a[section, rows].astype(F32)
            center = values - jnp.mean(values, axis=-1, keepdims=True)
            inverse = lax.rsqrt(jnp.mean(center * center, axis=-1, keepdims=True) + EPSILON)
            normed = center * inverse
            norm[section, rows] = normed
            inv[section, rows] = jnp.broadcast_to(inverse, (NORM_ROWS, LANES))
            pm[section, PAD + start : PAD + start + NORM_ROWS] = (
                normed * mask_rows(start, NORM_ROWS)[:, :1]
            ).astype(BF)
        halo_start(pm, section, 0)

    def convolve(section):
        halo_wait(pm, section, 0)

        @pl.loop(0, chunks)
        def _(chunk):
            columns = pl.ds(pl.multiple_of(chunk * LANES, LANES), LANES)
            conv = tap_sum(pm[section, :, columns].astype(F32), section, columns, True)
            gate = jax.nn.sigmoid(conv)
            act[section, :, columns] = (conv * gate).astype(BF)
            slope[section, :, columns] = gate * (1.0 + conv * (1.0 - gate))

    def result_copy(source, section, whole, core, send, recv, remote):
        rows = pl.ds(pl.multiple_of(part * core, part), part)
        if not remote:
            return pltpu.make_async_copy(source.at[section], whole.at[0, rows], recv.at[core])
        return pltpu.make_async_remote_copy(
            src_ref=source.at[section], dst_ref=whole.at[0, rows],
            send_sem=send.at[section], recv_sem=recv.at[core],
            device_id=(section, block), device_id_type=MESH,
        )

    def result_start(source, index, section, whole, send, recv):
        same = (seg == section) & (mp == block)
        def local():
            rows = pl.ds(pl.multiple_of(part * c, part), part)
            pltpu.make_async_copy(source.at[index], whole.at[0, rows], recv.at[c]).start()
        def remote():
            rows = pl.ds(pl.multiple_of(part * c, part), part)
            pltpu.make_async_remote_copy(
                src_ref=source.at[index], dst_ref=whole.at[0, rows],
                send_sem=send.at[section], recv_sem=recv.at[c],
                device_id=(section, block), device_id_type=MESH,
            ).start()
        pl.when(same)(local)
        pl.when(jnp.logical_not(same))(remote)

    def result_sent(source, index, section, whole, send, recv):
        same = (seg == section) & (mp == block)
        @pl.when(jnp.logical_not(same))
        def _():
            rows = pl.ds(pl.multiple_of(part * c, part), part)
            pltpu.make_async_remote_copy(
                src_ref=source.at[index], dst_ref=whole.at[0, rows],
                send_sem=send.at[section], recv_sem=recv.at[c],
                device_id=(section, block), device_id_type=MESH,
            ).wait_send()

    def result_wait(source, whole, send, recv):
        for core in range(2):
            from_seg, from_mp = device_of(mp, core)
            same = (seg == from_seg) & (mp == from_mp)
            rows = pl.ds(part * core, part)
            @pl.when(same)
            def _():
                pltpu.make_async_copy(source.at[0], whole.at[0, rows], recv.at[core]).wait()
            @pl.when(jnp.logical_not(same))
            def _():
                pltpu.make_async_remote_copy(
                    src_ref=source.at[0], dst_ref=whole.at[0, rows],
                    send_sem=send.at[0], recv_sem=recv.at[core],
                    device_id=(seg, mp), device_id_type=MESH,
                ).wait_recv()

    def product(section):
        for tile in range(tiles):
            columns = slice(tile * WIDE, (tile + 1) * WIDE)
            result = jnp.dot(act[section], w[section, :, columns], preferred_element_type=F32)
            a[section + 1, :, columns] = (a[section, :, columns].astype(F32) + result).astype(BF)
        result_start(a, section + 1, section, out_whole, out_send, out_recv)

    def forward_stage(kind, section):
        if kind == 0:
            if section == 0:
                x_wait(0)
                k_copy.wait()
                for by in range(1, n_sec):
                    k_move(by, lax.rem(seg + n_seg - by, n_seg)).wait_recv()
                for s in range(n_sec):
                    k_ref[s] = k_bf[s].astype(F32)
                for pad_ref in (pm, pg):

                    @pl.when(chunk_id == 0)
                    def _():
                        for s in range(n_sec):
                            pad_ref[s, 0:PAD, :] = jnp.zeros((PAD, width), BF)

                    @pl.when(chunk_id == last)
                    def _():
                        for s in range(n_sec):
                            pad_ref[s, part + PAD : part + 2 * PAD, :] = jnp.zeros((PAD, width), BF)

                kg[:, taps:, :] = jnp.zeros((n_sec, kg.shape[1] - taps, width), F32)
            normalize(section)
        elif kind == 1:
            convolve(section)
        else:
            for plane in range(2):
                pl.when(x == plane)(lambda: siblings(section, plane))
            product(section)

    def kg_copy(section, target, remote):
        start = 384 * (target // 2) + 128 * (target % 2)
        window = pl.ds(start, 2 * LANES)
        if not remote:
            return pltpu.make_async_copy(kg.at[section, :, window], kg_land.at[chunk_id], kg_recv.at[chunk_id])
        return pltpu.make_async_remote_copy(
            src_ref=kg.at[section, :, window], dst_ref=kg_land.at[chunk_id],
            send_sem=kg_send.at[section * n_mp + target], recv_sem=kg_recv.at[chunk_id],
            device_id=(section, target), device_id_type=MESH,
        )

    def tap_grads(section):
        @pl.loop(0, chunks)
        def _(chunk):
            columns = pl.ds(pl.multiple_of(chunk * LANES, LANES), LANES)
            padded = pm[section, :, columns].astype(F32)
            grad = pg[section, PAD : PAD + part, columns].astype(F32)
            rows = padded.shape[0]
            for r in range(8):
                moved = padded if r == 0 else pltpu.roll(padded, rows - r, 0)
                for base in range(0, 2 * PAD, 8):
                    tap = base + r - 1
                    if 0 <= tap < taps:
                        kg[section, tap : tap + 1, columns] = jnp.sum(
                            grad * moved[base : base + part], axis=0, keepdims=True
                        )

        for target in range(n_mp):
            same = (seg == section) & (mp == target)
            pl.when(same)(lambda: kg_copy(section, target, False).start())
            pl.when(jnp.logical_not(same))(lambda: kg_copy(section, target, True).start())

    def backward(section):
        for tile in range(tiles):
            columns = slice(tile * WIDE, (tile + 1) * WIDE)
            grad = lax.dot_general(
                up[section + 1], w[section, columns, :], (((1,), (1,)), ((), ())),
                preferred_element_type=F32,
            )
            pg[section, PAD : PAD + part, columns] = (grad * slope[section, :, columns]).astype(BF)
        halo_start(pg, section, 2)
        tap_grads(section)
        if section == n_sec - 1:
            product(section)
        halo_wait(pg, section, 2)

        @pl.loop(0, chunks)
        def _(chunk):
            columns = pl.ds(pl.multiple_of(chunk * LANES, LANES), LANES)
            gs[:, columns] = tap_sum(
                pg[section, :, columns].astype(F32), section, columns, False
            ) * mask_rows(0, part)

        for start in range(0, part, NORM_ROWS):
            rows = slice(start, start + NORM_ROWS)
            masked = gs[rows]
            normed = norm[section, rows]
            first = jnp.mean(masked, axis=-1, keepdims=True)
            second = jnp.mean(masked * normed, axis=-1, keepdims=True)
            grad = inv[section, rows][:, :1] * (masked - first - normed * second)
            up[section, rows] = (up[section + 1, rows].astype(F32) + grad).astype(BF)
        result_start(up, section, section, gin_whole, gin_send, gin_recv)

    slots = [0, 0]
    for index, (kind, section) in enumerate(STAGES):
        for plane, table in ((0, INNER_0), (1, INNER_1)):
            if table[index]:
                start = slots[plane]

                @pl.when(inner & (x == plane))
                def _():
                    run_events(table[index], plane, False, start)

                slots[plane] += sum(event % 4 < 3 for event in table[index])
        pl.when(inner)(lambda: forward_stage(kind, section))
    for plane, table in ((0, INNER_0), (1, INNER_1)):
        start = slots[plane]

        @pl.when(inner & (x == plane))
        def _():
            run_events(table[len(STAGES)], plane, False, start)
            siblings(n_sec - 1, plane)

    @pl.when(inner)
    def _():
        x_wait(1)
        for section in reversed(range(n_sec)):
            backward(section)

    window = pl.ds(0, 2 * LANES)
    sums = jnp.zeros((kg.shape[1], 2 * LANES), F32)
    for number in range(2 * n_mp):
        from_seg, from_mp = device_of(number // 2, number % 2)
        same = (seg == from_seg) & (mp == from_mp)

        @pl.when(same)
        def _():
            pltpu.make_async_copy(
                kg.at[0, :, window], kg_land.at[number], kg_recv.at[number]
            ).wait()

        @pl.when(jnp.logical_not(same))
        def _():
            pltpu.make_async_remote_copy(
                src_ref=kg.at[0, :, window], dst_ref=kg_land.at[number],
                send_sem=kg_send.at[0], recv_sem=kg_recv.at[number],
                device_id=(seg, mp), device_id_type=MESH,
            ).wait_recv()

        sums = sums + kg_land[number]
    scale = (2 * part * n_mp) ** (-0.5)
    even, odd = sums[:taps, :own], sums[:taps, 2 * LANES - own :]
    kg_out[0] = jnp.where(y == 0, even, odd) * scale

    result_wait(a, out_whole, out_send, out_recv)
    result_wait(up, gin_whole, gin_send, gin_recv)

    own_copy(0).wait_send()
    for index in range(2):
        pl.when(sends_x & (to_mp != mp))(lambda: x_move(index, True).wait_send())
    for plane, table in ((0, CORNER_0), (1, CORNER_1)):
        pl.when(corner & (x == plane))(lambda: finish_events((table,), plane, True))
    for plane, table in ((0, INNER_0), (1, INNER_1)):
        pl.when(inner & (x == plane))(lambda: finish_events(table, plane, False))

    @pl.when(inner)
    def _():
        own_copy(1).wait_send()
        for by in range(1, n_sec):
            k_move(by, seg).wait_send()
        for section in range(n_sec):
            halo_sent(pm, section, 0)
            halo_sent(pg, section, 2)
            result_sent(a, section + 1, section, out_whole, out_send, out_recv)
            result_sent(up, section, section, gin_whole, gin_send, gin_recv)
            for target in range(n_mp):
                same = (seg == section) & (mp == target)
                pl.when(jnp.logical_not(same))(lambda: kg_copy(section, target, True).wait_send())


def spread_call(frames_in, section_weights, conv_kernels, valid_length, out_cotangent):
    frames, width = frames_in.shape
    taps = conv_kernels.shape[1]
    n_sec, n_mp = lax.axis_size("segment"), lax.axis_size("mp")
    own = width // n_mp
    part = frames // 2
    vmem = pl.BlockSpec(memory_space=pltpu.VMEM)
    smem = pl.BlockSpec(memory_space=pltpu.SMEM)
    whole = pl.BlockSpec(memory_space=pl.ANY)
    tap_rows = -(-taps // 8) * 8
    dma = pltpu.SemaphoreType.DMA
    return pl.pallas_call(
        spread,
        out_shape=(
            jax.ShapeDtypeStruct((1, frames, width), BF),
            jax.ShapeDtypeStruct((1, frames, width), BF),
            jax.ShapeDtypeStruct((1, taps, own), F32),
        ),
        in_specs=[whole, whole, whole, smem, whole],
        out_specs=(whole, whole, vmem),
        scratch_shapes=[
            pltpu.VMEM((n_sec, width, width), BF),
            pltpu.VMEM((n_sec + 1, part, width), BF),
            pltpu.VMEM((n_sec + 1, part, width), BF),
            pltpu.VMEM((n_sec, part, width), F32),
            pltpu.VMEM((n_sec, part, LANES), F32),
            pltpu.VMEM((n_sec, part + 2 * PAD, width), BF),
            pltpu.VMEM((n_sec, part + 2 * PAD, width), BF),
            pltpu.VMEM((n_sec, part, width), BF),
            pltpu.VMEM((n_sec, part, width), F32),
            pltpu.VMEM((part, width), F32),
            pltpu.VMEM((n_sec, taps, width), BF),
            pltpu.VMEM((n_sec, taps, width), F32),
            pltpu.VMEM((n_sec, tap_rows, width), F32),
            pltpu.VMEM((2 * n_mp, tap_rows, 2 * LANES), F32),
            dma((2,)), dma((2,)), dma((2,)), dma((n_sec - 1,)), dma((n_sec,)),
            dma((2,)), dma((SENDS,)), dma((n_sec * n_mp,)), dma((n_sec * n_mp,)), dma((n_sec * n_mp,)),
            dma((4 * n_sec,)), dma((4 * n_sec,)),
            dma((n_sec,)), dma((2,)), dma((n_sec,)), dma((2,)),
            dma((n_sec * n_mp,)), dma((2 * n_mp,)),
        ],
        compiler_params=pltpu.CompilerParams(
            collective_id=1, has_side_effects=True, vmem_limit_bytes=60 * 2**20
        ),
    )(frames_in, section_weights[0], conv_kernels[0], valid_length, out_cotangent)


def cascade(
    relay, x_any, w_any, k_any, vl_ref, cot_any,
    out_whole, gin_whole, kg_out,
    cur, up, norm, inv, pm, pg, act, slope, gs, out_ref, gin_ref, w_ref, k_bf, k_ref, kg_ref, kg_land,
    halo_send, halo_recv, in_send, in_recv, up_send, up_recv,
    local_sem, w_send, w_recv, end_send, end_recv, kg_send, kg_recv, turn_sem,
):
    frames, width = x_any.shape
    taps = k_ref.shape[0]
    seg, mp = lax.axis_index("segment"), lax.axis_index("mp")
    n_seg, n_mp = lax.axis_size("segment"), lax.axis_size("mp")
    chunks = width // LANES
    blocks = frames // ROWS
    tiles = width // WIDE

    barrier = pltpu.get_barrier_semaphore()
    steps_mp = range(1, n_mp) if relay else (1, n_mp - 1)
    for axis, index, count, steps in (
        ("segment", seg, n_seg, (1, n_seg - 1)), ("mp", mp, n_mp, steps_mp)
    ):
        for by in steps:
            pl.semaphore_signal(
                barrier, inc=1, device_id={axis: lax.rem(index + by, count)}, device_id_type=MESH
            )
    own = width // n_mp
    w_rows = pl.ds(pl.multiple_of(mp * own, own), own) if relay else pl.ds(0, width)
    w_copy = pltpu.make_async_copy(w_any, w_ref.at[w_rows], local_sem.at[0])
    x_copy = pltpu.make_async_copy(x_any, cur, local_sem.at[1])
    cot_copy = pltpu.make_async_copy(cot_any, up, local_sem.at[2])
    k_copy = pltpu.make_async_copy(k_any, k_bf, local_sem.at[3])
    out_copy = pltpu.make_async_copy(out_ref, out_whole.at[0], local_sem.at[4])
    gin_copy = pltpu.make_async_copy(gin_ref, gin_whole.at[0], local_sem.at[5])
    w_copy.start()
    k_copy.start()

    @pl.when(seg == 0)
    def _():
        x_copy.start()

    @pl.when(seg == n_seg - 1)
    def _():
        cot_copy.start()

    pl.semaphore_wait(barrier, 2 + len(steps_mp))

    row, column = lax.div(mp, 2), lax.rem(mp, 2)
    n_row = n_mp // 2

    half = own // 2

    def block_copy(block, way, count=own):
        rows = pl.ds(pl.multiple_of(block * own, own), count)
        target = (mp + 2, mp - 2, mp + 1 - 2 * column)[way]
        return pltpu.make_async_remote_copy(
            src_ref=w_ref.at[rows], dst_ref=w_ref.at[rows],
            send_sem=w_send.at[way, block], recv_sem=w_recv.at[block],
            device_id={"mp": target}, device_id_type=MESH,
        )

    def end_copy(way):
        block = (0 if way == 0 else n_mp - 2) + 1 - column
        rows = pl.ds(pl.multiple_of(block * own + half, half), half)
        return pltpu.make_async_remote_copy(
            src_ref=w_ref.at[rows], dst_ref=w_ref.at[rows],
            send_sem=end_send.at[way], recv_sem=end_recv.at[way],
            device_id={"mp": mp + 2 if way == 0 else mp - 2}, device_id_type=MESH,
        )

    def each_block(distance, act_on, arrive):
        if distance == 0:
            pl.when(row < n_row - 1)(lambda: act_on(mp, 0))
            pl.when(row > 0)(lambda: act_on(mp, 1))
            act_on(mp, 2)
            return
        low, high = mp - 2 * distance, mp + 2 * distance

        @pl.when(row >= distance)
        def _():
            arrive(low)
            pl.when(row < n_row - 1)(lambda: act_on(low, 0))
            pl.when(row == distance)(lambda: act_on(low, 2, half))
            pl.when(row > distance)(lambda: act_on(low, 2))

        @pl.when(row + distance < n_row)
        def _():
            arrive(high)
            pl.when(row > 0)(lambda: act_on(high, 1))
            pl.when(row + distance == n_row - 1)(lambda: act_on(high, 2, half))
            pl.when(row + distance < n_row - 1)(lambda: act_on(high, 2))

    def pass_on(distance):
        each_block(
            distance,
            lambda *what: block_copy(*what).start(),
            lambda block: block_copy(block, 0).wait_recv(),
        )
        if distance == 1:
            for way, end in ((0, 0), (1, n_row - 1)):

                @pl.when(row == end)
                def _():
                    block_copy(2 * end + 1 - column, 2).wait_recv()
                    end_copy(way).start()

    def passed():
        for distance in range(n_row):
            each_block(
                distance,
                lambda *what: block_copy(*what).wait_send(),
                lambda block: None,
            )
        pl.when(row < n_row - 1)(lambda: end_copy(0).wait_send())
        pl.when(row > 0)(lambda: end_copy(1).wait_send())

    def gather_rest(first):
        if relay:
            for distance in range(first, n_row):
                pass_on(distance)

            @pl.when(row > 0)
            def _():
                end_copy(0).wait_recv()
                pl.when(row < n_row - 1)(lambda: end_copy(0).start())

            @pl.when(row < n_row - 1)
            def _():
                end_copy(1).wait_recv()
                pl.when(row > 0)(lambda: end_copy(1).start())

            for index in range(n_row):
                block = index * 2 + 1 - column
                if index in (0, n_row - 1):
                    pl.when(row != index)(lambda: block_copy(block, 2, half).wait_recv())
                else:
                    block_copy(block, 2).wait_recv()

    def kg_copy(target, sender):
        start = 384 * lax.div(target, 2) + 128 * lax.rem(target, 2)
        window = pl.ds(pl.multiple_of(start, LANES), 2 * LANES)
        return pltpu.make_async_remote_copy(
            src_ref=kg_ref.at[:, window], dst_ref=kg_land.at[sender],
            send_sem=kg_send.at[target], recv_sem=kg_recv.at[sender],
            device_id={"mp": target}, device_id_type=MESH,
        )

    w_copy.wait()
    if relay:

        @pl.when(seg != 1)
        def _():
            pass_on(0)

    k_copy.wait()
    k_ref[...] = k_bf[...].astype(F32)
    kg_ref[...] = jnp.zeros(kg_ref.shape, F32)

    def halo_copy(pad_ref, first, to_right):
        rows_from = pl.ds(frames, PAD) if to_right else pl.ds(PAD, PAD)
        rows_to = pl.ds(0, PAD) if to_right else pl.ds(frames + PAD, PAD)
        target = lax.rem(mp + (1 if to_right else n_mp - 1), n_mp)
        slot = first + (0 if to_right else 1)
        return pltpu.make_async_remote_copy(
            src_ref=pad_ref.at[rows_from], dst_ref=pad_ref.at[rows_to],
            send_sem=halo_send.at[slot], recv_sem=halo_recv.at[slot],
            device_id={"mp": target}, device_id_type=MESH,
        )

    def halo_start(pad_ref, first):
        @pl.when(mp < n_mp - 1)
        def _():
            halo_copy(pad_ref, first, True).start()

        @pl.when(mp > 0)
        def _():
            halo_copy(pad_ref, first, False).start()

    def halo_wait(pad_ref, first):
        @pl.when(mp > 0)
        def _():
            halo_copy(pad_ref, first, True).wait_recv()

        @pl.when(mp < n_mp - 1)
        def _():
            halo_copy(pad_ref, first, False).wait_recv()

    def halo_sent(pad_ref, first):
        @pl.when(mp < n_mp - 1)
        def _():
            halo_copy(pad_ref, first, True).wait_send()

        @pl.when(mp > 0)
        def _():
            halo_copy(pad_ref, first, False).wait_send()

    def halo_clear(pad_ref):
        @pl.when(mp == 0)
        def _():
            pad_ref[0:PAD, :] = jnp.zeros((PAD, width), BF)

        @pl.when(mp == n_mp - 1)
        def _():
            pad_ref[frames + PAD : frames + 2 * PAD, :] = jnp.zeros((PAD, width), BF)

    def in_copy(tile):
        columns = pl.ds(tile * WIDE, WIDE)
        return pltpu.make_async_remote_copy(
            src_ref=out_ref.at[:, columns], dst_ref=cur.at[:, columns],
            send_sem=in_send.at[tile], recv_sem=in_recv.at[tile],
            device_id={"segment": lax.rem(seg + 1, n_seg)}, device_id_type=MESH,
        )

    def up_copy(block):
        rows = pl.ds(block * ROWS, ROWS)
        return pltpu.make_async_remote_copy(
            src_ref=gin_ref.at[rows], dst_ref=up.at[rows],
            send_sem=up_send.at[block], recv_sem=up_recv.at[block],
            device_id={"segment": lax.rem(seg + n_seg - 1, n_seg)}, device_id_type=MESH,
        )

    def mask_rows(start, count):
        position = mp * frames + start + lax.broadcasted_iota(jnp.int32, (count, LANES), 0)
        return (position < vl_ref[0]).astype(F32)

    def back_product():
        for tile in range(tiles):
            columns = slice(tile * WIDE, (tile + 1) * WIDE)
            gs[:, columns] = lax.dot_general(
                up[...], w_ref[columns, :], (((1,), (1,)), ((), ())), preferred_element_type=F32
            )

    halo_clear(pm)
    halo_clear(pg)

    @pl.when(seg == n_seg - 1)
    def _():
        gather_rest(1)
        cot_copy.wait()
        back_product()

    @pl.when(seg == 0)
    def _():
        x_copy.wait()

    @pl.when(seg == 1)
    def _():
        if relay:
            pl.semaphore_wait(turn_sem, 1)
            pass_on(0)

    @pl.when((seg > 1) & (seg < n_seg - 1))
    def _():
        gather_rest(1)

    @pl.when(seg > 0)
    def _():
        for tile in range(tiles):
            in_copy(tile).wait_recv()

    def norm_rows(block):
        start = pl.multiple_of(block * ROWS, ROWS)
        rows = pl.ds(start, ROWS)
        values = cur[rows, :].astype(F32)
        center = values - jnp.mean(values, axis=-1, keepdims=True)
        inverse = lax.rsqrt(jnp.mean(center * center, axis=-1, keepdims=True) + EPSILON)
        normed = center * inverse
        norm[rows, :] = normed
        inv[rows, :] = jnp.broadcast_to(inverse, (ROWS, LANES))
        pm[pl.ds(pl.multiple_of(PAD + start, ROWS), ROWS), :] = (
            normed * mask_rows(start, ROWS)[:, :1]
        ).astype(BF)

    norm_rows(0)
    norm_rows(blocks - 1)
    halo_start(pm, 0)

    @pl.loop(1, blocks - 1)
    def _(block):
        norm_rows(block)

    if relay:

        @pl.when(seg < 2)
        def _():
            pass_on(1)

    halo_wait(pm, 0)

    def shifted(padded):
        total = padded.shape[0]
        return [padded if r == 0 else pltpu.roll(padded, total - r, 0) for r in range(8)]

    def tap_sum(padded, columns, forward):
        total = padded.shape[0]
        running = jnp.zeros((frames, LANES), F32)
        for r in range(8):
            moved = padded if r == 0 else pltpu.roll(padded, total - r, 0)
            for base in range(0, 2 * PAD, 8):
                offset = base + r
                if 1 <= offset <= taps:
                    tap = offset - 1 if forward else taps - offset
                    running = running + k_ref[tap : tap + 1, columns] * moved[base : base + frames]
        return running

    @pl.loop(0, chunks)
    def _(chunk):
        columns = pl.ds(pl.multiple_of(chunk * LANES, LANES), LANES)
        conv = tap_sum(pm[:, columns].astype(F32), columns, True)
        gate = jax.nn.sigmoid(conv)
        act[:, columns] = (conv * gate).astype(BF)
        slope[:, columns] = gate * (1.0 + conv * (1.0 - gate))

    if relay:

        @pl.when(seg < 2)
        def _():
            pass_on(2)

        @pl.when(seg == 0)
        def _():
            pl.semaphore_signal(
                turn_sem, inc=1, device_id={"segment": seg + 1}, device_id_type=MESH
            )

        @pl.when(seg < 2)
        def _():
            gather_rest(3)

    for tile in range(tiles):
        columns = slice(tile * WIDE, (tile + 1) * WIDE)
        product = jnp.dot(act[...], w_ref[:, columns], preferred_element_type=F32)
        out_ref[:, columns] = (cur[:, columns].astype(F32) + product).astype(BF)

        @pl.when(seg < n_seg - 1)
        def _():
            in_copy(tile).start()

    out_copy.start()

    @pl.when(seg < n_seg - 1)
    def _():
        for block in range(blocks):
            up_copy(block).wait_recv()
        back_product()

    def grad_rows(block):
        start = pl.multiple_of(block * ROWS, ROWS)
        rows = pl.ds(start, ROWS)
        pg[pl.ds(pl.multiple_of(PAD + start, ROWS), ROWS), :] = (
            gs[rows, :] * slope[rows, :]
        ).astype(BF)

    grad_rows(0)
    grad_rows(blocks - 1)
    halo_start(pg, 2)

    @pl.loop(1, blocks - 1)
    def _(block):
        grad_rows(block)

    kg_start = 384 * row + 128 * column
    kg_window = pl.ds(pl.multiple_of(kg_start, LANES), 2 * LANES)

    def tap_grads():
        @pl.loop(0, chunks)
        def _(chunk):
            columns = pl.ds(pl.multiple_of(chunk * LANES, LANES), LANES)
            padded = pm[:, columns].astype(F32)
            grad = pg[PAD : PAD + frames, columns].astype(F32)
            total = padded.shape[0]
            for r in range(8):
                moved = padded if r == 0 else pltpu.roll(padded, total - r, 0)
                for base in range(0, 2 * PAD, 8):
                    tap = base + r - 1
                    if 0 <= tap < taps:
                        kg_ref[tap : tap + 1, columns] = jnp.sum(
                            grad * moved[base : base + frames], axis=0, keepdims=True
                        )

        if relay:
            for by in range(1, n_mp):
                kg_copy(lax.rem(mp + by, n_mp), mp).start()

    @pl.when(seg == 0)
    def _():
        tap_grads()

    halo_wait(pg, 2)

    @pl.loop(0, chunks)
    def _(chunk):
        columns = pl.ds(pl.multiple_of(chunk * LANES, LANES), LANES)
        gs[:, columns] = tap_sum(pg[:, columns].astype(F32), columns, False) * mask_rows(0, frames)

    @pl.loop(0, blocks)
    def _(block):
        rows = pl.ds(pl.multiple_of(block * ROWS, ROWS), ROWS)
        masked = gs[rows, :]
        normed = norm[rows, :]
        first = jnp.mean(masked, axis=-1, keepdims=True)
        second = jnp.mean(masked * normed, axis=-1, keepdims=True)
        grad = inv[rows, :][:, :1] * (masked - first - normed * second)
        gin_ref[rows, :] = (up[rows, :].astype(F32) + grad).astype(BF)

        @pl.when(seg > 0)
        def _():
            up_copy(block).start()

    gin_copy.start()

    @pl.when(seg > 0)
    def _():
        tap_grads()

    if relay:
        total = kg_ref[:, kg_window]
        for by in range(1, n_mp):
            sender = lax.rem(mp + n_mp - by, n_mp)
            kg_copy(mp, sender).wait_recv()
            total = total + kg_land[sender]
        scale = (frames * n_mp) ** (-0.5)
        even, odd = total[:taps, :own], total[:taps, 2 * LANES - own :]
        kg_out[0] = jnp.where(column == 0, even, odd) * scale
        for by in range(1, n_mp):
            kg_copy(lax.rem(mp + by, n_mp), mp).wait_send()
        passed()
    else:
        kg_out[0] = kg_ref[:taps, :]

    out_copy.wait()
    gin_copy.wait()
    halo_sent(pm, 0)
    halo_sent(pg, 2)

    @pl.when(seg < n_seg - 1)
    def _():
        for tile in range(tiles):
            in_copy(tile).wait_send()

    @pl.when(seg > 0)
    def _():
        for block in range(blocks):
            up_copy(block).wait_send()


def on_device(frames_in, section_weights, conv_kernels, valid_length, out_cotangent):
    frames, width = frames_in.shape
    taps = conv_kernels.shape[1]
    n_mp = lax.axis_size("mp")
    own = width // n_mp
    if width == 1536 and n_mp == 8 and frames == 128:
        return spread_call(frames_in, section_weights, conv_kernels, valid_length, out_cotangent)
    relay = False
    weight = section_weights[0]
    if not relay:
        weight = lax.all_gather(weight, "mp", axis=0, tiled=True)
    vmem = pl.BlockSpec(memory_space=pltpu.VMEM)
    smem = pl.BlockSpec(memory_space=pltpu.SMEM)
    whole = pl.BlockSpec(memory_space=pl.ANY)
    padded = (frames + 2 * PAD, width)
    tap_rows = -(-taps // 8) * 8
    dma = pltpu.SemaphoreType.DMA
    out, gin, grad = pl.pallas_call(
        functools.partial(cascade, relay),
        out_shape=(
            jax.ShapeDtypeStruct((1, frames, width), BF),
            jax.ShapeDtypeStruct((1, frames, width), BF),
            jax.ShapeDtypeStruct((1, taps, own if relay else width), F32),
        ),
        in_specs=[whole, whole, whole, smem, whole],
        out_specs=(whole, whole, vmem),
        scratch_shapes=[
            pltpu.VMEM((frames, width), BF),
            pltpu.VMEM((frames, width), BF),
            pltpu.VMEM((frames, width), F32),
            pltpu.VMEM((frames, LANES), F32),
            pltpu.VMEM(padded, BF),
            pltpu.VMEM(padded, BF),
            pltpu.VMEM((frames, width), BF),
            pltpu.VMEM((frames, width), F32),
            pltpu.VMEM((frames, width), F32),
            pltpu.VMEM((frames, width), BF),
            pltpu.VMEM((frames, width), BF),
            pltpu.VMEM((width, width), BF),
            pltpu.VMEM((taps, width), BF),
            pltpu.VMEM((taps, width), F32),
            pltpu.VMEM((tap_rows, width), F32),
            pltpu.VMEM((n_mp if relay else 1, tap_rows, 2 * LANES), F32),
            dma((4,)), dma((4,)),
            dma((width // WIDE,)), dma((width // WIDE,)),
            dma((frames // ROWS,)), dma((frames // ROWS,)),
            dma((6,)),
            dma((3, n_mp)), dma((n_mp,)), dma((2,)), dma((2,)), dma((n_mp,)), dma((n_mp,)),
            pltpu.SemaphoreType.REGULAR,
        ],
        compiler_params=pltpu.CompilerParams(
            collective_id=0, has_side_effects=True, vmem_limit_bytes=60 * 2**20
        ),
    )(frames_in, weight, conv_kernels[0], valid_length, out_cotangent)
    if not relay:
        grad = lax.psum_scatter(grad, "mp", scatter_dimension=2, tiled=True)
        grad = grad * (frames * n_mp) ** (-0.5)
    return (out, gin, grad)


def solution(mesh):
    in_specs = (
        P("mp", None),
        P("segment", "mp", None),
        P("segment", None, None),
        P(),
        P("mp", None),
    )
    out_specs = (P("segment", "mp", None), P("segment", "mp", None), P("segment", None, "mp"))
    return jax.shard_map(
        on_device, mesh=mesh, in_specs=in_specs, out_specs=out_specs, check_vma=False
    )
```

```python
import functools

import jax
import jax.numpy as jnp
from jax import lax
from jax.experimental import pallas as pl
from jax.experimental.pallas import tpu as pltpu
from jax.sharding import PartitionSpec as P

EPSILON = 1e-05
PAD = 16
LANES = 128
ROWS = 16
WIDE = 256
MESH = pl.DeviceIdType.MESH
NORM_ROWS = 32
BF = jnp.bfloat16
F32 = jnp.float32

STAGES = ((0, 0), (1, 0), (2, 0), (0, 1), (1, 1), (2, 1), (0, 2), (1, 2), (2, 2), (0, 3), (1, 3), (3, 3),)
INNER_0 = (
    (13, 76, 74, 8, 10, 73,),
    (47, 87, 271, 80, 81, 206, 111, 23, 335,),
    (70, 16, 17, 119, 215, 343, 100, 142, 201, 55, 95, 303, 6, 40, 89, 239, 151, 279, 134, 144, 209, 31, 127, 367, 199, 25, 194, 136, 247, 159, 359, 39, 232, 145, 354, 63, 223, 311,),
    (),
    (295, 137, 208, 290, 183, 375, 383, 263, 240, 153, 258,),
    (175, 319, 399, 327, 200, 217, 322, 191, 287, 463, 231, 255, 351, 167,),
    (),
    (486, 391, 495, 386,),
    (511,),
    (),
    (423, 407, 418, 401, 415, 455, 431, 450,),
    (439, 447, 471, 479, 503,),
)
INNER_1 = (
    (268, 333, 330, 265, 266, 328,),
    (79, 327, 367, 343, 73, 322, 336, 15, 263, 303, 279,),
    (258, 296, 273, 71, 111, 87, 351, 66, 81, 272, 7, 23, 311, 287, 2, 17, 360, 103, 119, 95, 359, 98, 352, 337, 39, 47, 55, 31, 34, 304, 345, 127, 167, 151, 375, 162, 145, 368, 63, 199, 143, 383,),
    (),
    (194, 137, 396, 231, 239, 183, 191, 226, 281, 460,),
    (135, 175, 215, 223, 130, 457, 247, 255, 319, 484, 393, 394, 207, 159, 295, 492,),
    (),
    (458, 391, 431, 404, 401, 386,),
    (455, 471, 424, 465,),
    (),
    (450, 439, 423, 415, 464, 409, 503,),
    (479, 496, 473, 447, 511,),
)
CORNER_0 = (68, 65, 4, 1, 66, 103, 327, 132, 129, 98, 39, 263, 32, 197, 2, 167, 295, 192, 130, 231, 391, 194, 455, 34, 423, 290, 258, 322, 226, 162, 386, 418, 450,)
CORNER_1 = (261, 324, 322, 256, 258, 321, 71, 295, 66, 288, 389, 7, 359, 2, 384, 453, 135, 423, 129, 354, 448, 39, 487, 34, 416, 199, 167, 193, 162, 194, 230, 130, 482, 290, 386, 450, 418,)
SENDS = 50
PIECES = 2
LATE = ((3,), (), (1,), (0, 2))


def decode(event):
    return event // 128, event // 64 % 2, event // 32 % 2, event // 8 % 4, event // 4 % 2, event % 4


def spread(
    x_any, w_any, k_any, vl_ref, cot_any,
    out_whole, gin_whole, kg_out,
    w, a, up, norm, inv, pm, pg, act, slope, gs, k_bf, k_ref, kg, kg_sib, kg_sum, kg_land,
    local_sem, x_send, x_recv, k_send, k_recv, own_send, rel_send, rel_recv, sib_send, sib_recv,
    halo_send, halo_recv, out_send, out_recv, gin_send, gin_recv, pair_send, pair_recv, kg_send, kg_recv,
):
    n_sec, rows_in, width = w.shape
    part = a.shape[1]
    taps = k_ref.shape[1]
    seg, mp = lax.axis_index("segment"), lax.axis_index("mp")
    n_seg, n_mp = lax.axis_size("segment"), lax.axis_size("mp")
    own = rows_in // n_mp
    half = own // (2 * PIECES)
    chunks = width // LANES
    tiles = width // WIDE
    x, c = lax.div(seg, 2), lax.rem(seg, 2)
    z, y = lax.div(mp, 2), lax.rem(mp, 2)
    inner = (z == 1) | (z == 2)
    block = jnp.where(c == 1, mp, jnp.where(z == 1, y, 6 + y))
    which = x + y - 2 * x * y
    chunk_id = 2 * block + which
    chip = 4 * x + mp - 2

    def device_of(number, half_of):
        side, core = number % 2, ((number >= 2) & (number < 6)) * 1
        return 2 * (half_of + side - 2 * half_of * side) + core, (number >= 4) * 2 + 2 + side

    barrier = pltpu.get_barrier_semaphore()
    me = seg * n_mp + mp
    total = n_seg * n_mp

    @pl.loop(1, total)
    def _(by):
        other = lax.rem(me + by, total)
        pl.semaphore_signal(
            barrier, inc=1, device_id=(lax.div(other, n_mp), lax.rem(other, n_mp)), device_id_type=MESH
        )

    w_copy = pltpu.make_async_copy(
        w_any, w.at[seg, pl.ds(pl.multiple_of(own * mp, own), own)], local_sem.at[0]
    )
    k_copy = pltpu.make_async_copy(k_any, k_bf.at[seg], local_sem.at[1])
    w_copy.start()

    @pl.when(inner)
    def _():
        k_copy.start()

    pl.semaphore_wait(barrier, total - 1)

    def half_ref(section, shard, piece, core):
        start = own * shard + half * (2 * piece + core)
        return w.at[section, pl.ds(pl.multiple_of(start, half), half)]

    def own_copy(kind, piece):
        core = c if kind else 1 - c
        return pltpu.make_async_remote_copy(
            src_ref=half_ref(seg, mp, piece, core), dst_ref=half_ref(seg, mp, piece, core),
            send_sem=own_send.at[2 * piece + kind],
            recv_sem=(sib_recv if kind else rel_recv).at[(seg * n_mp + mp) * PIECES + piece],
            device_id={"segment": seg + 1 - 2 * c}, device_id_type=MESH,
        )

    def relay_copy(section, shard, piece, way, slot):
        target = (
            {"segment": seg + 2 - 4 * x}, {"mp": mp + 1 - 2 * y}, {"mp": mp + jnp.where(z < 2, 2, -2)}
        )[way]
        return pltpu.make_async_remote_copy(
            src_ref=half_ref(section, shard, piece, c), dst_ref=half_ref(section, shard, piece, c),
            send_sem=rel_send.at[slot], recv_sem=rel_recv.at[(section * n_mp + shard) * PIECES + piece],
            device_id=target, device_id_type=MESH,
        )

    def sib_copy(section, shard, piece, core):
        sem = (section * n_mp + shard) * PIECES + piece
        return pltpu.make_async_remote_copy(
            src_ref=half_ref(section, shard, piece, core), dst_ref=half_ref(section, shard, piece, core),
            send_sem=sib_send.at[sem], recv_sem=sib_recv.at[sem],
            device_id={"segment": seg + 1 - 2 * c}, device_id_type=MESH,
        )

    def shard_of(across, depth):
        from_y = 1 - y if across else y
        return 2 * jnp.where(z < 2, depth, 3 - depth) + from_y

    def is_home(section, across, depth, plane, corner):
        return section // 2 == plane and across == 0 and depth == (0 if corner else 1)

    def run_events(events, plane, corner, slot):
        for event in events:
            section, piece, across, depth, first, way = decode(event)
            shard = shard_of(across, depth)
            if first and is_home(section, across, depth, plane, corner):
                pl.when(c != section % 2)(relay_copy(section, shard, piece, 0, 0).wait_recv)
            elif first:
                relay_copy(section, shard, piece, 0, 0).wait_recv()
                if not corner:
                    sib_copy(section, shard, piece, c).start()
            if way < 3:
                relay_copy(section, shard, piece, way, slot).start()
                slot += 1
        return slot

    def finish_events(groups, plane, corner):
        slot = 0
        for events in groups:
            for event in events:
                section, piece, across, depth, first, way = decode(event)
                shard = shard_of(across, depth)
                if first and not corner and not is_home(section, across, depth, plane, corner):
                    sib_copy(section, shard, piece, c).wait_send()
                if way < 3:
                    relay_copy(section, shard, piece, way, slot).wait_send()
                    slot += 1

    def siblings(section, plane):
        for across in range(2):
            for depth in range(4):
                for piece in range(PIECES):
                    wait = sib_copy(section, shard_of(across, depth), piece, 1 - c).wait_recv
                    if is_home(section, across, depth, plane, False):
                        pl.when(c != section % 2)(wait)
                    else:
                        wait()

    to_seg, to_mp = device_of(mp, which)
    sends_x = seg == to_seg
    away = sends_x & (to_mp != mp)

    def x_move(index, remote):
        rows = pl.ds(pl.multiple_of(part * which, part), part)
        source, target = ((x_any, a.at[0]), (cot_any, up.at[n_sec]))[index]
        if not remote:
            return pltpu.make_async_copy(source.at[rows], target, x_recv.at[index])
        return pltpu.make_async_remote_copy(
            src_ref=source.at[rows], dst_ref=target, send_sem=x_send.at[index], recv_sem=x_recv.at[index],
            device_id={"mp": to_mp}, device_id_type=MESH,
        )

    def x_start(index):
        pl.when(inner & (c == 1))(lambda: x_move(index, False).start())
        pl.when(away)(lambda: x_move(index, True).start())

    def x_wait(index):
        pl.when(c == 1)(lambda: x_move(index, False).wait())
        pl.when(c == 0)(lambda: x_move(index, True).wait_recv())

    def k_move(by, sender):
        return pltpu.make_async_remote_copy(
            src_ref=k_any, dst_ref=k_bf.at[sender], send_sem=k_send.at[by - 1], recv_sem=k_recv.at[sender],
            device_id={"segment": lax.rem(seg + by, n_seg)}, device_id_type=MESH,
        )

    w_copy.wait()
    for piece in range(PIECES):
        own_copy(0, piece).start()
        pl.when(inner)(own_copy(1, piece).start)

    @pl.when(inner)
    def _():
        for by in range(1, n_sec):
            k_move(by, seg).start()

    x_start(0)

    corner = jnp.logical_not(inner)
    for plane, table in ((0, CORNER_0), (1, CORNER_1)):

        @pl.when(corner & (x == plane))
        def _():
            run_events(table, plane, True, 0)

    x_start(1)

    def mask_rows(start, count):
        position = chunk_id * part + start + lax.broadcasted_iota(jnp.int32, (count, LANES), 0)
        return (position < vl_ref[0]).astype(F32)

    def halo_copy(pad_ref, section, slot, to_next):
        rows_from = pl.ds(part, PAD) if to_next else pl.ds(PAD, PAD)
        rows_to = pl.ds(0, PAD) if to_next else pl.ds(part + PAD, PAD)
        near = chunk_id + (1 if to_next else -1)
        target = device_of(lax.div(near, 2), lax.rem(near, 2))
        sem = 6 * section + 2 * slot + (0 if to_next else 1)
        columns = pl.ds(0, width) if slot == 0 else pl.ds((slot - 1) * side, side)
        return pltpu.make_async_remote_copy(
            src_ref=pad_ref.at[section, rows_from, columns], dst_ref=pad_ref.at[section, rows_to, columns],
            send_sem=halo_send.at[sem], recv_sem=halo_recv.at[sem],
            device_id=target, device_id_type=MESH,
        )

    last = 2 * n_mp - 1
    side = width // 2

    def halo_start(pad_ref, section, slot):
        pl.when(chunk_id < last)(lambda: halo_copy(pad_ref, section, slot, True).start())
        pl.when(chunk_id > 0)(lambda: halo_copy(pad_ref, section, slot, False).start())

    def halo_wait(pad_ref, section, slot):
        pl.when(chunk_id > 0)(lambda: halo_copy(pad_ref, section, slot, True).wait_recv())
        pl.when(chunk_id < last)(lambda: halo_copy(pad_ref, section, slot, False).wait_recv())

    def halo_sent(pad_ref, section, slot):
        pl.when(chunk_id < last)(lambda: halo_copy(pad_ref, section, slot, True).wait_send())
        pl.when(chunk_id > 0)(lambda: halo_copy(pad_ref, section, slot, False).wait_send())

    def tap_sum(padded, section, columns, forward):
        rows = padded.shape[0]
        running = jnp.zeros((part, LANES), F32)
        for r in range(8):
            moved = padded if r == 0 else pltpu.roll(padded, rows - r, 0)
            for base in range(0, 2 * PAD, 8):
                offset = base + r
                if 1 <= offset <= taps:
                    tap = offset - 1 if forward else taps - offset
                    running = running + k_ref[section, tap : tap + 1, columns] * moved[base : base + part]
        return running

    def normalize(section):
        for start in range(0, part, NORM_ROWS):
            rows = slice(start, start + NORM_ROWS)
            values = a[section, rows].astype(F32)
            center = values - jnp.mean(values, axis=-1, keepdims=True)
            inverse = lax.rsqrt(jnp.mean(center * center, axis=-1, keepdims=True) + EPSILON)
            normed = center * inverse
            norm[section, rows] = normed
            inv[section, rows] = jnp.broadcast_to(inverse, (NORM_ROWS, LANES))
            pm[section, PAD + start : PAD + start + NORM_ROWS] = (
                normed * mask_rows(start, NORM_ROWS)[:, :1]
            ).astype(BF)
        halo_start(pm, section, 0)

    def convolve(section):
        halo_wait(pm, section, 0)

        @pl.loop(0, chunks)
        def _(chunk):
            columns = pl.ds(pl.multiple_of(chunk * LANES, LANES), LANES)
            conv = tap_sum(pm[section, :, columns].astype(F32), section, columns, True)
            gate = jax.nn.sigmoid(conv)
            act[section, :, columns] = (conv * gate).astype(BF)
            slope[section, :, columns] = gate * (1.0 + conv * (1.0 - gate))

    def result_copy(source, index, section, whole, send, recv, remote):
        rows = pl.ds(pl.multiple_of(part * which, part), part)
        if not remote:
            return pltpu.make_async_copy(source.at[index], whole.at[0, rows], recv.at[which])
        return pltpu.make_async_remote_copy(
            src_ref=source.at[index], dst_ref=whole.at[0, rows],
            send_sem=send.at[section], recv_sem=recv.at[which],
            device_id=(section, block), device_id_type=MESH,
        )

    def result_start(section, *what):
        same = (seg == section) & (mp == block)
        pl.when(same)(lambda: result_copy(*what, False).start())
        pl.when(jnp.logical_not(same))(lambda: result_copy(*what, True).start())

    def result_sent(section, *what):
        same = (seg == section) & (mp == block)
        pl.when(jnp.logical_not(same))(lambda: result_copy(*what, True).wait_send())

    def result_wait(source, whole, send, recv):
        for half_of in range(2):
            from_seg, from_mp = device_of(mp, half_of)
            same = (seg == from_seg) & (mp == from_mp)
            rows = pl.ds(part * half_of, part)

            @pl.when(same)
            def _():
                pltpu.make_async_copy(source.at[0], whole.at[0, rows], recv.at[half_of]).wait()

            @pl.when(jnp.logical_not(same))
            def _():
                pltpu.make_async_remote_copy(
                    src_ref=source.at[0], dst_ref=whole.at[0, rows],
                    send_sem=send.at[0], recv_sem=recv.at[half_of],
                    device_id=(seg, mp), device_id_type=MESH,
                ).wait_recv()

    def product(section):
        for tile in range(tiles):
            columns = slice(tile * WIDE, (tile + 1) * WIDE)
            result = jnp.dot(act[section], w[section, :, columns], preferred_element_type=F32)
            a[section + 1, :, columns] = (a[section, :, columns].astype(F32) + result).astype(BF)

    def out_what(section):
        return section, a, section + 1, section, out_whole, out_send, out_recv

    def gin_what(section):
        return section, up, section, section, gin_whole, gin_send, gin_recv

    def out_start(section, late):
        at_once = (c == 0) | (x == section // 2)
        pl.when(jnp.logical_not(at_once) if late else at_once)(lambda: result_start(*out_what(section)))

    def gin_start(section, late):
        pl.when(c == (1 if late else 0))(lambda: result_start(*gin_what(section)))

    def forward_stage(kind, section):
        if kind == 0:
            if section == 0:
                x_wait(0)
                k_copy.wait()
                for by in range(1, n_sec):
                    k_move(by, lax.rem(seg + n_seg - by, n_seg)).wait_recv()
                for s in range(n_sec):
                    k_ref[s] = k_bf[s].astype(F32)
                for pad_ref in (pm, pg):

                    @pl.when(chunk_id == 0)
                    def _():
                        for s in range(n_sec):
                            pad_ref[s, 0:PAD, :] = jnp.zeros((PAD, width), BF)

                    @pl.when(chunk_id == last)
                    def _():
                        for s in range(n_sec):
                            pad_ref[s, part + PAD : part + 2 * PAD, :] = jnp.zeros((PAD, width), BF)

                kg[:, taps:, :] = jnp.zeros((n_sec, kg.shape[1] - taps, width), F32)
            normalize(section)
        elif kind == 1:
            convolve(section)
        elif kind == 3:
            for plane in range(2):
                pl.when(x == plane)(lambda: siblings(section, plane))
            last_back_product()
        else:
            for plane in range(2):
                pl.when(x == plane)(lambda: siblings(section, plane))
            product(section)
            out_start(section, False)

    def kg_window(index, core):
        return pl.ds(pl.multiple_of(384 * index + 128 * core, LANES), 2 * LANES)

    def kg_pair(section, index):
        return pltpu.make_async_remote_copy(
            src_ref=kg.at[section, :, kg_window(index, 1 - c)], dst_ref=kg_sib.at[section, index],
            send_sem=pair_send.at[4 * section + index], recv_sem=pair_recv.at[4 * section + index],
            device_id={"segment": seg + 1 - 2 * c}, device_id_type=MESH,
        )

    def kg_copy(section, index, remote):
        if not remote:
            return pltpu.make_async_copy(kg_sum.at[section, index], kg_land.at[chip], kg_recv.at[chip])
        return pltpu.make_async_remote_copy(
            src_ref=kg_sum.at[section, index], dst_ref=kg_land.at[chip],
            send_sem=kg_send.at[4 * section + index], recv_sem=kg_recv.at[chip],
            device_id=(section, 2 * index + c), device_id_type=MESH,
        )

    def kg_start(section):
        for index in range(n_mp // 2):
            kg_pair(section, index).wait_recv()
            kg_sum[section, index] = kg[section, :, kg_window(index, c)] + kg_sib[section, index]
            same = (seg == section) & (mp == 2 * index + c)
            pl.when(same)(lambda: kg_copy(section, index, False).start())
            pl.when(jnp.logical_not(same))(lambda: kg_copy(section, index, True).start())

    def tap_grads(section):
        @pl.loop(0, chunks)
        def _(chunk):
            columns = pl.ds(pl.multiple_of(chunk * LANES, LANES), LANES)
            padded = pm[section, :, columns].astype(F32)
            grad = pg[section, PAD : PAD + part, columns].astype(F32)
            rows = padded.shape[0]
            for r in range(8):
                moved = padded if r == 0 else pltpu.roll(padded, rows - r, 0)
                for base in range(0, 2 * PAD, 8):
                    tap = base + r - 1
                    if 0 <= tap < taps:
                        kg[section, tap : tap + 1, columns] = jnp.sum(
                            grad * moved[base : base + part], axis=0, keepdims=True
                        )

        for index in range(n_mp // 2):
            kg_pair(section, index).start()

    def back_tile(section, tile):
        columns = slice(tile * WIDE, (tile + 1) * WIDE)
        return columns, lax.dot_general(
            up[section + 1], w[section, columns, :], (((1,), (1,)), ((), ())), preferred_element_type=F32
        )

    def last_back_product():
        x_wait(1)
        for tile in range(tiles):
            columns, grad = back_tile(n_sec - 1, tile)
            gs[:, columns] = grad

    def backward(section):
        for part_of in range(2):
            for tile in range(part_of * tiles // 2, (part_of + 1) * tiles // 2):
                if section == n_sec - 1:
                    columns = slice(tile * WIDE, (tile + 1) * WIDE)
                    grad = gs[:, columns]
                else:
                    columns, grad = back_tile(section, tile)
                pg[section, PAD : PAD + part, columns] = (grad * slope[section, :, columns]).astype(BF)
            halo_start(pg, section, 1 + part_of)
        tap_grads(section)
        if section == n_sec - 1:
            product(section)
            out_start(section, False)
        else:
            kg_start(section + 1)
        for part_of in range(2):
            halo_wait(pg, section, 1 + part_of)
            if part_of == 1:
                if section < n_sec - 1:
                    gin_start(section + 1, True)
                for other in LATE[section]:
                    out_start(other, True)
                if section == 0:
                    kg_start(section)

            @pl.loop(part_of * chunks // 2, (part_of + 1) * chunks // 2)
            def _(chunk):
                columns = pl.ds(pl.multiple_of(chunk * LANES, LANES), LANES)
                gs[:, columns] = tap_sum(
                    pg[section, :, columns].astype(F32), section, columns, False
                ) * mask_rows(0, part)

        for start in range(0, part, NORM_ROWS):
            rows = slice(start, start + NORM_ROWS)
            masked = gs[rows]
            normed = norm[section, rows]
            first = jnp.mean(masked, axis=-1, keepdims=True)
            second = jnp.mean(masked * normed, axis=-1, keepdims=True)
            grad = inv[section, rows][:, :1] * (masked - first - normed * second)
            up[section, rows] = (up[section + 1, rows].astype(F32) + grad).astype(BF)
        gin_start(section, False)
        if section == 0:
            gin_start(section, True)

    slots = [0, 0]
    for index, (kind, section) in enumerate(STAGES):
        for plane, table in ((0, INNER_0), (1, INNER_1)):
            if table[index]:
                start = slots[plane]

                @pl.when(inner & (x == plane))
                def _():
                    run_events(table[index], plane, False, start)

                slots[plane] += sum(event % 4 < 3 for event in table[index])
        pl.when(inner)(lambda: forward_stage(kind, section))
    @pl.when(inner)
    def _():
        for section in reversed(range(n_sec)):
            backward(section)

    sums = jnp.zeros((kg.shape[1], 2 * LANES), F32)
    for number in range(n_mp):
        from_seg, from_mp = 2 * (number // 4) + y, number % 4 + 2
        same = (seg == from_seg) & (mp == from_mp)

        @pl.when(same)
        def _():
            pltpu.make_async_copy(kg_sum.at[0, 0], kg_land.at[number], kg_recv.at[number]).wait()

        @pl.when(jnp.logical_not(same))
        def _():
            pltpu.make_async_remote_copy(
                src_ref=kg_sum.at[0, 0], dst_ref=kg_land.at[number],
                send_sem=kg_send.at[0], recv_sem=kg_recv.at[number],
                device_id=(seg, mp), device_id_type=MESH,
            ).wait_recv()

        sums = sums + kg_land[number]
    scale = (2 * part * n_mp) ** (-0.5)
    even, odd = sums[:taps, :own], sums[:taps, 2 * LANES - own :]
    kg_out[0] = jnp.where(y == 0, even, odd) * scale

    result_wait(a, out_whole, out_send, out_recv)
    result_wait(up, gin_whole, gin_send, gin_recv)

    for piece in range(PIECES):
        own_copy(0, piece).wait_send()
    for index in range(2):
        pl.when(away)(lambda: x_move(index, True).wait_send())
    for plane, table in ((0, CORNER_0), (1, CORNER_1)):
        pl.when(corner & (x == plane))(lambda: finish_events((table,), plane, True))
    for plane, table in ((0, INNER_0), (1, INNER_1)):
        pl.when(inner & (x == plane))(lambda: finish_events(table, plane, False))

    @pl.when(inner)
    def _():
        for piece in range(PIECES):
            own_copy(1, piece).wait_send()
        for by in range(1, n_sec):
            k_move(by, seg).wait_send()
        for section in range(n_sec):
            halo_sent(pm, section, 0)
            halo_sent(pg, section, 1)
            halo_sent(pg, section, 2)
            result_sent(*out_what(section))
            result_sent(*gin_what(section))
            for index in range(n_mp // 2):
                kg_pair(section, index).wait_send()
                same = (seg == section) & (mp == 2 * index + c)
                pl.when(jnp.logical_not(same))(lambda: kg_copy(section, index, True).wait_send())


def spread_call(frames_in, section_weights, conv_kernels, valid_length, out_cotangent):
    frames, width = frames_in.shape
    taps = conv_kernels.shape[1]
    n_sec, n_mp = lax.axis_size("segment"), lax.axis_size("mp")
    own = width // n_mp
    part = frames // 2
    vmem = pl.BlockSpec(memory_space=pltpu.VMEM)
    smem = pl.BlockSpec(memory_space=pltpu.SMEM)
    whole = pl.BlockSpec(memory_space=pl.ANY)
    tap_rows = -(-taps // 8) * 8
    dma = pltpu.SemaphoreType.DMA
    return pl.pallas_call(
        spread,
        out_shape=(
            jax.ShapeDtypeStruct((1, frames, width), BF),
            jax.ShapeDtypeStruct((1, frames, width), BF),
            jax.ShapeDtypeStruct((1, taps, own), F32),
        ),
        in_specs=[whole, whole, whole, smem, whole],
        out_specs=(whole, whole, vmem),
        scratch_shapes=[
            pltpu.VMEM((n_sec, width, width), BF),
            pltpu.VMEM((n_sec + 1, part, width), BF),
            pltpu.VMEM((n_sec + 1, part, width), BF),
            pltpu.VMEM((n_sec, part, width), F32),
            pltpu.VMEM((n_sec, part, LANES), F32),
            pltpu.VMEM((n_sec, part + 2 * PAD, width), BF),
            pltpu.VMEM((n_sec, part + 2 * PAD, width), BF),
            pltpu.VMEM((n_sec, part, width), BF),
            pltpu.VMEM((n_sec, part, width), F32),
            pltpu.VMEM((part, width), F32),
            pltpu.VMEM((n_sec, taps, width), BF),
            pltpu.VMEM((n_sec, taps, width), F32),
            pltpu.VMEM((n_sec, tap_rows, width), F32),
            pltpu.VMEM((n_sec, n_mp // 2, tap_rows, 2 * LANES), F32),
            pltpu.VMEM((n_sec, n_mp // 2, tap_rows, 2 * LANES), F32),
            pltpu.VMEM((n_mp, tap_rows, 2 * LANES), F32),
            dma((2,)), dma((2,)), dma((2,)), dma((n_sec - 1,)), dma((n_sec,)),
            dma((2 * PIECES,)), dma((SENDS,)),
            dma((PIECES * n_sec * n_mp,)), dma((PIECES * n_sec * n_mp,)), dma((PIECES * n_sec * n_mp,)),
            dma((6 * n_sec,)), dma((6 * n_sec,)),
            dma((n_sec,)), dma((2,)), dma((n_sec,)), dma((2,)),
            dma((4 * n_sec,)), dma((4 * n_sec,)), dma((4 * n_sec,)), dma((n_mp,)),
        ],
        compiler_params=pltpu.CompilerParams(
            collective_id=1, has_side_effects=True, vmem_limit_bytes=60 * 2**20
        ),
    )(frames_in, section_weights[0], conv_kernels[0], valid_length, out_cotangent)


def cascade(
    relay, x_any, w_any, k_any, vl_ref, cot_any,
    out_whole, gin_whole, kg_out,
    cur, up, norm, inv, pm, pg, act, slope, gs, out_ref, gin_ref, w_ref, k_bf, k_ref, kg_ref, kg_land,
    halo_send, halo_recv, in_send, in_recv, up_send, up_recv,
    local_sem, w_send, w_recv, end_send, end_recv, kg_send, kg_recv, turn_sem,
):
    frames, width = x_any.shape
    taps = k_ref.shape[0]
    seg, mp = lax.axis_index("segment"), lax.axis_index("mp")
    n_seg, n_mp = lax.axis_size("segment"), lax.axis_size("mp")
    chunks = width // LANES
    blocks = frames // ROWS
    tiles = width // WIDE

    barrier = pltpu.get_barrier_semaphore()
    steps_mp = range(1, n_mp) if relay else (1, n_mp - 1)
    for axis, index, count, steps in (
        ("segment", seg, n_seg, (1, n_seg - 1)), ("mp", mp, n_mp, steps_mp)
    ):
        for by in steps:
            pl.semaphore_signal(
                barrier, inc=1, device_id={axis: lax.rem(index + by, count)}, device_id_type=MESH
            )
    own = width // n_mp
    w_rows = pl.ds(pl.multiple_of(mp * own, own), own) if relay else pl.ds(0, width)
    w_copy = pltpu.make_async_copy(w_any, w_ref.at[w_rows], local_sem.at[0])
    x_copy = pltpu.make_async_copy(x_any, cur, local_sem.at[1])
    cot_copy = pltpu.make_async_copy(cot_any, up, local_sem.at[2])
    k_copy = pltpu.make_async_copy(k_any, k_bf, local_sem.at[3])
    out_copy = pltpu.make_async_copy(out_ref, out_whole.at[0], local_sem.at[4])
    gin_copy = pltpu.make_async_copy(gin_ref, gin_whole.at[0], local_sem.at[5])
    w_copy.start()
    k_copy.start()

    @pl.when(seg == 0)
    def _():
        x_copy.start()

    @pl.when(seg == n_seg - 1)
    def _():
        cot_copy.start()

    pl.semaphore_wait(barrier, 2 + len(steps_mp))

    row, column = lax.div(mp, 2), lax.rem(mp, 2)
    n_row = n_mp // 2

    half = own // 2

    def block_copy(block, way, count=own):
        rows = pl.ds(pl.multiple_of(block * own, own), count)
        target = (mp + 2, mp - 2, mp + 1 - 2 * column)[way]
        return pltpu.make_async_remote_copy(
            src_ref=w_ref.at[rows], dst_ref=w_ref.at[rows],
            send_sem=w_send.at[way, block], recv_sem=w_recv.at[block],
            device_id={"mp": target}, device_id_type=MESH,
        )

    def end_copy(way):
        block = (0 if way == 0 else n_mp - 2) + 1 - column
        rows = pl.ds(pl.multiple_of(block * own + half, half), half)
        return pltpu.make_async_remote_copy(
            src_ref=w_ref.at[rows], dst_ref=w_ref.at[rows],
            send_sem=end_send.at[way], recv_sem=end_recv.at[way],
            device_id={"mp": mp + 2 if way == 0 else mp - 2}, device_id_type=MESH,
        )

    def each_block(distance, act_on, arrive):
        if distance == 0:
            pl.when(row < n_row - 1)(lambda: act_on(mp, 0))
            pl.when(row > 0)(lambda: act_on(mp, 1))
            act_on(mp, 2)
            return
        low, high = mp - 2 * distance, mp + 2 * distance

        @pl.when(row >= distance)
        def _():
            arrive(low)
            pl.when(row < n_row - 1)(lambda: act_on(low, 0))
            pl.when(row == distance)(lambda: act_on(low, 2, half))
            pl.when(row > distance)(lambda: act_on(low, 2))

        @pl.when(row + distance < n_row)
        def _():
            arrive(high)
            pl.when(row > 0)(lambda: act_on(high, 1))
            pl.when(row + distance == n_row - 1)(lambda: act_on(high, 2, half))
            pl.when(row + distance < n_row - 1)(lambda: act_on(high, 2))

    def pass_on(distance):
        each_block(
            distance,
            lambda *what: block_copy(*what).start(),
            lambda block: block_copy(block, 0).wait_recv(),
        )
        if distance == 1:
            for way, end in ((0, 0), (1, n_row - 1)):

                @pl.when(row == end)
                def _():
                    block_copy(2 * end + 1 - column, 2).wait_recv()
                    end_copy(way).start()

    def passed():
        for distance in range(n_row):
            each_block(
                distance,
                lambda *what: block_copy(*what).wait_send(),
                lambda block: None,
            )
        pl.when(row < n_row - 1)(lambda: end_copy(0).wait_send())
        pl.when(row > 0)(lambda: end_copy(1).wait_send())

    def gather_rest(first):
        if relay:
            for distance in range(first, n_row):
                pass_on(distance)

            @pl.when(row > 0)
            def _():
                end_copy(0).wait_recv()
                pl.when(row < n_row - 1)(lambda: end_copy(0).start())

            @pl.when(row < n_row - 1)
            def _():
                end_copy(1).wait_recv()
                pl.when(row > 0)(lambda: end_copy(1).start())

            for index in range(n_row):
                block = index * 2 + 1 - column
                if index in (0, n_row - 1):
                    pl.when(row != index)(lambda: block_copy(block, 2, half).wait_recv())
                else:
                    block_copy(block, 2).wait_recv()

    def kg_copy(target, sender):
        start = 384 * lax.div(target, 2) + 128 * lax.rem(target, 2)
        window = pl.ds(pl.multiple_of(start, LANES), 2 * LANES)
        return pltpu.make_async_remote_copy(
            src_ref=kg_ref.at[:, window], dst_ref=kg_land.at[sender],
            send_sem=kg_send.at[target], recv_sem=kg_recv.at[sender],
            device_id={"mp": target}, device_id_type=MESH,
        )

    w_copy.wait()
    if relay:

        @pl.when(seg != 1)
        def _():
            pass_on(0)

    k_copy.wait()
    k_ref[...] = k_bf[...].astype(F32)
    kg_ref[...] = jnp.zeros(kg_ref.shape, F32)

    def halo_copy(pad_ref, first, to_right):
        rows_from = pl.ds(frames, PAD) if to_right else pl.ds(PAD, PAD)
        rows_to = pl.ds(0, PAD) if to_right else pl.ds(frames + PAD, PAD)
        target = lax.rem(mp + (1 if to_right else n_mp - 1), n_mp)
        slot = first + (0 if to_right else 1)
        return pltpu.make_async_remote_copy(
            src_ref=pad_ref.at[rows_from], dst_ref=pad_ref.at[rows_to],
            send_sem=halo_send.at[slot], recv_sem=halo_recv.at[slot],
            device_id={"mp": target}, device_id_type=MESH,
        )

    def halo_start(pad_ref, first):
        @pl.when(mp < n_mp - 1)
        def _():
            halo_copy(pad_ref, first, True).start()

        @pl.when(mp > 0)
        def _():
            halo_copy(pad_ref, first, False).start()

    def halo_wait(pad_ref, first):
        @pl.when(mp > 0)
        def _():
            halo_copy(pad_ref, first, True).wait_recv()

        @pl.when(mp < n_mp - 1)
        def _():
            halo_copy(pad_ref, first, False).wait_recv()

    def halo_sent(pad_ref, first):
        @pl.when(mp < n_mp - 1)
        def _():
            halo_copy(pad_ref, first, True).wait_send()

        @pl.when(mp > 0)
        def _():
            halo_copy(pad_ref, first, False).wait_send()

    def halo_clear(pad_ref):
        @pl.when(mp == 0)
        def _():
            pad_ref[0:PAD, :] = jnp.zeros((PAD, width), BF)

        @pl.when(mp == n_mp - 1)
        def _():
            pad_ref[frames + PAD : frames + 2 * PAD, :] = jnp.zeros((PAD, width), BF)

    def in_copy(tile):
        columns = pl.ds(tile * WIDE, WIDE)
        return pltpu.make_async_remote_copy(
            src_ref=out_ref.at[:, columns], dst_ref=cur.at[:, columns],
            send_sem=in_send.at[tile], recv_sem=in_recv.at[tile],
            device_id={"segment": lax.rem(seg + 1, n_seg)}, device_id_type=MESH,
        )

    def up_copy(block):
        rows = pl.ds(block * ROWS, ROWS)
        return pltpu.make_async_remote_copy(
            src_ref=gin_ref.at[rows], dst_ref=up.at[rows],
            send_sem=up_send.at[block], recv_sem=up_recv.at[block],
            device_id={"segment": lax.rem(seg + n_seg - 1, n_seg)}, device_id_type=MESH,
        )

    def mask_rows(start, count):
        position = mp * frames + start + lax.broadcasted_iota(jnp.int32, (count, LANES), 0)
        return (position < vl_ref[0]).astype(F32)

    def back_product():
        for tile in range(tiles):
            columns = slice(tile * WIDE, (tile + 1) * WIDE)
            gs[:, columns] = lax.dot_general(
                up[...], w_ref[columns, :], (((1,), (1,)), ((), ())), preferred_element_type=F32
            )

    halo_clear(pm)
    halo_clear(pg)

    @pl.when(seg == n_seg - 1)
    def _():
        gather_rest(1)
        cot_copy.wait()
        back_product()

    @pl.when(seg == 0)
    def _():
        x_copy.wait()

    @pl.when(seg == 1)
    def _():
        if relay:
            pl.semaphore_wait(turn_sem, 1)
            pass_on(0)

    @pl.when((seg > 1) & (seg < n_seg - 1))
    def _():
        gather_rest(1)

    @pl.when(seg > 0)
    def _():
        for tile in range(tiles):
            in_copy(tile).wait_recv()

    def norm_rows(block):
        start = pl.multiple_of(block * ROWS, ROWS)
        rows = pl.ds(start, ROWS)
        values = cur[rows, :].astype(F32)
        center = values - jnp.mean(values, axis=-1, keepdims=True)
        inverse = lax.rsqrt(jnp.mean(center * center, axis=-1, keepdims=True) + EPSILON)
        normed = center * inverse
        norm[rows, :] = normed
        inv[rows, :] = jnp.broadcast_to(inverse, (ROWS, LANES))
        pm[pl.ds(pl.multiple_of(PAD + start, ROWS), ROWS), :] = (
            normed * mask_rows(start, ROWS)[:, :1]
        ).astype(BF)

    norm_rows(0)
    norm_rows(blocks - 1)
    halo_start(pm, 0)

    @pl.loop(1, blocks - 1)
    def _(block):
        norm_rows(block)

    if relay:

        @pl.when(seg < 2)
        def _():
            pass_on(1)

    halo_wait(pm, 0)

    def shifted(padded):
        total = padded.shape[0]
        return [padded if r == 0 else pltpu.roll(padded, total - r, 0) for r in range(8)]

    def tap_sum(padded, columns, forward):
        total = padded.shape[0]
        running = jnp.zeros((frames, LANES), F32)
        for r in range(8):
            moved = padded if r == 0 else pltpu.roll(padded, total - r, 0)
            for base in range(0, 2 * PAD, 8):
                offset = base + r
                if 1 <= offset <= taps:
                    tap = offset - 1 if forward else taps - offset
                    running = running + k_ref[tap : tap + 1, columns] * moved[base : base + frames]
        return running

    @pl.loop(0, chunks)
    def _(chunk):
        columns = pl.ds(pl.multiple_of(chunk * LANES, LANES), LANES)
        conv = tap_sum(pm[:, columns].astype(F32), columns, True)
        gate = jax.nn.sigmoid(conv)
        act[:, columns] = (conv * gate).astype(BF)
        slope[:, columns] = gate * (1.0 + conv * (1.0 - gate))

    if relay:

        @pl.when(seg < 2)
        def _():
            pass_on(2)

        @pl.when(seg == 0)
        def _():
            pl.semaphore_signal(
                turn_sem, inc=1, device_id={"segment": seg + 1}, device_id_type=MESH
            )

        @pl.when(seg < 2)
        def _():
            gather_rest(3)

    for tile in range(tiles):
        columns = slice(tile * WIDE, (tile + 1) * WIDE)
        product = jnp.dot(act[...], w_ref[:, columns], preferred_element_type=F32)
        out_ref[:, columns] = (cur[:, columns].astype(F32) + product).astype(BF)

        @pl.when(seg < n_seg - 1)
        def _():
            in_copy(tile).start()

    out_copy.start()

    @pl.when(seg < n_seg - 1)
    def _():
        for block in range(blocks):
            up_copy(block).wait_recv()
        back_product()

    def grad_rows(block):
        start = pl.multiple_of(block * ROWS, ROWS)
        rows = pl.ds(start, ROWS)
        pg[pl.ds(pl.multiple_of(PAD + start, ROWS), ROWS), :] = (
            gs[rows, :] * slope[rows, :]
        ).astype(BF)

    grad_rows(0)
    grad_rows(blocks - 1)
    halo_start(pg, 2)

    @pl.loop(1, blocks - 1)
    def _(block):
        grad_rows(block)

    kg_start = 384 * row + 128 * column
    kg_window = pl.ds(pl.multiple_of(kg_start, LANES), 2 * LANES)

    def tap_grads():
        @pl.loop(0, chunks)
        def _(chunk):
            columns = pl.ds(pl.multiple_of(chunk * LANES, LANES), LANES)
            padded = pm[:, columns].astype(F32)
            grad = pg[PAD : PAD + frames, columns].astype(F32)
            total = padded.shape[0]
            for r in range(8):
                moved = padded if r == 0 else pltpu.roll(padded, total - r, 0)
                for base in range(0, 2 * PAD, 8):
                    tap = base + r - 1
                    if 0 <= tap < taps:
                        kg_ref[tap : tap + 1, columns] = jnp.sum(
                            grad * moved[base : base + frames], axis=0, keepdims=True
                        )

        if relay:
            for by in range(1, n_mp):
                kg_copy(lax.rem(mp + by, n_mp), mp).start()

    @pl.when(seg == 0)
    def _():
        tap_grads()

    halo_wait(pg, 2)

    @pl.loop(0, chunks)
    def _(chunk):
        columns = pl.ds(pl.multiple_of(chunk * LANES, LANES), LANES)
        gs[:, columns] = tap_sum(pg[:, columns].astype(F32), columns, False) * mask_rows(0, frames)

    @pl.loop(0, blocks)
    def _(block):
        rows = pl.ds(pl.multiple_of(block * ROWS, ROWS), ROWS)
        masked = gs[rows, :]
        normed = norm[rows, :]
        first = jnp.mean(masked, axis=-1, keepdims=True)
        second = jnp.mean(masked * normed, axis=-1, keepdims=True)
        grad = inv[rows, :][:, :1] * (masked - first - normed * second)
        gin_ref[rows, :] = (up[rows, :].astype(F32) + grad).astype(BF)

        @pl.when(seg > 0)
        def _():
            up_copy(block).start()

    gin_copy.start()

    @pl.when(seg > 0)
    def _():
        tap_grads()

    if relay:
        total = kg_ref[:, kg_window]
        for by in range(1, n_mp):
            sender = lax.rem(mp + n_mp - by, n_mp)
            kg_copy(mp, sender).wait_recv()
            total = total + kg_land[sender]
        scale = (frames * n_mp) ** (-0.5)
        even, odd = total[:taps, :own], total[:taps, 2 * LANES - own :]
        kg_out[0] = jnp.where(column == 0, even, odd) * scale
        for by in range(1, n_mp):
            kg_copy(lax.rem(mp + by, n_mp), mp).wait_send()
        passed()
    else:
        kg_out[0] = kg_ref[:taps, :]

    out_copy.wait()
    gin_copy.wait()
    halo_sent(pm, 0)
    halo_sent(pg, 2)

    @pl.when(seg < n_seg - 1)
    def _():
        for tile in range(tiles):
            in_copy(tile).wait_send()

    @pl.when(seg > 0)
    def _():
        for block in range(blocks):
            up_copy(block).wait_send()


def on_device(frames_in, section_weights, conv_kernels, valid_length, out_cotangent):
    frames, width = frames_in.shape
    taps = conv_kernels.shape[1]
    n_mp = lax.axis_size("mp")
    own = width // n_mp
    if width == 1536 and n_mp == 8 and frames == 128:
        return spread_call(frames_in, section_weights, conv_kernels, valid_length, out_cotangent)
    relay = False
    weight = section_weights[0]
    if not relay:
        weight = lax.all_gather(weight, "mp", axis=0, tiled=True)
    vmem = pl.BlockSpec(memory_space=pltpu.VMEM)
    smem = pl.BlockSpec(memory_space=pltpu.SMEM)
    whole = pl.BlockSpec(memory_space=pl.ANY)
    padded = (frames + 2 * PAD, width)
    tap_rows = -(-taps // 8) * 8
    dma = pltpu.SemaphoreType.DMA
    out, gin, grad = pl.pallas_call(
        functools.partial(cascade, relay),
        out_shape=(
            jax.ShapeDtypeStruct((1, frames, width), BF),
            jax.ShapeDtypeStruct((1, frames, width), BF),
            jax.ShapeDtypeStruct((1, taps, own if relay else width), F32),
        ),
        in_specs=[whole, whole, whole, smem, whole],
        out_specs=(whole, whole, vmem),
        scratch_shapes=[
            pltpu.VMEM((frames, width), BF),
            pltpu.VMEM((frames, width), BF),
            pltpu.VMEM((frames, width), F32),
            pltpu.VMEM((frames, LANES), F32),
            pltpu.VMEM(padded, BF),
            pltpu.VMEM(padded, BF),
            pltpu.VMEM((frames, width), BF),
            pltpu.VMEM((frames, width), F32),
            pltpu.VMEM((frames, width), F32),
            pltpu.VMEM((frames, width), BF),
            pltpu.VMEM((frames, width), BF),
            pltpu.VMEM((width, width), BF),
            pltpu.VMEM((taps, width), BF),
            pltpu.VMEM((taps, width), F32),
            pltpu.VMEM((tap_rows, width), F32),
            pltpu.VMEM((n_mp if relay else 1, tap_rows, 2 * LANES), F32),
            dma((4,)), dma((4,)),
            dma((width // WIDE,)), dma((width // WIDE,)),
            dma((frames // ROWS,)), dma((frames // ROWS,)),
            dma((6,)),
            dma((3, n_mp)), dma((n_mp,)), dma((2,)), dma((2,)), dma((n_mp,)), dma((n_mp,)),
            pltpu.SemaphoreType.REGULAR,
        ],
        compiler_params=pltpu.CompilerParams(
            collective_id=0, has_side_effects=True, vmem_limit_bytes=60 * 2**20
        ),
    )(frames_in, weight, conv_kernels[0], valid_length, out_cotangent)
    if not relay:
        grad = lax.psum_scatter(grad, "mp", scatter_dimension=2, tiled=True)
        grad = grad * (frames * n_mp) ** (-0.5)
    return (out, gin, grad)


def solution(mesh):
    in_specs = (
        P("mp", None),
        P("segment", "mp", None),
        P("segment", None, None),
        P(),
        P("mp", None),
    )
    out_specs = (P("segment", "mp", None), P("segment", "mp", None), P("segment", None, "mp"))
    return jax.shard_map(
        on_device, mesh=mesh, in_specs=in_specs, out_specs=out_specs, check_vma=False
    )
```

```python
import functools

import jax
import jax.numpy as jnp
from jax import lax
from jax.experimental import pallas as pl
from jax.experimental.pallas import tpu as pltpu
from jax.sharding import PartitionSpec as P

EPSILON = 1e-05
PAD = 16
LANES = 128
ROWS = 16
WIDE = 256
MESH = pl.DeviceIdType.MESH
NORM_ROWS = 32
BF = jnp.bfloat16
F32 = jnp.float32

STAGES = ((0, 0, 0), (1, 0, 0), (1, 0, 1), (2, 0, 0), (2, 0, 1), (0, 1, 0), (1, 1, 0), (1, 1, 1), (2, 1, 0), (2, 1, 1), (0, 2, 0), (1, 2, 0), (1, 2, 1), (2, 2, 0), (2, 2, 1), (0, 3, 0), (1, 3, 0), (1, 3, 1), (3, 3, 0),)
INNER_0 = (
    (13, 76, 74, 8, 10, 73,),
    (47, 87, 271, 80, 81, 206, 111, 23, 335, 70, 16, 17,),
    (),
    (119, 215, 343, 100, 142, 201, 55, 95, 303, 6, 40, 89, 239, 151, 279, 134, 144, 209, 31, 127, 367, 199, 25, 194, 136, 247, 159, 359, 39, 232, 145, 354, 63, 223, 311,),
    (),
    (),
    (295, 137, 208, 290, 183, 375, 383, 263, 240, 153, 258,),
    (),
    (175, 319, 399, 327, 200, 217, 322, 191, 287, 463, 231, 255, 351, 167,),
    (),
    (486,),
    (391, 495, 386,),
    (),
    (511, 423,),
    (),
    (407, 418, 401,),
    (415, 455, 431, 450,),
    (),
    (439, 447, 471, 479, 503,),
)
INNER_1 = (
    (268, 333, 330, 265, 266, 328,),
    (79, 327, 367, 343, 73, 322, 336, 15, 263, 303, 279, 258, 296, 273,),
    (),
    (71, 111, 87, 351, 66, 81, 272, 7, 23, 311, 287, 2, 17, 360, 103, 119, 95, 359, 98, 352, 337, 39, 47, 55, 31, 34, 304, 345, 127, 167, 151, 375, 162, 145, 368, 63, 199, 143, 383,),
    (),
    (),
    (194, 137, 396, 231, 239, 183, 191, 226, 281, 460,),
    (),
    (135, 175, 215, 223, 130, 457, 247, 255, 319, 484, 393, 394, 207, 159, 295, 492,),
    (458,),
    (),
    (391, 431, 404, 401, 386,),
    (455, 471, 424, 465,),
    (450,),
    (),
    (439,),
    (423, 415, 464, 409, 503,),
    (479, 496, 473,),
    (447, 511,),
)
CORNER_0 = (68, 65, 4, 1, 66, 103, 327, 132, 129, 98, 39, 263, 32, 197, 2, 167, 295, 192, 130, 231, 391, 194, 455, 34, 423, 290, 258, 322, 226, 162, 386, 418, 450,)
CORNER_1 = (261, 324, 322, 256, 258, 321, 71, 295, 66, 288, 389, 7, 359, 2, 384, 453, 135, 423, 129, 354, 448, 39, 487, 34, 416, 199, 167, 193, 162, 194, 230, 130, 482, 290, 386, 450, 418,)
SENDS = 50
PIECES = 2
LATE = ((3,), (), (1,), (0, 2))


def decode(event):
    return event // 128, event // 64 % 2, event // 32 % 2, event // 8 % 4, event // 4 % 2, event % 4


def spread(
    x_any, w_any, k_any, vl_ref, cot_any,
    out_whole, gin_whole, kg_out,
    w, a, up, norm, inv, pm, pg, act, slope, gs, k_bf, k_ref, kg, kg_sib, kg_sum, kg_land,
    local_sem, x_send, x_recv, k_send, k_recv, own_send, rel_send, rel_recv, sib_send, sib_recv,
    halo_send, halo_recv, out_send, out_recv, gin_send, gin_recv, pair_send, pair_recv, kg_send, kg_recv,
):
    n_sec, rows_in, width = w.shape
    part = a.shape[1]
    taps = k_ref.shape[1]
    seg, mp = lax.axis_index("segment"), lax.axis_index("mp")
    n_seg, n_mp = lax.axis_size("segment"), lax.axis_size("mp")
    own = rows_in // n_mp
    half = own // (2 * PIECES)
    chunks = width // LANES
    tiles = width // WIDE
    x, c = lax.div(seg, 2), lax.rem(seg, 2)
    z, y = lax.div(mp, 2), lax.rem(mp, 2)
    inner = (z == 1) | (z == 2)
    block = jnp.where(c == 1, mp, jnp.where(z == 1, y, 6 + y))
    which = x + y - 2 * x * y
    chunk_id = 2 * block + which
    chip = 4 * x + mp - 2

    def device_of(number, half_of):
        side, core = number % 2, ((number >= 2) & (number < 6)) * 1
        return 2 * (half_of + side - 2 * half_of * side) + core, (number >= 4) * 2 + 2 + side

    barrier = pltpu.get_barrier_semaphore()
    me = seg * n_mp + mp
    total = n_seg * n_mp

    @pl.loop(1, total)
    def _(by):
        other = lax.rem(me + by, total)
        pl.semaphore_signal(
            barrier, inc=1, device_id=(lax.div(other, n_mp), lax.rem(other, n_mp)), device_id_type=MESH
        )

    w_copy = pltpu.make_async_copy(
        w_any, w.at[seg, pl.ds(pl.multiple_of(own * mp, own), own)], local_sem.at[0]
    )
    k_copy = pltpu.make_async_copy(k_any, k_bf.at[seg], local_sem.at[1])
    w_copy.start()

    @pl.when(inner)
    def _():
        k_copy.start()

    pl.semaphore_wait(barrier, total - 1)

    def half_ref(section, shard, piece, core):
        start = own * shard + half * (2 * piece + core)
        return w.at[section, pl.ds(pl.multiple_of(start, half), half)]

    def own_copy(kind, piece):
        core = c if kind else 1 - c
        return pltpu.make_async_remote_copy(
            src_ref=half_ref(seg, mp, piece, core), dst_ref=half_ref(seg, mp, piece, core),
            send_sem=own_send.at[2 * piece + kind],
            recv_sem=(sib_recv if kind else rel_recv).at[(seg * n_mp + mp) * PIECES + piece],
            device_id={"segment": seg + 1 - 2 * c}, device_id_type=MESH,
        )

    def relay_copy(section, shard, piece, way, slot):
        target = (
            {"segment": seg + 2 - 4 * x}, {"mp": mp + 1 - 2 * y}, {"mp": mp + jnp.where(z < 2, 2, -2)}
        )[way]
        return pltpu.make_async_remote_copy(
            src_ref=half_ref(section, shard, piece, c), dst_ref=half_ref(section, shard, piece, c),
            send_sem=rel_send.at[slot], recv_sem=rel_recv.at[(section * n_mp + shard) * PIECES + piece],
            device_id=target, device_id_type=MESH,
        )

    def sib_copy(section, shard, piece, core):
        sem = (section * n_mp + shard) * PIECES + piece
        return pltpu.make_async_remote_copy(
            src_ref=half_ref(section, shard, piece, core), dst_ref=half_ref(section, shard, piece, core),
            send_sem=sib_send.at[sem], recv_sem=sib_recv.at[sem],
            device_id={"segment": seg + 1 - 2 * c}, device_id_type=MESH,
        )

    def shard_of(across, depth):
        from_y = 1 - y if across else y
        return 2 * jnp.where(z < 2, depth, 3 - depth) + from_y

    def is_home(section, across, depth, plane, corner):
        return section // 2 == plane and across == 0 and depth == (0 if corner else 1)

    def run_events(events, plane, corner, slot):
        for event in events:
            section, piece, across, depth, first, way = decode(event)
            shard = shard_of(across, depth)
            if first and is_home(section, across, depth, plane, corner):
                pl.when(c != section % 2)(relay_copy(section, shard, piece, 0, 0).wait_recv)
            elif first:
                relay_copy(section, shard, piece, 0, 0).wait_recv()
                if not corner:
                    sib_copy(section, shard, piece, c).start()
            if way < 3:
                relay_copy(section, shard, piece, way, slot).start()
                slot += 1
        return slot

    def finish_events(groups, plane, corner):
        slot = 0
        for events in groups:
            for event in events:
                section, piece, across, depth, first, way = decode(event)
                shard = shard_of(across, depth)
                if first and not corner and not is_home(section, across, depth, plane, corner):
                    sib_copy(section, shard, piece, c).wait_send()
                if way < 3:
                    relay_copy(section, shard, piece, way, slot).wait_send()
                    slot += 1

    def siblings(section, plane):
        for across in range(2):
            for depth in range(4):
                for piece in range(PIECES):
                    wait = sib_copy(section, shard_of(across, depth), piece, 1 - c).wait_recv
                    if is_home(section, across, depth, plane, False):
                        pl.when(c != section % 2)(wait)
                    else:
                        wait()

    to_seg, to_mp = device_of(mp, which)
    sends_x = seg == to_seg
    away = sends_x & (to_mp != mp)

    def x_move(index, remote):
        rows = pl.ds(pl.multiple_of(part * which, part), part)
        source, target = ((x_any, a.at[0]), (cot_any, up.at[n_sec]))[index]
        if not remote:
            return pltpu.make_async_copy(source.at[rows], target, x_recv.at[index])
        return pltpu.make_async_remote_copy(
            src_ref=source.at[rows], dst_ref=target, send_sem=x_send.at[index], recv_sem=x_recv.at[index],
            device_id={"mp": to_mp}, device_id_type=MESH,
        )

    def x_start(index):
        pl.when(inner & (c == 1))(lambda: x_move(index, False).start())
        pl.when(away)(lambda: x_move(index, True).start())

    def x_wait(index):
        pl.when(c == 1)(lambda: x_move(index, False).wait())
        pl.when(c == 0)(lambda: x_move(index, True).wait_recv())

    def k_move(by, sender):
        return pltpu.make_async_remote_copy(
            src_ref=k_any, dst_ref=k_bf.at[sender], send_sem=k_send.at[by - 1], recv_sem=k_recv.at[sender],
            device_id={"segment": lax.rem(seg + by, n_seg)}, device_id_type=MESH,
        )

    w_copy.wait()
    for piece in range(PIECES):
        own_copy(0, piece).start()
        pl.when(inner)(own_copy(1, piece).start)

    @pl.when(inner)
    def _():
        for by in range(1, n_sec):
            k_move(by, seg).start()

    x_start(0)

    corner = jnp.logical_not(inner)
    for plane, table in ((0, CORNER_0), (1, CORNER_1)):

        @pl.when(corner & (x == plane))
        def _():
            run_events(table, plane, True, 0)

    x_start(1)

    def mask_rows(start, count):
        position = chunk_id * part + start + lax.broadcasted_iota(jnp.int32, (count, LANES), 0)
        return (position < vl_ref[0]).astype(F32)

    def halo_copy(pad_ref, section, slot, to_next):
        rows_from = pl.ds(part, PAD) if to_next else pl.ds(PAD, PAD)
        rows_to = pl.ds(0, PAD) if to_next else pl.ds(part + PAD, PAD)
        near = chunk_id + (1 if to_next else -1)
        target = device_of(lax.div(near, 2), lax.rem(near, 2))
        sem = 6 * section + 2 * slot + (0 if to_next else 1)
        columns = pl.ds(0, width) if slot == 0 else pl.ds((slot - 1) * side, side)
        return pltpu.make_async_remote_copy(
            src_ref=pad_ref.at[section, rows_from, columns], dst_ref=pad_ref.at[section, rows_to, columns],
            send_sem=halo_send.at[sem], recv_sem=halo_recv.at[sem],
            device_id=target, device_id_type=MESH,
        )

    last = 2 * n_mp - 1
    side = width // 2

    def halo_start(pad_ref, section, slot):
        pl.when(chunk_id < last)(lambda: halo_copy(pad_ref, section, slot, True).start())
        pl.when(chunk_id > 0)(lambda: halo_copy(pad_ref, section, slot, False).start())

    def halo_wait(pad_ref, section, slot):
        pl.when(chunk_id > 0)(lambda: halo_copy(pad_ref, section, slot, True).wait_recv())
        pl.when(chunk_id < last)(lambda: halo_copy(pad_ref, section, slot, False).wait_recv())

    def halo_sent(pad_ref, section, slot):
        pl.when(chunk_id < last)(lambda: halo_copy(pad_ref, section, slot, True).wait_send())
        pl.when(chunk_id > 0)(lambda: halo_copy(pad_ref, section, slot, False).wait_send())

    def tap_sum(padded, section, columns, forward):
        rows = padded.shape[0]
        running = jnp.zeros((part, LANES), F32)
        for r in range(8):
            moved = padded if r == 0 else pltpu.roll(padded, rows - r, 0)
            for base in range(0, 2 * PAD, 8):
                offset = base + r
                if 1 <= offset <= taps:
                    tap = offset - 1 if forward else taps - offset
                    running = running + k_ref[section, tap : tap + 1, columns] * moved[base : base + part]
        return running

    def normalize(section):
        for start in range(0, part, NORM_ROWS):
            rows = slice(start, start + NORM_ROWS)
            values = a[section, rows].astype(F32)
            center = values - jnp.mean(values, axis=-1, keepdims=True)
            inverse = lax.rsqrt(jnp.mean(center * center, axis=-1, keepdims=True) + EPSILON)
            normed = center * inverse
            norm[section, rows] = normed
            inv[section, rows] = jnp.broadcast_to(inverse, (NORM_ROWS, LANES))
            pm[section, PAD + start : PAD + start + NORM_ROWS] = (
                normed * mask_rows(start, NORM_ROWS)[:, :1]
            ).astype(BF)
        halo_start(pm, section, 0)

    def convolve(section, step):
        if step == 0:
            halo_wait(pm, section, 0)

        @pl.loop(step * chunks // 2, (step + 1) * chunks // 2)
        def _(chunk):
            columns = pl.ds(pl.multiple_of(chunk * LANES, LANES), LANES)
            conv = tap_sum(pm[section, :, columns].astype(F32), section, columns, True)
            gate = jax.nn.sigmoid(conv)
            act[section, :, columns] = (conv * gate).astype(BF)
            slope[section, :, columns] = gate * (1.0 + conv * (1.0 - gate))

    def result_copy(source, index, section, whole, send, recv, remote):
        rows = pl.ds(pl.multiple_of(part * which, part), part)
        if not remote:
            return pltpu.make_async_copy(source.at[index], whole.at[0, rows], recv.at[which])
        return pltpu.make_async_remote_copy(
            src_ref=source.at[index], dst_ref=whole.at[0, rows],
            send_sem=send.at[section], recv_sem=recv.at[which],
            device_id=(section, block), device_id_type=MESH,
        )

    def result_start(section, *what):
        same = (seg == section) & (mp == block)
        pl.when(same)(lambda: result_copy(*what, False).start())
        pl.when(jnp.logical_not(same))(lambda: result_copy(*what, True).start())

    def result_sent(section, *what):
        same = (seg == section) & (mp == block)
        pl.when(jnp.logical_not(same))(lambda: result_copy(*what, True).wait_send())

    def result_wait(source, whole, send, recv):
        for half_of in range(2):
            from_seg, from_mp = device_of(mp, half_of)
            same = (seg == from_seg) & (mp == from_mp)
            rows = pl.ds(part * half_of, part)

            @pl.when(same)
            def _():
                pltpu.make_async_copy(source.at[0], whole.at[0, rows], recv.at[half_of]).wait()

            @pl.when(jnp.logical_not(same))
            def _():
                pltpu.make_async_remote_copy(
                    src_ref=source.at[0], dst_ref=whole.at[0, rows],
                    send_sem=send.at[0], recv_sem=recv.at[half_of],
                    device_id=(seg, mp), device_id_type=MESH,
                ).wait_recv()

    def product(section, step):
        for tile in range(step * tiles // 2, (step + 1) * tiles // 2):
            columns = slice(tile * WIDE, (tile + 1) * WIDE)
            result = jnp.dot(act[section], w[section, :, columns], preferred_element_type=F32)
            a[section + 1, :, columns] = (a[section, :, columns].astype(F32) + result).astype(BF)

    def out_what(section):
        return section, a, section + 1, section, out_whole, out_send, out_recv

    def gin_what(section):
        return section, up, section, section, gin_whole, gin_send, gin_recv

    def out_start(section, late):
        at_once = (c == 0) | (x == section // 2)
        pl.when(jnp.logical_not(at_once) if late else at_once)(lambda: result_start(*out_what(section)))

    def gin_start(section, late):
        pl.when(c == (1 if late else 0))(lambda: result_start(*gin_what(section)))

    def forward_stage(kind, section, step):
        if kind == 0:
            if section == 0:
                x_wait(0)
                k_copy.wait()
                for by in range(1, n_sec):
                    k_move(by, lax.rem(seg + n_seg - by, n_seg)).wait_recv()
                for s in range(n_sec):
                    k_ref[s] = k_bf[s].astype(F32)
                for pad_ref in (pm, pg):

                    @pl.when(chunk_id == 0)
                    def _():
                        for s in range(n_sec):
                            pad_ref[s, 0:PAD, :] = jnp.zeros((PAD, width), BF)

                    @pl.when(chunk_id == last)
                    def _():
                        for s in range(n_sec):
                            pad_ref[s, part + PAD : part + 2 * PAD, :] = jnp.zeros((PAD, width), BF)

                kg[:, taps:, :] = jnp.zeros((n_sec, kg.shape[1] - taps, width), F32)
            normalize(section)
        elif kind == 1:
            convolve(section, step)
        elif kind == 3:
            for plane in range(2):
                pl.when(x == plane)(lambda: siblings(section, plane))
            last_back_product()
        else:
            if step == 0:
                for plane in range(2):
                    pl.when(x == plane)(lambda: siblings(section, plane))
            product(section, step)
            if step == 1:
                out_start(section, False)

    def kg_window(index, core):
        return pl.ds(pl.multiple_of(384 * index + 128 * core, LANES), 2 * LANES)

    def kg_pair(section):
        return pltpu.make_async_remote_copy(
            src_ref=kg.at[section], dst_ref=kg_sib.at[section],
            send_sem=pair_send.at[section], recv_sem=pair_recv.at[section],
            device_id={"segment": seg + 1 - 2 * c}, device_id_type=MESH,
        )

    def kg_copy(section, index, remote):
        if not remote:
            return pltpu.make_async_copy(kg_sum.at[section, index], kg_land.at[chip], kg_recv.at[chip])
        return pltpu.make_async_remote_copy(
            src_ref=kg_sum.at[section, index], dst_ref=kg_land.at[chip],
            send_sem=kg_send.at[4 * section + index], recv_sem=kg_recv.at[chip],
            device_id=(section, 2 * index + c), device_id_type=MESH,
        )

    def kg_start(section):
        kg_pair(section).wait_recv()
        for index in range(n_mp // 2):
            window = kg_window(index, c)
            kg_sum[section, index] = kg[section, :, window] + kg_sib[section, :, window]
            same = (seg == section) & (mp == 2 * index + c)
            pl.when(same)(lambda: kg_copy(section, index, False).start())
            pl.when(jnp.logical_not(same))(lambda: kg_copy(section, index, True).start())

    def tap_grads(section):
        @pl.loop(0, chunks)
        def _(chunk):
            columns = pl.ds(pl.multiple_of(chunk * LANES, LANES), LANES)
            padded = pm[section, :, columns].astype(F32)
            grad = pg[section, PAD : PAD + part, columns].astype(F32)
            rows = padded.shape[0]
            for r in range(8):
                moved = padded if r == 0 else pltpu.roll(padded, rows - r, 0)
                for base in range(0, 2 * PAD, 8):
                    tap = base + r - 1
                    if 0 <= tap < taps:
                        kg[section, tap : tap + 1, columns] = jnp.sum(
                            grad * moved[base : base + part], axis=0, keepdims=True
                        )

        kg_pair(section).start()

    def back_tile(section, tile):
        columns = slice(tile * WIDE, (tile + 1) * WIDE)
        return columns, lax.dot_general(
            up[section + 1], w[section, columns, :], (((1,), (1,)), ((), ())), preferred_element_type=F32
        )

    def last_back_product():
        x_wait(1)
        for tile in range(tiles):
            columns, grad = back_tile(n_sec - 1, tile)
            gs[:, columns] = grad

    def backward(section):
        for part_of in range(2):
            for tile in range(part_of * tiles // 2, (part_of + 1) * tiles // 2):
                if section == n_sec - 1:
                    columns = slice(tile * WIDE, (tile + 1) * WIDE)
                    grad = gs[:, columns]
                else:
                    columns, grad = back_tile(section, tile)
                pg[section, PAD : PAD + part, columns] = (grad * slope[section, :, columns]).astype(BF)
            halo_start(pg, section, 1 + part_of)
        tap_grads(section)
        if section == n_sec - 1:
            product(section, 0)
            product(section, 1)
            out_start(section, False)
        else:
            kg_start(section + 1)
        for part_of in range(2):
            halo_wait(pg, section, 1 + part_of)
            if part_of == 1:
                if section < n_sec - 1:
                    gin_start(section + 1, True)
                for other in LATE[section]:
                    out_start(other, True)
                if section == 0:
                    kg_start(section)

            @pl.loop(part_of * chunks // 2, (part_of + 1) * chunks // 2)
            def _(chunk):
                columns = pl.ds(pl.multiple_of(chunk * LANES, LANES), LANES)
                gs[:, columns] = tap_sum(
                    pg[section, :, columns].astype(F32), section, columns, False
                ) * mask_rows(0, part)

        for start in range(0, part, NORM_ROWS):
            rows = slice(start, start + NORM_ROWS)
            masked = gs[rows]
            normed = norm[section, rows]
            first = jnp.mean(masked, axis=-1, keepdims=True)
            second = jnp.mean(masked * normed, axis=-1, keepdims=True)
            grad = inv[section, rows][:, :1] * (masked - first - normed * second)
            up[section, rows] = (up[section + 1, rows].astype(F32) + grad).astype(BF)
        gin_start(section, False)
        if section == 0:
            gin_start(section, True)

    slots = [0, 0]
    for index, (kind, section, step) in enumerate(STAGES):
        for plane, table in ((0, INNER_0), (1, INNER_1)):
            if table[index]:
                start = slots[plane]

                @pl.when(inner & (x == plane))
                def _():
                    run_events(table[index], plane, False, start)

                slots[plane] += sum(event % 4 < 3 for event in table[index])
        pl.when(inner)(lambda: forward_stage(kind, section, step))
    @pl.when(inner)
    def _():
        for section in reversed(range(n_sec)):
            backward(section)

    sums = jnp.zeros((kg.shape[1], 2 * LANES), F32)
    for number in range(n_mp):
        from_seg, from_mp = 2 * (number // 4) + y, number % 4 + 2
        same = (seg == from_seg) & (mp == from_mp)

        @pl.when(same)
        def _():
            pltpu.make_async_copy(kg_sum.at[0, 0], kg_land.at[number], kg_recv.at[number]).wait()

        @pl.when(jnp.logical_not(same))
        def _():
            pltpu.make_async_remote_copy(
                src_ref=kg_sum.at[0, 0], dst_ref=kg_land.at[number],
                send_sem=kg_send.at[0], recv_sem=kg_recv.at[number],
                device_id=(seg, mp), device_id_type=MESH,
            ).wait_recv()

        sums = sums + kg_land[number]
    scale = (2 * part * n_mp) ** (-0.5)
    even, odd = sums[:taps, :own], sums[:taps, 2 * LANES - own :]
    kg_out[:, 0, :] = jnp.where(y == 0, even, odd) * scale

    result_wait(a, out_whole, out_send, out_recv)
    result_wait(up, gin_whole, gin_send, gin_recv)

    for piece in range(PIECES):
        own_copy(0, piece).wait_send()
    for index in range(2):
        pl.when(away)(lambda: x_move(index, True).wait_send())
    for plane, table in ((0, CORNER_0), (1, CORNER_1)):
        pl.when(corner & (x == plane))(lambda: finish_events((table,), plane, True))
    for plane, table in ((0, INNER_0), (1, INNER_1)):
        pl.when(inner & (x == plane))(lambda: finish_events(table, plane, False))

    @pl.when(inner)
    def _():
        for piece in range(PIECES):
            own_copy(1, piece).wait_send()
        for by in range(1, n_sec):
            k_move(by, seg).wait_send()
        for section in range(n_sec):
            halo_sent(pm, section, 0)
            halo_sent(pg, section, 1)
            halo_sent(pg, section, 2)
            result_sent(*out_what(section))
            result_sent(*gin_what(section))
            kg_pair(section).wait_send()
            for index in range(n_mp // 2):
                same = (seg == section) & (mp == 2 * index + c)
                pl.when(jnp.logical_not(same))(lambda: kg_copy(section, index, True).wait_send())


def spread_call(frames_in, section_weights, conv_kernels, valid_length, out_cotangent):
    frames, width = frames_in.shape
    taps = conv_kernels.shape[1]
    n_sec, n_mp = lax.axis_size("segment"), lax.axis_size("mp")
    own = width // n_mp
    part = frames // 2
    vmem = pl.BlockSpec(memory_space=pltpu.VMEM)
    smem = pl.BlockSpec(memory_space=pltpu.SMEM)
    whole = pl.BlockSpec(memory_space=pl.ANY)
    tap_rows = -(-taps // 8) * 8
    dma = pltpu.SemaphoreType.DMA
    out, gin, grad = pl.pallas_call(
        spread,
        out_shape=(
            jax.ShapeDtypeStruct((1, frames, width), BF),
            jax.ShapeDtypeStruct((1, frames, width), BF),
            jax.ShapeDtypeStruct((taps, 1, own), F32),
        ),
        in_specs=[whole, whole, whole, smem, whole],
        out_specs=(whole, whole, vmem),
        scratch_shapes=[
            pltpu.VMEM((n_sec, width, width), BF),
            pltpu.VMEM((n_sec + 1, part, width), BF),
            pltpu.VMEM((n_sec + 1, part, width), BF),
            pltpu.VMEM((n_sec, part, width), F32),
            pltpu.VMEM((n_sec, part, LANES), F32),
            pltpu.VMEM((n_sec, part + 2 * PAD, width), BF),
            pltpu.VMEM((n_sec, part + 2 * PAD, width), BF),
            pltpu.VMEM((n_sec, part, width), BF),
            pltpu.VMEM((n_sec, part, width), F32),
            pltpu.VMEM((part, width), F32),
            pltpu.VMEM((n_sec, taps, width), BF),
            pltpu.VMEM((n_sec, taps, width), F32),
            pltpu.VMEM((n_sec, tap_rows, width), F32),
            pltpu.VMEM((n_sec, tap_rows, width), F32),
            pltpu.VMEM((n_sec, n_mp // 2, tap_rows, 2 * LANES), F32),
            pltpu.VMEM((n_mp, tap_rows, 2 * LANES), F32),
            dma((2,)), dma((2,)), dma((2,)), dma((n_sec - 1,)), dma((n_sec,)),
            dma((2 * PIECES,)), dma((SENDS,)),
            dma((PIECES * n_sec * n_mp,)), dma((PIECES * n_sec * n_mp,)), dma((PIECES * n_sec * n_mp,)),
            dma((6 * n_sec,)), dma((6 * n_sec,)),
            dma((n_sec,)), dma((2,)), dma((n_sec,)), dma((2,)),
            dma((n_sec,)), dma((n_sec,)), dma((4 * n_sec,)), dma((n_mp,)),
        ],
        compiler_params=pltpu.CompilerParams(
            collective_id=1, has_side_effects=True, vmem_limit_bytes=60 * 2**20
        ),
    )(frames_in, section_weights[0], conv_kernels[0], valid_length, out_cotangent)
    return out, gin, grad.transpose(1, 0, 2)


def cascade(
    relay, x_any, w_any, k_any, vl_ref, cot_any,
    out_whole, gin_whole, kg_out,
    cur, up, norm, inv, pm, pg, act, slope, gs, out_ref, gin_ref, w_ref, k_bf, k_ref, kg_ref, kg_land,
    halo_send, halo_recv, in_send, in_recv, up_send, up_recv,
    local_sem, w_send, w_recv, end_send, end_recv, kg_send, kg_recv, turn_sem,
):
    frames, width = x_any.shape
    taps = k_ref.shape[0]
    seg, mp = lax.axis_index("segment"), lax.axis_index("mp")
    n_seg, n_mp = lax.axis_size("segment"), lax.axis_size("mp")
    chunks = width // LANES
    blocks = frames // ROWS
    tiles = width // WIDE

    barrier = pltpu.get_barrier_semaphore()
    steps_mp = range(1, n_mp) if relay else (1, n_mp - 1)
    for axis, index, count, steps in (
        ("segment", seg, n_seg, (1, n_seg - 1)), ("mp", mp, n_mp, steps_mp)
    ):
        for by in steps:
            pl.semaphore_signal(
                barrier, inc=1, device_id={axis: lax.rem(index + by, count)}, device_id_type=MESH
            )
    own = width // n_mp
    w_rows = pl.ds(pl.multiple_of(mp * own, own), own) if relay else pl.ds(0, width)
    w_copy = pltpu.make_async_copy(w_any, w_ref.at[w_rows], local_sem.at[0])
    x_copy = pltpu.make_async_copy(x_any, cur, local_sem.at[1])
    cot_copy = pltpu.make_async_copy(cot_any, up, local_sem.at[2])
    k_copy = pltpu.make_async_copy(k_any, k_bf, local_sem.at[3])
    out_copy = pltpu.make_async_copy(out_ref, out_whole.at[0], local_sem.at[4])
    gin_copy = pltpu.make_async_copy(gin_ref, gin_whole.at[0], local_sem.at[5])
    w_copy.start()
    k_copy.start()

    @pl.when(seg == 0)
    def _():
        x_copy.start()

    @pl.when(seg == n_seg - 1)
    def _():
        cot_copy.start()

    pl.semaphore_wait(barrier, 2 + len(steps_mp))

    row, column = lax.div(mp, 2), lax.rem(mp, 2)
    n_row = n_mp // 2

    half = own // 2

    def block_copy(block, way, count=own):
        rows = pl.ds(pl.multiple_of(block * own, own), count)
        target = (mp + 2, mp - 2, mp + 1 - 2 * column)[way]
        return pltpu.make_async_remote_copy(
            src_ref=w_ref.at[rows], dst_ref=w_ref.at[rows],
            send_sem=w_send.at[way, block], recv_sem=w_recv.at[block],
            device_id={"mp": target}, device_id_type=MESH,
        )

    def end_copy(way):
        block = (0 if way == 0 else n_mp - 2) + 1 - column
        rows = pl.ds(pl.multiple_of(block * own + half, half), half)
        return pltpu.make_async_remote_copy(
            src_ref=w_ref.at[rows], dst_ref=w_ref.at[rows],
            send_sem=end_send.at[way], recv_sem=end_recv.at[way],
            device_id={"mp": mp + 2 if way == 0 else mp - 2}, device_id_type=MESH,
        )

    def each_block(distance, act_on, arrive):
        if distance == 0:
            pl.when(row < n_row - 1)(lambda: act_on(mp, 0))
            pl.when(row > 0)(lambda: act_on(mp, 1))
            act_on(mp, 2)
            return
        low, high = mp - 2 * distance, mp + 2 * distance

        @pl.when(row >= distance)
        def _():
            arrive(low)
            pl.when(row < n_row - 1)(lambda: act_on(low, 0))
            pl.when(row == distance)(lambda: act_on(low, 2, half))
            pl.when(row > distance)(lambda: act_on(low, 2))

        @pl.when(row + distance < n_row)
        def _():
            arrive(high)
            pl.when(row > 0)(lambda: act_on(high, 1))
            pl.when(row + distance == n_row - 1)(lambda: act_on(high, 2, half))
            pl.when(row + distance < n_row - 1)(lambda: act_on(high, 2))

    def pass_on(distance):
        each_block(
            distance,
            lambda *what: block_copy(*what).start(),
            lambda block: block_copy(block, 0).wait_recv(),
        )
        if distance == 1:
            for way, end in ((0, 0), (1, n_row - 1)):

                @pl.when(row == end)
                def _():
                    block_copy(2 * end + 1 - column, 2).wait_recv()
                    end_copy(way).start()

    def passed():
        for distance in range(n_row):
            each_block(
                distance,
                lambda *what: block_copy(*what).wait_send(),
                lambda block: None,
            )
        pl.when(row < n_row - 1)(lambda: end_copy(0).wait_send())
        pl.when(row > 0)(lambda: end_copy(1).wait_send())

    def gather_rest(first):
        if relay:
            for distance in range(first, n_row):
                pass_on(distance)

            @pl.when(row > 0)
            def _():
                end_copy(0).wait_recv()
                pl.when(row < n_row - 1)(lambda: end_copy(0).start())

            @pl.when(row < n_row - 1)
            def _():
                end_copy(1).wait_recv()
                pl.when(row > 0)(lambda: end_copy(1).start())

            for index in range(n_row):
                block = index * 2 + 1 - column
                if index in (0, n_row - 1):
                    pl.when(row != index)(lambda: block_copy(block, 2, half).wait_recv())
                else:
                    block_copy(block, 2).wait_recv()

    def kg_copy(target, sender):
        start = 384 * lax.div(target, 2) + 128 * lax.rem(target, 2)
        window = pl.ds(pl.multiple_of(start, LANES), 2 * LANES)
        return pltpu.make_async_remote_copy(
            src_ref=kg_ref.at[:, window], dst_ref=kg_land.at[sender],
            send_sem=kg_send.at[target], recv_sem=kg_recv.at[sender],
            device_id={"mp": target}, device_id_type=MESH,
        )

    w_copy.wait()
    if relay:

        @pl.when(seg != 1)
        def _():
            pass_on(0)

    k_copy.wait()
    k_ref[...] = k_bf[...].astype(F32)
    kg_ref[...] = jnp.zeros(kg_ref.shape, F32)

    def halo_copy(pad_ref, first, to_right):
        rows_from = pl.ds(frames, PAD) if to_right else pl.ds(PAD, PAD)
        rows_to = pl.ds(0, PAD) if to_right else pl.ds(frames + PAD, PAD)
        target = lax.rem(mp + (1 if to_right else n_mp - 1), n_mp)
        slot = first + (0 if to_right else 1)
        return pltpu.make_async_remote_copy(
            src_ref=pad_ref.at[rows_from], dst_ref=pad_ref.at[rows_to],
            send_sem=halo_send.at[slot], recv_sem=halo_recv.at[slot],
            device_id={"mp": target}, device_id_type=MESH,
        )

    def halo_start(pad_ref, first):
        @pl.when(mp < n_mp - 1)
        def _():
            halo_copy(pad_ref, first, True).start()

        @pl.when(mp > 0)
        def _():
            halo_copy(pad_ref, first, False).start()

    def halo_wait(pad_ref, first):
        @pl.when(mp > 0)
        def _():
            halo_copy(pad_ref, first, True).wait_recv()

        @pl.when(mp < n_mp - 1)
        def _():
            halo_copy(pad_ref, first, False).wait_recv()

    def halo_sent(pad_ref, first):
        @pl.when(mp < n_mp - 1)
        def _():
            halo_copy(pad_ref, first, True).wait_send()

        @pl.when(mp > 0)
        def _():
            halo_copy(pad_ref, first, False).wait_send()

    def halo_clear(pad_ref):
        @pl.when(mp == 0)
        def _():
            pad_ref[0:PAD, :] = jnp.zeros((PAD, width), BF)

        @pl.when(mp == n_mp - 1)
        def _():
            pad_ref[frames + PAD : frames + 2 * PAD, :] = jnp.zeros((PAD, width), BF)

    def in_copy(tile):
        columns = pl.ds(tile * WIDE, WIDE)
        return pltpu.make_async_remote_copy(
            src_ref=out_ref.at[:, columns], dst_ref=cur.at[:, columns],
            send_sem=in_send.at[tile], recv_sem=in_recv.at[tile],
            device_id={"segment": lax.rem(seg + 1, n_seg)}, device_id_type=MESH,
        )

    def up_copy(block):
        rows = pl.ds(block * ROWS, ROWS)
        return pltpu.make_async_remote_copy(
            src_ref=gin_ref.at[rows], dst_ref=up.at[rows],
            send_sem=up_send.at[block], recv_sem=up_recv.at[block],
            device_id={"segment": lax.rem(seg + n_seg - 1, n_seg)}, device_id_type=MESH,
        )

    def mask_rows(start, count):
        position = mp * frames + start + lax.broadcasted_iota(jnp.int32, (count, LANES), 0)
        return (position < vl_ref[0]).astype(F32)

    def back_product():
        for tile in range(tiles):
            columns = slice(tile * WIDE, (tile + 1) * WIDE)
            gs[:, columns] = lax.dot_general(
                up[...], w_ref[columns, :], (((1,), (1,)), ((), ())), preferred_element_type=F32
            )

    halo_clear(pm)
    halo_clear(pg)

    @pl.when(seg == n_seg - 1)
    def _():
        gather_rest(1)
        cot_copy.wait()
        back_product()

    @pl.when(seg == 0)
    def _():
        x_copy.wait()

    @pl.when(seg == 1)
    def _():
        if relay:
            pl.semaphore_wait(turn_sem, 1)
            pass_on(0)

    @pl.when((seg > 1) & (seg < n_seg - 1))
    def _():
        gather_rest(1)

    @pl.when(seg > 0)
    def _():
        for tile in range(tiles):
            in_copy(tile).wait_recv()

    def norm_rows(block):
        start = pl.multiple_of(block * ROWS, ROWS)
        rows = pl.ds(start, ROWS)
        values = cur[rows, :].astype(F32)
        center = values - jnp.mean(values, axis=-1, keepdims=True)
        inverse = lax.rsqrt(jnp.mean(center * center, axis=-1, keepdims=True) + EPSILON)
        normed = center * inverse
        norm[rows, :] = normed
        inv[rows, :] = jnp.broadcast_to(inverse, (ROWS, LANES))
        pm[pl.ds(pl.multiple_of(PAD + start, ROWS), ROWS), :] = (
            normed * mask_rows(start, ROWS)[:, :1]
        ).astype(BF)

    norm_rows(0)
    norm_rows(blocks - 1)
    halo_start(pm, 0)

    @pl.loop(1, blocks - 1)
    def _(block):
        norm_rows(block)

    if relay:

        @pl.when(seg < 2)
        def _():
            pass_on(1)

    halo_wait(pm, 0)

    def shifted(padded):
        total = padded.shape[0]
        return [padded if r == 0 else pltpu.roll(padded, total - r, 0) for r in range(8)]

    def tap_sum(padded, columns, forward):
        total = padded.shape[0]
        running = jnp.zeros((frames, LANES), F32)
        for r in range(8):
            moved = padded if r == 0 else pltpu.roll(padded, total - r, 0)
            for base in range(0, 2 * PAD, 8):
                offset = base + r
                if 1 <= offset <= taps:
                    tap = offset - 1 if forward else taps - offset
                    running = running + k_ref[tap : tap + 1, columns] * moved[base : base + frames]
        return running

    @pl.loop(0, chunks)
    def _(chunk):
        columns = pl.ds(pl.multiple_of(chunk * LANES, LANES), LANES)
        conv = tap_sum(pm[:, columns].astype(F32), columns, True)
        gate = jax.nn.sigmoid(conv)
        act[:, columns] = (conv * gate).astype(BF)
        slope[:, columns] = gate * (1.0 + conv * (1.0 - gate))

    if relay:

        @pl.when(seg < 2)
        def _():
            pass_on(2)

        @pl.when(seg == 0)
        def _():
            pl.semaphore_signal(
                turn_sem, inc=1, device_id={"segment": seg + 1}, device_id_type=MESH
            )

        @pl.when(seg < 2)
        def _():
            gather_rest(3)

    for tile in range(tiles):
        columns = slice(tile * WIDE, (tile + 1) * WIDE)
        product = jnp.dot(act[...], w_ref[:, columns], preferred_element_type=F32)
        out_ref[:, columns] = (cur[:, columns].astype(F32) + product).astype(BF)

        @pl.when(seg < n_seg - 1)
        def _():
            in_copy(tile).start()

    out_copy.start()

    @pl.when(seg < n_seg - 1)
    def _():
        for block in range(blocks):
            up_copy(block).wait_recv()
        back_product()

    def grad_rows(block):
        start = pl.multiple_of(block * ROWS, ROWS)
        rows = pl.ds(start, ROWS)
        pg[pl.ds(pl.multiple_of(PAD + start, ROWS), ROWS), :] = (
            gs[rows, :] * slope[rows, :]
        ).astype(BF)

    grad_rows(0)
    grad_rows(blocks - 1)
    halo_start(pg, 2)

    @pl.loop(1, blocks - 1)
    def _(block):
        grad_rows(block)

    kg_start = 384 * row + 128 * column
    kg_window = pl.ds(pl.multiple_of(kg_start, LANES), 2 * LANES)

    def tap_grads():
        @pl.loop(0, chunks)
        def _(chunk):
            columns = pl.ds(pl.multiple_of(chunk * LANES, LANES), LANES)
            padded = pm[:, columns].astype(F32)
            grad = pg[PAD : PAD + frames, columns].astype(F32)
            total = padded.shape[0]
            for r in range(8):
                moved = padded if r == 0 else pltpu.roll(padded, total - r, 0)
                for base in range(0, 2 * PAD, 8):
                    tap = base + r - 1
                    if 0 <= tap < taps:
                        kg_ref[tap : tap + 1, columns] = jnp.sum(
                            grad * moved[base : base + frames], axis=0, keepdims=True
                        )

        if relay:
            for by in range(1, n_mp):
                kg_copy(lax.rem(mp + by, n_mp), mp).start()

    @pl.when(seg == 0)
    def _():
        tap_grads()

    halo_wait(pg, 2)

    @pl.loop(0, chunks)
    def _(chunk):
        columns = pl.ds(pl.multiple_of(chunk * LANES, LANES), LANES)
        gs[:, columns] = tap_sum(pg[:, columns].astype(F32), columns, False) * mask_rows(0, frames)

    @pl.loop(0, blocks)
    def _(block):
        rows = pl.ds(pl.multiple_of(block * ROWS, ROWS), ROWS)
        masked = gs[rows, :]
        normed = norm[rows, :]
        first = jnp.mean(masked, axis=-1, keepdims=True)
        second = jnp.mean(masked * normed, axis=-1, keepdims=True)
        grad = inv[rows, :][:, :1] * (masked - first - normed * second)
        gin_ref[rows, :] = (up[rows, :].astype(F32) + grad).astype(BF)

        @pl.when(seg > 0)
        def _():
            up_copy(block).start()

    gin_copy.start()

    @pl.when(seg > 0)
    def _():
        tap_grads()

    if relay:
        total = kg_ref[:, kg_window]
        for by in range(1, n_mp):
            sender = lax.rem(mp + n_mp - by, n_mp)
            kg_copy(mp, sender).wait_recv()
            total = total + kg_land[sender]
        scale = (frames * n_mp) ** (-0.5)
        even, odd = total[:taps, :own], total[:taps, 2 * LANES - own :]
        kg_out[0] = jnp.where(column == 0, even, odd) * scale
        for by in range(1, n_mp):
            kg_copy(lax.rem(mp + by, n_mp), mp).wait_send()
        passed()
    else:
        kg_out[0] = kg_ref[:taps, :]

    out_copy.wait()
    gin_copy.wait()
    halo_sent(pm, 0)
    halo_sent(pg, 2)

    @pl.when(seg < n_seg - 1)
    def _():
        for tile in range(tiles):
            in_copy(tile).wait_send()

    @pl.when(seg > 0)
    def _():
        for block in range(blocks):
            up_copy(block).wait_send()


def on_device(frames_in, section_weights, conv_kernels, valid_length, out_cotangent):
    frames, width = frames_in.shape
    taps = conv_kernels.shape[1]
    n_mp = lax.axis_size("mp")
    own = width // n_mp
    if width == 1536 and n_mp == 8 and frames == 128:
        return spread_call(frames_in, section_weights, conv_kernels, valid_length, out_cotangent)
    relay = False
    weight = section_weights[0]
    if not relay:
        weight = lax.all_gather(weight, "mp", axis=0, tiled=True)
    vmem = pl.BlockSpec(memory_space=pltpu.VMEM)
    smem = pl.BlockSpec(memory_space=pltpu.SMEM)
    whole = pl.BlockSpec(memory_space=pl.ANY)
    padded = (frames + 2 * PAD, width)
    tap_rows = -(-taps // 8) * 8
    dma = pltpu.SemaphoreType.DMA
    out, gin, grad = pl.pallas_call(
        functools.partial(cascade, relay),
        out_shape=(
            jax.ShapeDtypeStruct((1, frames, width), BF),
            jax.ShapeDtypeStruct((1, frames, width), BF),
            jax.ShapeDtypeStruct((1, taps, own if relay else width), F32),
        ),
        in_specs=[whole, whole, whole, smem, whole],
        out_specs=(whole, whole, vmem),
        scratch_shapes=[
            pltpu.VMEM((frames, width), BF),
            pltpu.VMEM((frames, width), BF),
            pltpu.VMEM((frames, width), F32),
            pltpu.VMEM((frames, LANES), F32),
            pltpu.VMEM(padded, BF),
            pltpu.VMEM(padded, BF),
            pltpu.VMEM((frames, width), BF),
            pltpu.VMEM((frames, width), F32),
            pltpu.VMEM((frames, width), F32),
            pltpu.VMEM((frames, width), BF),
            pltpu.VMEM((frames, width), BF),
            pltpu.VMEM((width, width), BF),
            pltpu.VMEM((taps, width), BF),
            pltpu.VMEM((taps, width), F32),
            pltpu.VMEM((tap_rows, width), F32),
            pltpu.VMEM((n_mp if relay else 1, tap_rows, 2 * LANES), F32),
            dma((4,)), dma((4,)),
            dma((width // WIDE,)), dma((width // WIDE,)),
            dma((frames // ROWS,)), dma((frames // ROWS,)),
            dma((6,)),
            dma((3, n_mp)), dma((n_mp,)), dma((2,)), dma((2,)), dma((n_mp,)), dma((n_mp,)),
            pltpu.SemaphoreType.REGULAR,
        ],
        compiler_params=pltpu.CompilerParams(
            collective_id=0, has_side_effects=True, vmem_limit_bytes=60 * 2**20
        ),
    )(frames_in, weight, conv_kernels[0], valid_length, out_cotangent)
    if not relay:
        grad = lax.psum_scatter(grad, "mp", scatter_dimension=2, tiled=True)
        grad = grad * (frames * n_mp) ** (-0.5)
    return (out, gin, grad)


def solution(mesh):
    in_specs = (
        P("mp", None),
        P("segment", "mp", None),
        P("segment", None, None),
        P(),
        P("mp", None),
    )
    out_specs = (P("segment", "mp", None), P("segment", "mp", None), P("segment", None, "mp"))
    return jax.shard_map(
        on_device, mesh=mesh, in_specs=in_specs, out_specs=out_specs, check_vma=False
    )
```

```python
import functools

import jax
import jax.numpy as jnp
from jax import lax
from jax.experimental import pallas as pl
from jax.experimental.pallas import tpu as pltpu
from jax.sharding import PartitionSpec as P

EPSILON = 1e-05
PAD = 16
LANES = 128
ROWS = 16
WIDE = 256
MESH = pl.DeviceIdType.MESH
NORM_ROWS = 32
BF = jnp.bfloat16
F32 = jnp.float32

STAGES = ((0, 0, 0), (1, 0, 0), (1, 0, 1), (2, 0, 0), (2, 0, 1), (0, 1, 0), (1, 1, 0), (1, 1, 1), (2, 1, 0), (2, 1, 1), (0, 2, 0), (1, 2, 0), (1, 2, 1), (2, 2, 0), (2, 2, 1), (0, 3, 0), (1, 3, 0), (1, 3, 1), (3, 3, 0),)
INNER_0 = (
    (13, 76, 74, 8, 10, 73,),
    (47, 87, 271, 80, 81, 206, 111, 23, 335, 70, 16, 17,),
    (),
    (119, 215, 343, 100, 142, 201, 55, 95, 303, 6, 40, 89, 239, 151, 279, 134, 144, 209, 31, 127, 367, 199, 25, 194, 136, 247, 159, 359, 39, 232, 145, 354, 63, 223, 311,),
    (),
    (),
    (295, 137, 208, 290, 183, 375, 383, 263, 240, 153, 258,),
    (),
    (175, 319, 399, 327, 200, 217, 322, 191, 287, 463, 231, 255, 351, 167,),
    (),
    (486,),
    (391, 495, 386,),
    (),
    (511, 423,),
    (),
    (407, 418, 401,),
    (415, 455, 431, 450,),
    (),
    (439, 447, 471, 479, 503,),
)
INNER_1 = (
    (268, 333, 330, 265, 266, 328,),
    (79, 327, 367, 343, 73, 322, 336, 15, 263, 303, 279, 258, 296, 273,),
    (),
    (71, 111, 87, 351, 66, 81, 272, 7, 23, 311, 287, 2, 17, 360, 103, 119, 95, 359, 98, 352, 337, 39, 47, 55, 31, 34, 304, 345, 127, 167, 151, 375, 162, 145, 368, 63, 199, 143, 383,),
    (),
    (),
    (194, 137, 396, 231, 239, 183, 191, 226, 281, 460,),
    (),
    (135, 175, 215, 223, 130, 457, 247, 255, 319, 484, 393, 394, 207, 159, 295, 492,),
    (458,),
    (),
    (391, 431, 404, 401, 386,),
    (455, 471, 424, 465,),
    (450,),
    (),
    (439,),
    (423, 415, 464, 409, 503,),
    (479, 496, 473,),
    (447, 511,),
)
CORNER_0 = (68, 65, 4, 1, 66, 103, 327, 132, 129, 98, 39, 263, 32, 197, 2, 167, 295, 192, 130, 231, 391, 194, 455, 34, 423, 290, 258, 322, 226, 162, 386, 418, 450,)
CORNER_1 = (261, 324, 322, 256, 258, 321, 71, 295, 66, 288, 389, 7, 359, 2, 384, 453, 135, 423, 129, 354, 448, 39, 487, 34, 416, 199, 167, 193, 162, 194, 230, 130, 482, 290, 386, 450, 418,)
SENDS = 50
PIECES = 2
LATE = ((3,), (), (1,), (0, 2))


def decode(event):
    return event // 128, event // 64 % 2, event // 32 % 2, event // 8 % 4, event // 4 % 2, event % 4


def spread(
    x_any, w_any, k_any, vl_ref, cot_any,
    out_whole, gin_whole, kg_out,
    w, a, up, norm, inv, pm, pg, act, slope, gs, k_bf, k_ref, kg, kg_sib, kg_sum, kg_land,
    local_sem, x_send, x_recv, k_send, k_recv, own_send, rel_send, rel_recv, sib_send, sib_recv,
    halo_send, halo_recv, out_send, out_recv, gin_send, gin_recv, pair_send, pair_recv, kg_send, kg_recv,
):
    n_sec, rows_in, width = w.shape
    part = a.shape[1]
    taps = k_ref.shape[1]
    seg, mp = lax.axis_index("segment"), lax.axis_index("mp")
    n_seg, n_mp = lax.axis_size("segment"), lax.axis_size("mp")
    own = rows_in // n_mp
    half = own // (2 * PIECES)
    chunks = width // LANES
    tiles = width // WIDE
    x, c = lax.div(seg, 2), lax.rem(seg, 2)
    z, y = lax.div(mp, 2), lax.rem(mp, 2)
    inner = (z == 1) | (z == 2)
    block = jnp.where(c == 1, mp, jnp.where(z == 1, y, 6 + y))
    which = x + y - 2 * x * y
    chunk_id = 2 * block + which
    chip = 4 * x + mp - 2

    def device_of(number, half_of):
        side, core = number % 2, ((number >= 2) & (number < 6)) * 1
        return 2 * (half_of + side - 2 * half_of * side) + core, (number >= 4) * 2 + 2 + side

    barrier = pltpu.get_barrier_semaphore()
    me = seg * n_mp + mp
    total = n_seg * n_mp

    @pl.loop(1, total)
    def _(by):
        other = lax.rem(me + by, total)
        pl.semaphore_signal(
            barrier, inc=1, device_id=(lax.div(other, n_mp), lax.rem(other, n_mp)), device_id_type=MESH
        )

    w_copy = pltpu.make_async_copy(
        w_any, w.at[seg, pl.ds(pl.multiple_of(own * mp, own), own)], local_sem.at[0]
    )
    k_copy = pltpu.make_async_copy(k_any, k_bf.at[seg], local_sem.at[1])
    w_copy.start()

    @pl.when(inner)
    def _():
        k_copy.start()

    pl.semaphore_wait(barrier, total - 1)

    def half_ref(section, shard, piece, core):
        start = own * shard + half * (2 * piece + core)
        return w.at[section, pl.ds(pl.multiple_of(start, half), half)]

    def own_copy(kind, piece):
        core = c if kind else 1 - c
        return pltpu.make_async_remote_copy(
            src_ref=half_ref(seg, mp, piece, core), dst_ref=half_ref(seg, mp, piece, core),
            send_sem=own_send.at[2 * piece + kind],
            recv_sem=(sib_recv if kind else rel_recv).at[(seg * n_mp + mp) * PIECES + piece],
            device_id={"segment": seg + 1 - 2 * c}, device_id_type=MESH,
        )

    def relay_copy(section, shard, piece, way, slot):
        target = (
            {"segment": seg + 2 - 4 * x}, {"mp": mp + 1 - 2 * y}, {"mp": mp + jnp.where(z < 2, 2, -2)}
        )[way]
        return pltpu.make_async_remote_copy(
            src_ref=half_ref(section, shard, piece, c), dst_ref=half_ref(section, shard, piece, c),
            send_sem=rel_send.at[slot], recv_sem=rel_recv.at[(section * n_mp + shard) * PIECES + piece],
            device_id=target, device_id_type=MESH,
        )

    def sib_copy(section, shard, piece, core):
        sem = (section * n_mp + shard) * PIECES + piece
        return pltpu.make_async_remote_copy(
            src_ref=half_ref(section, shard, piece, core), dst_ref=half_ref(section, shard, piece, core),
            send_sem=sib_send.at[sem], recv_sem=sib_recv.at[sem],
            device_id={"segment": seg + 1 - 2 * c}, device_id_type=MESH,
        )

    def shard_of(across, depth):
        from_y = 1 - y if across else y
        return 2 * jnp.where(z < 2, depth, 3 - depth) + from_y

    def is_home(section, across, depth, plane, corner):
        return section // 2 == plane and across == 0 and depth == (0 if corner else 1)

    def run_events(events, plane, corner, slot):
        for event in events:
            section, piece, across, depth, first, way = decode(event)
            shard = shard_of(across, depth)
            if first and is_home(section, across, depth, plane, corner):
                pl.when(c != section % 2)(relay_copy(section, shard, piece, 0, 0).wait_recv)
            elif first:
                relay_copy(section, shard, piece, 0, 0).wait_recv()
                if not corner:
                    sib_copy(section, shard, piece, c).start()
            if way < 3:
                relay_copy(section, shard, piece, way, slot).start()
                slot += 1
        return slot

    def finish_events(groups, plane, corner):
        slot = 0
        for events in groups:
            for event in events:
                section, piece, across, depth, first, way = decode(event)
                shard = shard_of(across, depth)
                if first and not corner and not is_home(section, across, depth, plane, corner):
                    sib_copy(section, shard, piece, c).wait_send()
                if way < 3:
                    relay_copy(section, shard, piece, way, slot).wait_send()
                    slot += 1

    def siblings(section, plane):
        for across in range(2):
            for depth in range(4):
                for piece in range(PIECES):
                    wait = sib_copy(section, shard_of(across, depth), piece, 1 - c).wait_recv
                    if is_home(section, across, depth, plane, False):
                        pl.when(c != section % 2)(wait)
                    else:
                        wait()

    to_seg, to_mp = device_of(mp, which)
    sends_x = seg == to_seg
    away = sends_x & (to_mp != mp)

    def x_move(index, remote):
        rows = pl.ds(pl.multiple_of(part * which, part), part)
        source, target = ((x_any, a.at[0]), (cot_any, up.at[n_sec]))[index]
        if not remote:
            return pltpu.make_async_copy(source.at[rows], target, x_recv.at[index])
        return pltpu.make_async_remote_copy(
            src_ref=source.at[rows], dst_ref=target, send_sem=x_send.at[index], recv_sem=x_recv.at[index],
            device_id={"mp": to_mp}, device_id_type=MESH,
        )

    def x_start(index):
        pl.when(inner & (c == 1))(lambda: x_move(index, False).start())
        pl.when(away)(lambda: x_move(index, True).start())

    def x_wait(index):
        pl.when(c == 1)(lambda: x_move(index, False).wait())
        pl.when(c == 0)(lambda: x_move(index, True).wait_recv())

    def k_move(by, sender):
        return pltpu.make_async_remote_copy(
            src_ref=k_any, dst_ref=k_bf.at[sender], send_sem=k_send.at[by - 1], recv_sem=k_recv.at[sender],
            device_id={"segment": lax.rem(seg + by, n_seg)}, device_id_type=MESH,
        )

    w_copy.wait()
    for piece in range(PIECES):
        own_copy(0, piece).start()
        pl.when(inner)(own_copy(1, piece).start)

    @pl.when(inner)
    def _():
        for by in range(1, n_sec):
            k_move(by, seg).start()

    x_start(0)

    corner = jnp.logical_not(inner)
    for plane, table in ((0, CORNER_0), (1, CORNER_1)):

        @pl.when(corner & (x == plane))
        def _():
            run_events(table, plane, True, 0)

    x_start(1)

    def mask_rows(start, count):
        position = chunk_id * part + start + lax.broadcasted_iota(jnp.int32, (count, LANES), 0)
        return (position < vl_ref[0]).astype(F32)

    def halo_copy(pad_ref, section, slot, to_next):
        rows_from = pl.ds(part, PAD) if to_next else pl.ds(PAD, PAD)
        rows_to = pl.ds(0, PAD) if to_next else pl.ds(part + PAD, PAD)
        near = chunk_id + (1 if to_next else -1)
        target = device_of(lax.div(near, 2), lax.rem(near, 2))
        sem = 6 * section + 2 * slot + (0 if to_next else 1)
        columns = pl.ds(0, width) if slot == 0 else pl.ds((slot - 1) * side, side)
        return pltpu.make_async_remote_copy(
            src_ref=pad_ref.at[section, rows_from, columns], dst_ref=pad_ref.at[section, rows_to, columns],
            send_sem=halo_send.at[sem], recv_sem=halo_recv.at[sem],
            device_id=target, device_id_type=MESH,
        )

    last = 2 * n_mp - 1
    side = width // 2

    def halo_start(pad_ref, section, slot):
        pl.when(chunk_id < last)(lambda: halo_copy(pad_ref, section, slot, True).start())
        pl.when(chunk_id > 0)(lambda: halo_copy(pad_ref, section, slot, False).start())

    def halo_wait(pad_ref, section, slot):
        pl.when(chunk_id > 0)(lambda: halo_copy(pad_ref, section, slot, True).wait_recv())
        pl.when(chunk_id < last)(lambda: halo_copy(pad_ref, section, slot, False).wait_recv())

    def halo_sent(pad_ref, section, slot):
        pl.when(chunk_id < last)(lambda: halo_copy(pad_ref, section, slot, True).wait_send())
        pl.when(chunk_id > 0)(lambda: halo_copy(pad_ref, section, slot, False).wait_send())

    def tap_sum(padded, section, columns, forward):
        rows = padded.shape[0]
        running = jnp.zeros((part, LANES), F32)
        for r in range(8):
            moved = padded if r == 0 else pltpu.roll(padded, rows - r, 0)
            for base in range(0, 2 * PAD, 8):
                offset = base + r
                if 1 <= offset <= taps:
                    tap = offset - 1 if forward else taps - offset
                    running = running + k_ref[section, tap : tap + 1, columns] * moved[base : base + part]
        return running

    def normalize(section):
        for start in range(0, part, NORM_ROWS):
            rows = slice(start, start + NORM_ROWS)
            values = a[section, rows].astype(F32)
            center = values - jnp.mean(values, axis=-1, keepdims=True)
            inverse = lax.rsqrt(jnp.mean(center * center, axis=-1, keepdims=True) + EPSILON)
            normed = center * inverse
            norm[section, rows] = normed
            inv[section, rows] = jnp.broadcast_to(inverse, (NORM_ROWS, LANES))
            pm[section, PAD + start : PAD + start + NORM_ROWS] = (
                normed * mask_rows(start, NORM_ROWS)[:, :1]
            ).astype(BF)
        halo_start(pm, section, 0)

    def convolve(section, step):
        if step == 0:
            halo_wait(pm, section, 0)

        @pl.loop(step * chunks // 2, (step + 1) * chunks // 2)
        def _(chunk):
            columns = pl.ds(pl.multiple_of(chunk * LANES, LANES), LANES)
            conv = tap_sum(pm[section, :, columns].astype(F32), section, columns, True)
            gate = jax.nn.sigmoid(conv)
            act[section, :, columns] = (conv * gate).astype(BF)
            slope[section, :, columns] = gate * (1.0 + conv * (1.0 - gate))

    def result_copy(source, index, section, whole, send, recv, remote):
        rows = pl.ds(pl.multiple_of(part * which, part), part)
        if not remote:
            return pltpu.make_async_copy(source.at[index], whole.at[0, rows], recv.at[which])
        return pltpu.make_async_remote_copy(
            src_ref=source.at[index], dst_ref=whole.at[0, rows],
            send_sem=send.at[section], recv_sem=recv.at[which],
            device_id=(section, block), device_id_type=MESH,
        )

    def result_start(section, *what):
        same = (seg == section) & (mp == block)
        pl.when(same)(lambda: result_copy(*what, False).start())
        pl.when(jnp.logical_not(same))(lambda: result_copy(*what, True).start())

    def result_sent(section, *what):
        same = (seg == section) & (mp == block)
        pl.when(jnp.logical_not(same))(lambda: result_copy(*what, True).wait_send())

    def result_wait(source, whole, send, recv):
        for half_of in range(2):
            from_seg, from_mp = device_of(mp, half_of)
            same = (seg == from_seg) & (mp == from_mp)
            rows = pl.ds(part * half_of, part)

            @pl.when(same)
            def _():
                pltpu.make_async_copy(source.at[0], whole.at[0, rows], recv.at[half_of]).wait()

            @pl.when(jnp.logical_not(same))
            def _():
                pltpu.make_async_remote_copy(
                    src_ref=source.at[0], dst_ref=whole.at[0, rows],
                    send_sem=send.at[0], recv_sem=recv.at[half_of],
                    device_id=(seg, mp), device_id_type=MESH,
                ).wait_recv()

    def product(section, step):
        for tile in range(step * tiles // 2, (step + 1) * tiles // 2):
            columns = slice(tile * WIDE, (tile + 1) * WIDE)
            result = jnp.dot(act[section], w[section, :, columns], preferred_element_type=F32)
            a[section + 1, :, columns] = (a[section, :, columns].astype(F32) + result).astype(BF)

    def out_what(section):
        return section, a, section + 1, section, out_whole, out_send, out_recv

    def gin_what(section):
        return section, up, section, section, gin_whole, gin_send, gin_recv

    def out_start(section, late):
        at_once = (c == 0) | (x == section // 2)
        pl.when(jnp.logical_not(at_once) if late else at_once)(lambda: result_start(*out_what(section)))

    def gin_start(section, late):
        pl.when(c == (1 if late else 0))(lambda: result_start(*gin_what(section)))

    def forward_stage(kind, section, step):
        if kind == 0:
            if section == 0:
                x_wait(0)
                k_copy.wait()
                for by in range(1, n_sec):
                    k_move(by, lax.rem(seg + n_seg - by, n_seg)).wait_recv()
                for s in range(n_sec):
                    k_ref[s] = k_bf[s].astype(F32)
                for pad_ref in (pm, pg):

                    @pl.when(chunk_id == 0)
                    def _():
                        for s in range(n_sec):
                            pad_ref[s, 0:PAD, :] = jnp.zeros((PAD, width), BF)

                    @pl.when(chunk_id == last)
                    def _():
                        for s in range(n_sec):
                            pad_ref[s, part + PAD : part + 2 * PAD, :] = jnp.zeros((PAD, width), BF)

                kg[:, taps:, :] = jnp.zeros((n_sec, kg.shape[1] - taps, width), F32)
            normalize(section)
        elif kind == 1:
            convolve(section, step)
        elif kind == 3:
            for plane in range(2):
                pl.when(x == plane)(lambda: siblings(section, plane))
            last_back_product()
        else:
            if step == 0:
                for plane in range(2):
                    pl.when(x == plane)(lambda: siblings(section, plane))
            product(section, step)
            if step == 1:
                out_start(section, False)

    def kg_window(index, core):
        return pl.ds(pl.multiple_of(384 * index + 128 * core, LANES), 2 * LANES)

    def kg_pair(section):
        return pltpu.make_async_remote_copy(
            src_ref=kg.at[section], dst_ref=kg_sib.at[section],
            send_sem=pair_send.at[section], recv_sem=pair_recv.at[section],
            device_id={"segment": seg + 1 - 2 * c}, device_id_type=MESH,
        )

    def kg_copy(section, index, remote):
        if not remote:
            return pltpu.make_async_copy(kg_sum.at[section, index], kg_land.at[chip], kg_recv.at[chip])
        return pltpu.make_async_remote_copy(
            src_ref=kg_sum.at[section, index], dst_ref=kg_land.at[chip],
            send_sem=kg_send.at[4 * section + index], recv_sem=kg_recv.at[chip],
            device_id=(section, 2 * index + c), device_id_type=MESH,
        )

    def kg_start(section):
        kg_pair(section).wait_recv()
        for index in range(n_mp // 2):
            window = kg_window(index, c)
            kg_sum[section, index] = (kg[section, :, window] + kg_sib[section, :, window]).astype(BF)
            same = (seg == section) & (mp == 2 * index + c)
            pl.when(same)(lambda: kg_copy(section, index, False).start())
            pl.when(jnp.logical_not(same))(lambda: kg_copy(section, index, True).start())

    def tap_grads(section):
        @pl.loop(0, chunks)
        def _(chunk):
            columns = pl.ds(pl.multiple_of(chunk * LANES, LANES), LANES)
            padded = pm[section, :, columns].astype(F32)
            grad = pg[section, PAD : PAD + part, columns].astype(F32)
            rows = padded.shape[0]
            for r in range(8):
                moved = padded if r == 0 else pltpu.roll(padded, rows - r, 0)
                for base in range(0, 2 * PAD, 8):
                    tap = base + r - 1
                    if 0 <= tap < taps:
                        kg[section, tap : tap + 1, columns] = jnp.sum(
                            grad * moved[base : base + part], axis=0, keepdims=True
                        )

        kg_pair(section).start()

    def back_tile(section, tile):
        columns = slice(tile * WIDE, (tile + 1) * WIDE)
        return columns, lax.dot_general(
            up[section + 1], w[section, columns, :], (((1,), (1,)), ((), ())), preferred_element_type=F32
        )

    def last_back_product():
        x_wait(1)
        for tile in range(tiles):
            columns, grad = back_tile(n_sec - 1, tile)
            gs[:, columns] = grad

    def backward(section):
        for part_of in range(2):
            for tile in range(part_of * tiles // 2, (part_of + 1) * tiles // 2):
                if section == n_sec - 1:
                    columns = slice(tile * WIDE, (tile + 1) * WIDE)
                    grad = gs[:, columns]
                else:
                    columns, grad = back_tile(section, tile)
                pg[section, PAD : PAD + part, columns] = (grad * slope[section, :, columns]).astype(BF)
            halo_start(pg, section, 1 + part_of)
        tap_grads(section)
        if section == n_sec - 1:
            product(section, 0)
            product(section, 1)
            out_start(section, False)
        else:
            kg_start(section + 1)
        for part_of in range(2):
            halo_wait(pg, section, 1 + part_of)
            if part_of == 0 and section == 0:
                kg_start(section)
            if part_of == 1:
                if section < n_sec - 1:
                    gin_start(section + 1, True)
                for other in LATE[section]:
                    out_start(other, True)

            @pl.loop(part_of * chunks // 2, (part_of + 1) * chunks // 2)
            def _(chunk):
                columns = pl.ds(pl.multiple_of(chunk * LANES, LANES), LANES)
                gs[:, columns] = tap_sum(
                    pg[section, :, columns].astype(F32), section, columns, False
                ) * mask_rows(0, part)

        for start in range(0, part, NORM_ROWS):
            rows = slice(start, start + NORM_ROWS)
            masked = gs[rows]
            normed = norm[section, rows]
            first = jnp.mean(masked, axis=-1, keepdims=True)
            second = jnp.mean(masked * normed, axis=-1, keepdims=True)
            grad = inv[section, rows][:, :1] * (masked - first - normed * second)
            up[section, rows] = (up[section + 1, rows].astype(F32) + grad).astype(BF)
        gin_start(section, False)
        if section == 0:
            gin_start(section, True)

    slots = [0, 0]
    for index, (kind, section, step) in enumerate(STAGES):
        for plane, table in ((0, INNER_0), (1, INNER_1)):
            if table[index]:
                start = slots[plane]

                @pl.when(inner & (x == plane))
                def _():
                    run_events(table[index], plane, False, start)

                slots[plane] += sum(event % 4 < 3 for event in table[index])
        pl.when(inner)(lambda: forward_stage(kind, section, step))
    @pl.when(inner)
    def _():
        for section in reversed(range(n_sec)):
            backward(section)

    sums = jnp.zeros((kg.shape[1], 2 * LANES), F32)
    for number in range(n_mp):
        from_seg, from_mp = 2 * (number // 4) + y, number % 4 + 2
        same = (seg == from_seg) & (mp == from_mp)

        @pl.when(same)
        def _():
            pltpu.make_async_copy(kg_sum.at[0, 0], kg_land.at[number], kg_recv.at[number]).wait()

        @pl.when(jnp.logical_not(same))
        def _():
            pltpu.make_async_remote_copy(
                src_ref=kg_sum.at[0, 0], dst_ref=kg_land.at[number],
                send_sem=kg_send.at[0], recv_sem=kg_recv.at[number],
                device_id=(seg, mp), device_id_type=MESH,
            ).wait_recv()

        sums = sums + kg_land[number].astype(F32)
    scale = (2 * part * n_mp) ** (-0.5)
    even, odd = sums[:taps, :own], sums[:taps, 2 * LANES - own :]
    kg_out[:, 0, :] = jnp.where(y == 0, even, odd) * scale

    result_wait(a, out_whole, out_send, out_recv)
    result_wait(up, gin_whole, gin_send, gin_recv)

    for piece in range(PIECES):
        own_copy(0, piece).wait_send()
    for index in range(2):
        pl.when(away)(lambda: x_move(index, True).wait_send())
    for plane, table in ((0, CORNER_0), (1, CORNER_1)):
        pl.when(corner & (x == plane))(lambda: finish_events((table,), plane, True))
    for plane, table in ((0, INNER_0), (1, INNER_1)):
        pl.when(inner & (x == plane))(lambda: finish_events(table, plane, False))

    @pl.when(inner)
    def _():
        for piece in range(PIECES):
            own_copy(1, piece).wait_send()
        for by in range(1, n_sec):
            k_move(by, seg).wait_send()
        for section in range(n_sec):
            halo_sent(pm, section, 0)
            halo_sent(pg, section, 1)
            halo_sent(pg, section, 2)
            result_sent(*out_what(section))
            result_sent(*gin_what(section))
            kg_pair(section).wait_send()
            for index in range(n_mp // 2):
                same = (seg == section) & (mp == 2 * index + c)
                pl.when(jnp.logical_not(same))(lambda: kg_copy(section, index, True).wait_send())


def spread_call(frames_in, section_weights, conv_kernels, valid_length, out_cotangent):
    frames, width = frames_in.shape
    taps = conv_kernels.shape[1]
    n_sec, n_mp = lax.axis_size("segment"), lax.axis_size("mp")
    own = width // n_mp
    part = frames // 2
    vmem = pl.BlockSpec(memory_space=pltpu.VMEM)
    smem = pl.BlockSpec(memory_space=pltpu.SMEM)
    whole = pl.BlockSpec(memory_space=pl.ANY)
    tap_rows = -(-taps // 8) * 8
    dma = pltpu.SemaphoreType.DMA
    out, gin, grad = pl.pallas_call(
        spread,
        out_shape=(
            jax.ShapeDtypeStruct((1, frames, width), BF),
            jax.ShapeDtypeStruct((1, frames, width), BF),
            jax.ShapeDtypeStruct((taps, 1, own), F32),
        ),
        in_specs=[whole, whole, whole, smem, whole],
        out_specs=(whole, whole, vmem),
        scratch_shapes=[
            pltpu.VMEM((n_sec, width, width), BF),
            pltpu.VMEM((n_sec + 1, part, width), BF),
            pltpu.VMEM((n_sec + 1, part, width), BF),
            pltpu.VMEM((n_sec, part, width), F32),
            pltpu.VMEM((n_sec, part, LANES), F32),
            pltpu.VMEM((n_sec, part + 2 * PAD, width), BF),
            pltpu.VMEM((n_sec, part + 2 * PAD, width), BF),
            pltpu.VMEM((n_sec, part, width), BF),
            pltpu.VMEM((n_sec, part, width), F32),
            pltpu.VMEM((part, width), F32),
            pltpu.VMEM((n_sec, taps, width), BF),
            pltpu.VMEM((n_sec, taps, width), F32),
            pltpu.VMEM((n_sec, tap_rows, width), F32),
            pltpu.VMEM((n_sec, tap_rows, width), F32),
            pltpu.VMEM((n_sec, n_mp // 2, tap_rows, 2 * LANES), BF),
            pltpu.VMEM((n_mp, tap_rows, 2 * LANES), BF),
            dma((2,)), dma((2,)), dma((2,)), dma((n_sec - 1,)), dma((n_sec,)),
            dma((2 * PIECES,)), dma((SENDS,)),
            dma((PIECES * n_sec * n_mp,)), dma((PIECES * n_sec * n_mp,)), dma((PIECES * n_sec * n_mp,)),
            dma((6 * n_sec,)), dma((6 * n_sec,)),
            dma((n_sec,)), dma((2,)), dma((n_sec,)), dma((2,)),
            dma((n_sec,)), dma((n_sec,)), dma((4 * n_sec,)), dma((n_mp,)),
        ],
        compiler_params=pltpu.CompilerParams(
            collective_id=1, has_side_effects=True, vmem_limit_bytes=60 * 2**20
        ),
    )(frames_in, section_weights[0], conv_kernels[0], valid_length, out_cotangent)
    return out, gin, grad.transpose(1, 0, 2)


def cascade(
    relay, x_any, w_any, k_any, vl_ref, cot_any,
    out_whole, gin_whole, kg_out,
    cur, up, norm, inv, pm, pg, act, slope, gs, out_ref, gin_ref, w_ref, k_bf, k_ref, kg_ref, kg_land,
    halo_send, halo_recv, in_send, in_recv, up_send, up_recv,
    local_sem, w_send, w_recv, end_send, end_recv, kg_send, kg_recv, turn_sem,
):
    frames, width = x_any.shape
    taps = k_ref.shape[0]
    seg, mp = lax.axis_index("segment"), lax.axis_index("mp")
    n_seg, n_mp = lax.axis_size("segment"), lax.axis_size("mp")
    chunks = width // LANES
    blocks = frames // ROWS
    tiles = width // WIDE

    barrier = pltpu.get_barrier_semaphore()
    steps_mp = range(1, n_mp) if relay else (1, n_mp - 1)
    for axis, index, count, steps in (
        ("segment", seg, n_seg, (1, n_seg - 1)), ("mp", mp, n_mp, steps_mp)
    ):
        for by in steps:
            pl.semaphore_signal(
                barrier, inc=1, device_id={axis: lax.rem(index + by, count)}, device_id_type=MESH
            )
    own = width // n_mp
    w_rows = pl.ds(pl.multiple_of(mp * own, own), own) if relay else pl.ds(0, width)
    w_copy = pltpu.make_async_copy(w_any, w_ref.at[w_rows], local_sem.at[0])
    x_copy = pltpu.make_async_copy(x_any, cur, local_sem.at[1])
    cot_copy = pltpu.make_async_copy(cot_any, up, local_sem.at[2])
    k_copy = pltpu.make_async_copy(k_any, k_bf, local_sem.at[3])
    out_copy = pltpu.make_async_copy(out_ref, out_whole.at[0], local_sem.at[4])
    gin_copy = pltpu.make_async_copy(gin_ref, gin_whole.at[0], local_sem.at[5])
    w_copy.start()
    k_copy.start()

    @pl.when(seg == 0)
    def _():
        x_copy.start()

    @pl.when(seg == n_seg - 1)
    def _():
        cot_copy.start()

    pl.semaphore_wait(barrier, 2 + len(steps_mp))

    row, column = lax.div(mp, 2), lax.rem(mp, 2)
    n_row = n_mp // 2

    half = own // 2

    def block_copy(block, way, count=own):
        rows = pl.ds(pl.multiple_of(block * own, own), count)
        target = (mp + 2, mp - 2, mp + 1 - 2 * column)[way]
        return pltpu.make_async_remote_copy(
            src_ref=w_ref.at[rows], dst_ref=w_ref.at[rows],
            send_sem=w_send.at[way, block], recv_sem=w_recv.at[block],
            device_id={"mp": target}, device_id_type=MESH,
        )

    def end_copy(way):
        block = (0 if way == 0 else n_mp - 2) + 1 - column
        rows = pl.ds(pl.multiple_of(block * own + half, half), half)
        return pltpu.make_async_remote_copy(
            src_ref=w_ref.at[rows], dst_ref=w_ref.at[rows],
            send_sem=end_send.at[way], recv_sem=end_recv.at[way],
            device_id={"mp": mp + 2 if way == 0 else mp - 2}, device_id_type=MESH,
        )

    def each_block(distance, act_on, arrive):
        if distance == 0:
            pl.when(row < n_row - 1)(lambda: act_on(mp, 0))
            pl.when(row > 0)(lambda: act_on(mp, 1))
            act_on(mp, 2)
            return
        low, high = mp - 2 * distance, mp + 2 * distance

        @pl.when(row >= distance)
        def _():
            arrive(low)
            pl.when(row < n_row - 1)(lambda: act_on(low, 0))
            pl.when(row == distance)(lambda: act_on(low, 2, half))
            pl.when(row > distance)(lambda: act_on(low, 2))

        @pl.when(row + distance < n_row)
        def _():
            arrive(high)
            pl.when(row > 0)(lambda: act_on(high, 1))
            pl.when(row + distance == n_row - 1)(lambda: act_on(high, 2, half))
            pl.when(row + distance < n_row - 1)(lambda: act_on(high, 2))

    def pass_on(distance):
        each_block(
            distance,
            lambda *what: block_copy(*what).start(),
            lambda block: block_copy(block, 0).wait_recv(),
        )
        if distance == 1:
            for way, end in ((0, 0), (1, n_row - 1)):

                @pl.when(row == end)
                def _():
                    block_copy(2 * end + 1 - column, 2).wait_recv()
                    end_copy(way).start()

    def passed():
        for distance in range(n_row):
            each_block(
                distance,
                lambda *what: block_copy(*what).wait_send(),
                lambda block: None,
            )
        pl.when(row < n_row - 1)(lambda: end_copy(0).wait_send())
        pl.when(row > 0)(lambda: end_copy(1).wait_send())

    def gather_rest(first):
        if relay:
            for distance in range(first, n_row):
                pass_on(distance)

            @pl.when(row > 0)
            def _():
                end_copy(0).wait_recv()
                pl.when(row < n_row - 1)(lambda: end_copy(0).start())

            @pl.when(row < n_row - 1)
            def _():
                end_copy(1).wait_recv()
                pl.when(row > 0)(lambda: end_copy(1).start())

            for index in range(n_row):
                block = index * 2 + 1 - column
                if index in (0, n_row - 1):
                    pl.when(row != index)(lambda: block_copy(block, 2, half).wait_recv())
                else:
                    block_copy(block, 2).wait_recv()

    def kg_copy(target, sender):
        start = 384 * lax.div(target, 2) + 128 * lax.rem(target, 2)
        window = pl.ds(pl.multiple_of(start, LANES), 2 * LANES)
        return pltpu.make_async_remote_copy(
            src_ref=kg_ref.at[:, window], dst_ref=kg_land.at[sender],
            send_sem=kg_send.at[target], recv_sem=kg_recv.at[sender],
            device_id={"mp": target}, device_id_type=MESH,
        )

    w_copy.wait()
    if relay:

        @pl.when(seg != 1)
        def _():
            pass_on(0)

    k_copy.wait()
    k_ref[...] = k_bf[...].astype(F32)
    kg_ref[...] = jnp.zeros(kg_ref.shape, F32)

    def halo_copy(pad_ref, first, to_right):
        rows_from = pl.ds(frames, PAD) if to_right else pl.ds(PAD, PAD)
        rows_to = pl.ds(0, PAD) if to_right else pl.ds(frames + PAD, PAD)
        target = lax.rem(mp + (1 if to_right else n_mp - 1), n_mp)
        slot = first + (0 if to_right else 1)
        return pltpu.make_async_remote_copy(
            src_ref=pad_ref.at[rows_from], dst_ref=pad_ref.at[rows_to],
            send_sem=halo_send.at[slot], recv_sem=halo_recv.at[slot],
            device_id={"mp": target}, device_id_type=MESH,
        )

    def halo_start(pad_ref, first):
        @pl.when(mp < n_mp - 1)
        def _():
            halo_copy(pad_ref, first, True).start()

        @pl.when(mp > 0)
        def _():
            halo_copy(pad_ref, first, False).start()

    def halo_wait(pad_ref, first):
        @pl.when(mp > 0)
        def _():
            halo_copy(pad_ref, first, True).wait_recv()

        @pl.when(mp < n_mp - 1)
        def _():
            halo_copy(pad_ref, first, False).wait_recv()

    def halo_sent(pad_ref, first):
        @pl.when(mp < n_mp - 1)
        def _():
            halo_copy(pad_ref, first, True).wait_send()

        @pl.when(mp > 0)
        def _():
            halo_copy(pad_ref, first, False).wait_send()

    def halo_clear(pad_ref):
        @pl.when(mp == 0)
        def _():
            pad_ref[0:PAD, :] = jnp.zeros((PAD, width), BF)

        @pl.when(mp == n_mp - 1)
        def _():
            pad_ref[frames + PAD : frames + 2 * PAD, :] = jnp.zeros((PAD, width), BF)

    def in_copy(tile):
        columns = pl.ds(tile * WIDE, WIDE)
        return pltpu.make_async_remote_copy(
            src_ref=out_ref.at[:, columns], dst_ref=cur.at[:, columns],
            send_sem=in_send.at[tile], recv_sem=in_recv.at[tile],
            device_id={"segment": lax.rem(seg + 1, n_seg)}, device_id_type=MESH,
        )

    def up_copy(block):
        rows = pl.ds(block * ROWS, ROWS)
        return pltpu.make_async_remote_copy(
            src_ref=gin_ref.at[rows], dst_ref=up.at[rows],
            send_sem=up_send.at[block], recv_sem=up_recv.at[block],
            device_id={"segment": lax.rem(seg + n_seg - 1, n_seg)}, device_id_type=MESH,
        )

    def mask_rows(start, count):
        position = mp * frames + start + lax.broadcasted_iota(jnp.int32, (count, LANES), 0)
        return (position < vl_ref[0]).astype(F32)

    def back_product():
        for tile in range(tiles):
            columns = slice(tile * WIDE, (tile + 1) * WIDE)
            gs[:, columns] = lax.dot_general(
                up[...], w_ref[columns, :], (((1,), (1,)), ((), ())), preferred_element_type=F32
            )

    halo_clear(pm)
    halo_clear(pg)

    @pl.when(seg == n_seg - 1)
    def _():
        gather_rest(1)
        cot_copy.wait()
        back_product()

    @pl.when(seg == 0)
    def _():
        x_copy.wait()

    @pl.when(seg == 1)
    def _():
        if relay:
            pl.semaphore_wait(turn_sem, 1)
            pass_on(0)

    @pl.when((seg > 1) & (seg < n_seg - 1))
    def _():
        gather_rest(1)

    @pl.when(seg > 0)
    def _():
        for tile in range(tiles):
            in_copy(tile).wait_recv()

    def norm_rows(block):
        start = pl.multiple_of(block * ROWS, ROWS)
        rows = pl.ds(start, ROWS)
        values = cur[rows, :].astype(F32)
        center = values - jnp.mean(values, axis=-1, keepdims=True)
        inverse = lax.rsqrt(jnp.mean(center * center, axis=-1, keepdims=True) + EPSILON)
        normed = center * inverse
        norm[rows, :] = normed
        inv[rows, :] = jnp.broadcast_to(inverse, (ROWS, LANES))
        pm[pl.ds(pl.multiple_of(PAD + start, ROWS), ROWS), :] = (
            normed * mask_rows(start, ROWS)[:, :1]
        ).astype(BF)

    norm_rows(0)
    norm_rows(blocks - 1)
    halo_start(pm, 0)

    @pl.loop(1, blocks - 1)
    def _(block):
        norm_rows(block)

    if relay:

        @pl.when(seg < 2)
        def _():
            pass_on(1)

    halo_wait(pm, 0)

    def shifted(padded):
        total = padded.shape[0]
        return [padded if r == 0 else pltpu.roll(padded, total - r, 0) for r in range(8)]

    def tap_sum(padded, columns, forward):
        total = padded.shape[0]
        running = jnp.zeros((frames, LANES), F32)
        for r in range(8):
            moved = padded if r == 0 else pltpu.roll(padded, total - r, 0)
            for base in range(0, 2 * PAD, 8):
                offset = base + r
                if 1 <= offset <= taps:
                    tap = offset - 1 if forward else taps - offset
                    running = running + k_ref[tap : tap + 1, columns] * moved[base : base + frames]
        return running

    @pl.loop(0, chunks)
    def _(chunk):
        columns = pl.ds(pl.multiple_of(chunk * LANES, LANES), LANES)
        conv = tap_sum(pm[:, columns].astype(F32), columns, True)
        gate = jax.nn.sigmoid(conv)
        act[:, columns] = (conv * gate).astype(BF)
        slope[:, columns] = gate * (1.0 + conv * (1.0 - gate))

    if relay:

        @pl.when(seg < 2)
        def _():
            pass_on(2)

        @pl.when(seg == 0)
        def _():
            pl.semaphore_signal(
                turn_sem, inc=1, device_id={"segment": seg + 1}, device_id_type=MESH
            )

        @pl.when(seg < 2)
        def _():
            gather_rest(3)

    for tile in range(tiles):
        columns = slice(tile * WIDE, (tile + 1) * WIDE)
        product = jnp.dot(act[...], w_ref[:, columns], preferred_element_type=F32)
        out_ref[:, columns] = (cur[:, columns].astype(F32) + product).astype(BF)

        @pl.when(seg < n_seg - 1)
        def _():
            in_copy(tile).start()

    out_copy.start()

    @pl.when(seg < n_seg - 1)
    def _():
        for block in range(blocks):
            up_copy(block).wait_recv()
        back_product()

    def grad_rows(block):
        start = pl.multiple_of(block * ROWS, ROWS)
        rows = pl.ds(start, ROWS)
        pg[pl.ds(pl.multiple_of(PAD + start, ROWS), ROWS), :] = (
            gs[rows, :] * slope[rows, :]
        ).astype(BF)

    grad_rows(0)
    grad_rows(blocks - 1)
    halo_start(pg, 2)

    @pl.loop(1, blocks - 1)
    def _(block):
        grad_rows(block)

    kg_start = 384 * row + 128 * column
    kg_window = pl.ds(pl.multiple_of(kg_start, LANES), 2 * LANES)

    def tap_grads():
        @pl.loop(0, chunks)
        def _(chunk):
            columns = pl.ds(pl.multiple_of(chunk * LANES, LANES), LANES)
            padded = pm[:, columns].astype(F32)
            grad = pg[PAD : PAD + frames, columns].astype(F32)
            total = padded.shape[0]
            for r in range(8):
                moved = padded if r == 0 else pltpu.roll(padded, total - r, 0)
                for base in range(0, 2 * PAD, 8):
                    tap = base + r - 1
                    if 0 <= tap < taps:
                        kg_ref[tap : tap + 1, columns] = jnp.sum(
                            grad * moved[base : base + frames], axis=0, keepdims=True
                        )

        if relay:
            for by in range(1, n_mp):
                kg_copy(lax.rem(mp + by, n_mp), mp).start()

    @pl.when(seg == 0)
    def _():
        tap_grads()

    halo_wait(pg, 2)

    @pl.loop(0, chunks)
    def _(chunk):
        columns = pl.ds(pl.multiple_of(chunk * LANES, LANES), LANES)
        gs[:, columns] = tap_sum(pg[:, columns].astype(F32), columns, False) * mask_rows(0, frames)

    @pl.loop(0, blocks)
    def _(block):
        rows = pl.ds(pl.multiple_of(block * ROWS, ROWS), ROWS)
        masked = gs[rows, :]
        normed = norm[rows, :]
        first = jnp.mean(masked, axis=-1, keepdims=True)
        second = jnp.mean(masked * normed, axis=-1, keepdims=True)
        grad = inv[rows, :][:, :1] * (masked - first - normed * second)
        gin_ref[rows, :] = (up[rows, :].astype(F32) + grad).astype(BF)

        @pl.when(seg > 0)
        def _():
            up_copy(block).start()

    gin_copy.start()

    @pl.when(seg > 0)
    def _():
        tap_grads()

    if relay:
        total = kg_ref[:, kg_window]
        for by in range(1, n_mp):
            sender = lax.rem(mp + n_mp - by, n_mp)
            kg_copy(mp, sender).wait_recv()
            total = total + kg_land[sender]
        scale = (frames * n_mp) ** (-0.5)
        even, odd = total[:taps, :own], total[:taps, 2 * LANES - own :]
        kg_out[0] = jnp.where(column == 0, even, odd) * scale
        for by in range(1, n_mp):
            kg_copy(lax.rem(mp + by, n_mp), mp).wait_send()
        passed()
    else:
        kg_out[0] = kg_ref[:taps, :]

    out_copy.wait()
    gin_copy.wait()
    halo_sent(pm, 0)
    halo_sent(pg, 2)

    @pl.when(seg < n_seg - 1)
    def _():
        for tile in range(tiles):
            in_copy(tile).wait_send()

    @pl.when(seg > 0)
    def _():
        for block in range(blocks):
            up_copy(block).wait_send()


def on_device(frames_in, section_weights, conv_kernels, valid_length, out_cotangent):
    frames, width = frames_in.shape
    taps = conv_kernels.shape[1]
    n_mp = lax.axis_size("mp")
    own = width // n_mp
    if width == 1536 and n_mp == 8 and frames == 128:
        return spread_call(frames_in, section_weights, conv_kernels, valid_length, out_cotangent)
    relay = False
    weight = section_weights[0]
    if not relay:
        weight = lax.all_gather(weight, "mp", axis=0, tiled=True)
    vmem = pl.BlockSpec(memory_space=pltpu.VMEM)
    smem = pl.BlockSpec(memory_space=pltpu.SMEM)
    whole = pl.BlockSpec(memory_space=pl.ANY)
    padded = (frames + 2 * PAD, width)
    tap_rows = -(-taps // 8) * 8
    dma = pltpu.SemaphoreType.DMA
    out, gin, grad = pl.pallas_call(
        functools.partial(cascade, relay),
        out_shape=(
            jax.ShapeDtypeStruct((1, frames, width), BF),
            jax.ShapeDtypeStruct((1, frames, width), BF),
            jax.ShapeDtypeStruct((1, taps, own if relay else width), F32),
        ),
        in_specs=[whole, whole, whole, smem, whole],
        out_specs=(whole, whole, vmem),
        scratch_shapes=[
            pltpu.VMEM((frames, width), BF),
            pltpu.VMEM((frames, width), BF),
            pltpu.VMEM((frames, width), F32),
            pltpu.VMEM((frames, LANES), F32),
            pltpu.VMEM(padded, BF),
            pltpu.VMEM(padded, BF),
            pltpu.VMEM((frames, width), BF),
            pltpu.VMEM((frames, width), F32),
            pltpu.VMEM((frames, width), F32),
            pltpu.VMEM((frames, width), BF),
            pltpu.VMEM((frames, width), BF),
            pltpu.VMEM((width, width), BF),
            pltpu.VMEM((taps, width), BF),
            pltpu.VMEM((taps, width), F32),
            pltpu.VMEM((tap_rows, width), F32),
            pltpu.VMEM((n_mp if relay else 1, tap_rows, 2 * LANES), F32),
            dma((4,)), dma((4,)),
            dma((width // WIDE,)), dma((width // WIDE,)),
            dma((frames // ROWS,)), dma((frames // ROWS,)),
            dma((6,)),
            dma((3, n_mp)), dma((n_mp,)), dma((2,)), dma((2,)), dma((n_mp,)), dma((n_mp,)),
            pltpu.SemaphoreType.REGULAR,
        ],
        compiler_params=pltpu.CompilerParams(
            collective_id=0, has_side_effects=True, vmem_limit_bytes=60 * 2**20
        ),
    )(frames_in, weight, conv_kernels[0], valid_length, out_cotangent)
    if not relay:
        grad = lax.psum_scatter(grad, "mp", scatter_dimension=2, tiled=True)
        grad = grad * (frames * n_mp) ** (-0.5)
    return (out, gin, grad)


def solution(mesh):
    in_specs = (
        P("mp", None),
        P("segment", "mp", None),
        P("segment", None, None),
        P(),
        P("mp", None),
    )
    out_specs = (P("segment", "mp", None), P("segment", "mp", None), P("segment", None, "mp"))
    return jax.shard_map(
        on_device, mesh=mesh, in_specs=in_specs, out_specs=out_specs, check_vma=False
    )
```

```python
import functools

import jax
import jax.numpy as jnp
from jax import lax
from jax.experimental import pallas as pl
from jax.experimental.pallas import tpu as pltpu
from jax.sharding import PartitionSpec as P

EPSILON = 1e-05
PAD = 16
LANES = 128
ROWS = 16
WIDE = 256
MESH = pl.DeviceIdType.MESH
NORM_ROWS = 32
BF = jnp.bfloat16
F32 = jnp.float32

STAGES = ((0, 0, 0), (1, 0, 0), (1, 0, 1), (2, 0, 0), (2, 0, 1), (0, 1, 0), (1, 1, 0), (1, 1, 1), (2, 1, 0), (2, 1, 1), (0, 2, 0), (1, 2, 0), (1, 2, 1), (2, 2, 0), (2, 2, 1), (0, 3, 0), (1, 3, 0), (1, 3, 1), (3, 3, 0),)
INNER_0 = (
    (13, 76, 74, 8, 10, 73,),
    (47, 87, 271, 80, 81, 206, 111, 23, 335, 70, 16, 17,),
    (),
    (119, 215, 343, 100, 142, 201, 55, 95, 303, 6, 40, 89, 239, 151, 279, 134, 144, 209, 31, 127, 367, 199, 25, 194, 136, 247, 159, 359, 39, 232, 145, 354, 63, 223, 311,),
    (),
    (),
    (295, 137, 208, 290, 183, 375, 383, 263, 240, 153, 258,),
    (),
    (175, 319, 399, 327, 200, 217, 322, 191, 287, 463, 231, 255, 351, 167,),
    (),
    (486,),
    (391, 495, 386,),
    (),
    (511, 423,),
    (),
    (407, 418, 401,),
    (415, 455, 431, 450,),
    (),
    (439, 447, 471, 479, 503,),
)
INNER_1 = (
    (268, 333, 330, 265, 266, 328,),
    (79, 327, 367, 343, 73, 322, 336, 15, 263, 303, 279, 258, 296, 273,),
    (),
    (71, 111, 87, 351, 66, 81, 272, 7, 23, 311, 287, 2, 17, 360, 103, 119, 95, 359, 98, 352, 337, 39, 47, 55, 31, 34, 304, 345, 127, 167, 151, 375, 162, 145, 368, 63, 199, 143, 383,),
    (),
    (),
    (194, 137, 396, 231, 239, 183, 191, 226, 281, 460,),
    (),
    (135, 175, 215, 223, 130, 457, 247, 255, 319, 484, 393, 394, 207, 159, 295, 492,),
    (458,),
    (),
    (391, 431, 404, 401, 386,),
    (455, 471, 424, 465,),
    (450,),
    (),
    (439,),
    (423, 415, 464, 409, 503,),
    (479, 496, 473,),
    (447, 511,),
)
CORNER_0 = (68, 65, 4, 1, 66, 103, 327, 132, 129, 98, 39, 263, 32, 197, 2, 167, 295, 192, 130, 231, 391, 194, 455, 34, 423, 290, 258, 322, 226, 162, 386, 418, 450,)
CORNER_1 = (261, 324, 322, 256, 258, 321, 71, 295, 66, 288, 389, 7, 359, 2, 384, 453, 135, 423, 129, 354, 448, 39, 487, 34, 416, 199, 167, 193, 162, 194, 230, 130, 482, 290, 386, 450, 418,)
SENDS = 50
PIECES = 2
LATE = ((3,), (), (1,), (0, 2))


def decode(event):
    return event // 128, event // 64 % 2, event // 32 % 2, event // 8 % 4, event // 4 % 2, event % 4


def spread(
    x_any, w_any, k_any, vl_ref, cot_any,
    out_whole, gin_whole, kg_out,
    w, a, up, norm, inv, pm, pg, act, slope, gs, k_bf, k_ref, kg, kg_sib, kg_sum, kg_land,
    local_sem, x_send, x_recv, k_send, k_recv, own_send, rel_send, rel_recv, sib_send, sib_recv,
    halo_send, halo_recv, out_send, out_recv, gin_send, gin_recv, pair_send, pair_recv, kg_send, kg_recv,
):
    n_sec, rows_in, width = w.shape
    part = a.shape[1]
    taps = k_ref.shape[1]
    seg, mp = lax.axis_index("segment"), lax.axis_index("mp")
    n_seg, n_mp = lax.axis_size("segment"), lax.axis_size("mp")
    own = rows_in // n_mp
    half = own // (2 * PIECES)
    chunks = width // LANES
    tiles = width // WIDE
    x, c = lax.div(seg, 2), lax.rem(seg, 2)
    z, y = lax.div(mp, 2), lax.rem(mp, 2)
    inner = (z == 1) | (z == 2)
    block = jnp.where(c == 1, mp, jnp.where(z == 1, y, 6 + y))
    which = x + y - 2 * x * y
    chunk_id = 2 * block + which
    chip = 4 * x + mp - 2

    def device_of(number, half_of):
        side, core = number % 2, ((number >= 2) & (number < 6)) * 1
        return 2 * (half_of + side - 2 * half_of * side) + core, (number >= 4) * 2 + 2 + side

    barrier = pltpu.get_barrier_semaphore()
    last = 2 * n_mp - 1
    prev_id, next_id = chunk_id - 1, chunk_id + 1
    greetings = [(None, (lax.rem(seg + by, n_seg), mp)) for by in range(1, n_seg)]
    greetings.append((None, (seg, mp + 1 - 2 * y)))
    greetings.append((z > 0, (seg, mp - 2)))
    greetings.append((z < n_mp // 2 - 1, (seg, mp + 2)))
    greetings.append((inner & (chunk_id > 0), device_of(lax.div(prev_id, 2), lax.rem(prev_id, 2))))
    greetings.append((inner & (chunk_id < last), device_of(lax.div(next_id, 2), lax.rem(next_id, 2))))

    def greet(device):
        pl.semaphore_signal(barrier, inc=1, device_id=device, device_id_type=MESH)

    for there, device in greetings:
        if there is None:
            greet(device)
        else:
            pl.when(there)(lambda: greet(device))

    w_copy = pltpu.make_async_copy(
        w_any, w.at[seg, pl.ds(pl.multiple_of(own * mp, own), own)], local_sem.at[0]
    )
    k_copy = pltpu.make_async_copy(k_any, k_bf.at[seg], local_sem.at[1])
    w_copy.start()

    @pl.when(inner)
    def _():
        k_copy.start()

    count = n_seg
    for there, _ in greetings[n_seg:]:
        count = count + jnp.where(there, 1, 0)
    pl.semaphore_wait(barrier, count)

    def half_ref(section, shard, piece, core):
        start = own * shard + half * (2 * piece + core)
        return w.at[section, pl.ds(pl.multiple_of(start, half), half)]

    def own_copy(kind, piece):
        core = c if kind else 1 - c
        return pltpu.make_async_remote_copy(
            src_ref=half_ref(seg, mp, piece, core), dst_ref=half_ref(seg, mp, piece, core),
            send_sem=own_send.at[2 * piece + kind],
            recv_sem=(sib_recv if kind else rel_recv).at[(seg * n_mp + mp) * PIECES + piece],
            device_id={"segment": seg + 1 - 2 * c}, device_id_type=MESH,
        )

    def relay_copy(section, shard, piece, way, slot):
        target = (
            {"segment": seg + 2 - 4 * x}, {"mp": mp + 1 - 2 * y}, {"mp": mp + jnp.where(z < 2, 2, -2)}
        )[way]
        return pltpu.make_async_remote_copy(
            src_ref=half_ref(section, shard, piece, c), dst_ref=half_ref(section, shard, piece, c),
            send_sem=rel_send.at[slot], recv_sem=rel_recv.at[(section * n_mp + shard) * PIECES + piece],
            device_id=target, device_id_type=MESH,
        )

    def sib_copy(section, shard, piece, core):
        sem = (section * n_mp + shard) * PIECES + piece
        return pltpu.make_async_remote_copy(
            src_ref=half_ref(section, shard, piece, core), dst_ref=half_ref(section, shard, piece, core),
            send_sem=sib_send.at[sem], recv_sem=sib_recv.at[sem],
            device_id={"segment": seg + 1 - 2 * c}, device_id_type=MESH,
        )

    def shard_of(across, depth):
        from_y = 1 - y if across else y
        return 2 * jnp.where(z < 2, depth, 3 - depth) + from_y

    def is_home(section, across, depth, plane, corner):
        return section // 2 == plane and across == 0 and depth == (0 if corner else 1)

    def run_events(events, plane, corner, slot):
        for event in events:
            section, piece, across, depth, first, way = decode(event)
            shard = shard_of(across, depth)
            if first and is_home(section, across, depth, plane, corner):
                pl.when(c != section % 2)(relay_copy(section, shard, piece, 0, 0).wait_recv)
            elif first:
                relay_copy(section, shard, piece, 0, 0).wait_recv()
                if not corner:
                    sib_copy(section, shard, piece, c).start()
            if way < 3:
                relay_copy(section, shard, piece, way, slot).start()
                slot += 1
        return slot

    def finish_events(groups, plane, corner):
        slot = 0
        for events in groups:
            for event in events:
                section, piece, across, depth, first, way = decode(event)
                shard = shard_of(across, depth)
                if first and not corner and not is_home(section, across, depth, plane, corner):
                    sib_copy(section, shard, piece, c).wait_send()
                if way < 3:
                    relay_copy(section, shard, piece, way, slot).wait_send()
                    slot += 1

    def siblings(section, plane):
        for across in range(2):
            for depth in range(4):
                for piece in range(PIECES):
                    wait = sib_copy(section, shard_of(across, depth), piece, 1 - c).wait_recv
                    if is_home(section, across, depth, plane, False):
                        pl.when(c != section % 2)(wait)
                    else:
                        wait()

    to_seg, to_mp = device_of(mp, which)
    sends_x = seg == to_seg
    away = sends_x & (to_mp != mp)

    def x_move(index, remote):
        rows = pl.ds(pl.multiple_of(part * which, part), part)
        source, target = ((x_any, a.at[0]), (cot_any, up.at[n_sec]))[index]
        if not remote:
            return pltpu.make_async_copy(source.at[rows], target, x_recv.at[index])
        return pltpu.make_async_remote_copy(
            src_ref=source.at[rows], dst_ref=target, send_sem=x_send.at[index], recv_sem=x_recv.at[index],
            device_id={"mp": to_mp}, device_id_type=MESH,
        )

    def x_start(index):
        pl.when(inner & (c == 1))(lambda: x_move(index, False).start())
        pl.when(away)(lambda: x_move(index, True).start())

    def x_wait(index):
        pl.when(c == 1)(lambda: x_move(index, False).wait())
        pl.when(c == 0)(lambda: x_move(index, True).wait_recv())

    def k_move(by, sender):
        return pltpu.make_async_remote_copy(
            src_ref=k_any, dst_ref=k_bf.at[sender], send_sem=k_send.at[by - 1], recv_sem=k_recv.at[sender],
            device_id={"segment": lax.rem(seg + by, n_seg)}, device_id_type=MESH,
        )

    w_copy.wait()
    for piece in range(PIECES):
        own_copy(0, piece).start()
        pl.when(inner)(own_copy(1, piece).start)

    @pl.when(inner)
    def _():
        for by in range(1, n_sec):
            k_move(by, seg).start()

    x_start(0)

    corner = jnp.logical_not(inner)
    for plane, table in ((0, CORNER_0), (1, CORNER_1)):

        @pl.when(corner & (x == plane))
        def _():
            run_events(table, plane, True, 0)

    x_start(1)

    def mask_rows(start, count):
        position = chunk_id * part + start + lax.broadcasted_iota(jnp.int32, (count, LANES), 0)
        return (position < vl_ref[0]).astype(F32)

    def halo_copy(pad_ref, section, slot, to_next):
        rows_from = pl.ds(part, PAD) if to_next else pl.ds(PAD, PAD)
        rows_to = pl.ds(0, PAD) if to_next else pl.ds(part + PAD, PAD)
        near = chunk_id + (1 if to_next else -1)
        target = device_of(lax.div(near, 2), lax.rem(near, 2))
        sem = 6 * section + 2 * slot + (0 if to_next else 1)
        columns = pl.ds(0, width) if slot == 0 else pl.ds((slot - 1) * side, side)
        return pltpu.make_async_remote_copy(
            src_ref=pad_ref.at[section, rows_from, columns], dst_ref=pad_ref.at[section, rows_to, columns],
            send_sem=halo_send.at[sem], recv_sem=halo_recv.at[sem],
            device_id=target, device_id_type=MESH,
        )

    side = width // 2

    def halo_start(pad_ref, section, slot):
        pl.when(chunk_id < last)(lambda: halo_copy(pad_ref, section, slot, True).start())
        pl.when(chunk_id > 0)(lambda: halo_copy(pad_ref, section, slot, False).start())

    def halo_wait(pad_ref, section, slot):
        pl.when(chunk_id > 0)(lambda: halo_copy(pad_ref, section, slot, True).wait_recv())
        pl.when(chunk_id < last)(lambda: halo_copy(pad_ref, section, slot, False).wait_recv())

    def halo_sent(pad_ref, section, slot):
        pl.when(chunk_id < last)(lambda: halo_copy(pad_ref, section, slot, True).wait_send())
        pl.when(chunk_id > 0)(lambda: halo_copy(pad_ref, section, slot, False).wait_send())

    def tap_sum(padded, section, columns, forward):
        rows = padded.shape[0]
        running = jnp.zeros((part, LANES), F32)
        for r in range(8):
            moved = padded if r == 0 else pltpu.roll(padded, rows - r, 0)
            for base in range(0, 2 * PAD, 8):
                offset = base + r
                if 1 <= offset <= taps:
                    tap = offset - 1 if forward else taps - offset
                    running = running + k_ref[section, tap : tap + 1, columns] * moved[base : base + part]
        return running

    def normalize(section):
        for start in range(0, part, NORM_ROWS):
            rows = slice(start, start + NORM_ROWS)
            values = a[section, rows].astype(F32)
            center = values - jnp.mean(values, axis=-1, keepdims=True)
            inverse = lax.rsqrt(jnp.mean(center * center, axis=-1, keepdims=True) + EPSILON)
            normed = center * inverse
            norm[section, rows] = normed
            inv[section, rows] = jnp.broadcast_to(inverse, (NORM_ROWS, LANES))
            pm[section, PAD + start : PAD + start + NORM_ROWS] = (
                normed * mask_rows(start, NORM_ROWS)[:, :1]
            ).astype(BF)
        halo_start(pm, section, 0)

    def convolve(section, step):
        if step == 0:
            halo_wait(pm, section, 0)

        @pl.loop(step * chunks // 2, (step + 1) * chunks // 2)
        def _(chunk):
            columns = pl.ds(pl.multiple_of(chunk * LANES, LANES), LANES)
            conv = tap_sum(pm[section, :, columns].astype(F32), section, columns, True)
            gate = jax.nn.sigmoid(conv)
            act[section, :, columns] = (conv * gate).astype(BF)
            slope[section, :, columns] = gate * (1.0 + conv * (1.0 - gate))

    def result_copy(source, index, section, whole, send, recv, remote):
        rows = pl.ds(pl.multiple_of(part * which, part), part)
        if not remote:
            return pltpu.make_async_copy(source.at[index], whole.at[0, rows], recv.at[which])
        return pltpu.make_async_remote_copy(
            src_ref=source.at[index], dst_ref=whole.at[0, rows],
            send_sem=send.at[section], recv_sem=recv.at[which],
            device_id=(section, block), device_id_type=MESH,
        )

    def result_start(section, *what):
        same = (seg == section) & (mp == block)
        pl.when(same)(lambda: result_copy(*what, False).start())
        pl.when(jnp.logical_not(same))(lambda: result_copy(*what, True).start())

    def result_sent(section, *what):
        same = (seg == section) & (mp == block)
        pl.when(jnp.logical_not(same))(lambda: result_copy(*what, True).wait_send())

    def result_wait(source, whole, send, recv):
        for half_of in range(2):
            from_seg, from_mp = device_of(mp, half_of)
            same = (seg == from_seg) & (mp == from_mp)
            rows = pl.ds(part * half_of, part)

            @pl.when(same)
            def _():
                pltpu.make_async_copy(source.at[0], whole.at[0, rows], recv.at[half_of]).wait()

            @pl.when(jnp.logical_not(same))
            def _():
                pltpu.make_async_remote_copy(
                    src_ref=source.at[0], dst_ref=whole.at[0, rows],
                    send_sem=send.at[0], recv_sem=recv.at[half_of],
                    device_id=(seg, mp), device_id_type=MESH,
                ).wait_recv()

    def product(section, step):
        for tile in range(step * tiles // 2, (step + 1) * tiles // 2):
            columns = slice(tile * WIDE, (tile + 1) * WIDE)
            result = jnp.dot(act[section], w[section, :, columns], preferred_element_type=F32)
            a[section + 1, :, columns] = (a[section, :, columns].astype(F32) + result).astype(BF)

    def out_what(section):
        return section, a, section + 1, section, out_whole, out_send, out_recv

    def gin_what(section):
        return section, up, section, section, gin_whole, gin_send, gin_recv

    def out_start(section, late):
        at_once = (c == 0) | (x == section // 2)
        pl.when(jnp.logical_not(at_once) if late else at_once)(lambda: result_start(*out_what(section)))

    def gin_start(section, late):
        pl.when(c == (1 if late else 0))(lambda: result_start(*gin_what(section)))

    def forward_stage(kind, section, step):
        if kind == 0:
            if section == 0:
                x_wait(0)
                k_copy.wait()
                for by in range(1, n_sec):
                    k_move(by, lax.rem(seg + n_seg - by, n_seg)).wait_recv()
                for s in range(n_sec):
                    k_ref[s] = k_bf[s].astype(F32)
                for pad_ref in (pm, pg):

                    @pl.when(chunk_id == 0)
                    def _():
                        for s in range(n_sec):
                            pad_ref[s, 0:PAD, :] = jnp.zeros((PAD, width), BF)

                    @pl.when(chunk_id == last)
                    def _():
                        for s in range(n_sec):
                            pad_ref[s, part + PAD : part + 2 * PAD, :] = jnp.zeros((PAD, width), BF)

                kg[:, taps:, :] = jnp.zeros((n_sec, kg.shape[1] - taps, width), F32)
            normalize(section)
        elif kind == 1:
            convolve(section, step)
        elif kind == 3:
            for plane in range(2):
                pl.when(x == plane)(lambda: siblings(section, plane))
            last_back_product()
        else:
            if step == 0:
                for plane in range(2):
                    pl.when(x == plane)(lambda: siblings(section, plane))
            product(section, step)
            if step == 1:
                out_start(section, False)

    def kg_window(index, core):
        return pl.ds(pl.multiple_of(384 * index + 128 * core, LANES), 2 * LANES)

    def kg_pair(section):
        return pltpu.make_async_remote_copy(
            src_ref=kg.at[section], dst_ref=kg_sib.at[section],
            send_sem=pair_send.at[section], recv_sem=pair_recv.at[section],
            device_id={"segment": seg + 1 - 2 * c}, device_id_type=MESH,
        )

    def kg_copy(section, index, remote):
        if not remote:
            return pltpu.make_async_copy(kg_sum.at[section, index], kg_land.at[chip], kg_recv.at[chip])
        return pltpu.make_async_remote_copy(
            src_ref=kg_sum.at[section, index], dst_ref=kg_land.at[chip],
            send_sem=kg_send.at[4 * section + index], recv_sem=kg_recv.at[chip],
            device_id=(section, 2 * index + c), device_id_type=MESH,
        )

    def kg_start(section):
        kg_pair(section).wait_recv()
        for index in range(n_mp // 2):
            window = kg_window(index, c)
            kg_sum[section, index] = kg[section, :, window] + kg_sib[section, :, window]
            same = (seg == section) & (mp == 2 * index + c)
            pl.when(same)(lambda: kg_copy(section, index, False).start())
            pl.when(jnp.logical_not(same))(lambda: kg_copy(section, index, True).start())

    def tap_grads(section):
        @pl.loop(0, chunks)
        def _(chunk):
            columns = pl.ds(pl.multiple_of(chunk * LANES, LANES), LANES)
            padded = pm[section, :, columns].astype(F32)
            grad = pg[section, PAD : PAD + part, columns].astype(F32)
            rows = padded.shape[0]
            for r in range(8):
                moved = padded if r == 0 else pltpu.roll(padded, rows - r, 0)
                for base in range(0, 2 * PAD, 8):
                    tap = base + r - 1
                    if 0 <= tap < taps:
                        kg[section, tap : tap + 1, columns] = jnp.sum(
                            grad * moved[base : base + part], axis=0, keepdims=True
                        )

        kg_pair(section).start()

    def back_tile(section, tile):
        columns = slice(tile * WIDE, (tile + 1) * WIDE)
        return columns, lax.dot_general(
            up[section + 1], w[section, columns, :], (((1,), (1,)), ((), ())), preferred_element_type=F32
        )

    def last_back_product():
        x_wait(1)
        for tile in range(tiles):
            columns, grad = back_tile(n_sec - 1, tile)
            gs[:, columns] = grad

    def backward(section):
        for part_of in range(2):
            for tile in range(part_of * tiles // 2, (part_of + 1) * tiles // 2):
                if section == n_sec - 1:
                    columns = slice(tile * WIDE, (tile + 1) * WIDE)
                    grad = gs[:, columns]
                else:
                    columns, grad = back_tile(section, tile)
                pg[section, PAD : PAD + part, columns] = (grad * slope[section, :, columns]).astype(BF)
            halo_start(pg, section, 1 + part_of)
        tap_grads(section)
        if section == n_sec - 1:
            product(section, 0)
            product(section, 1)
            out_start(section, False)
        else:
            kg_start(section + 1)
        for part_of in range(2):
            halo_wait(pg, section, 1 + part_of)
            if part_of == 1:
                if section < n_sec - 1:
                    gin_start(section + 1, True)
                for other in LATE[section]:
                    out_start(other, True)
                if section == 0:
                    kg_start(section)

            @pl.loop(part_of * chunks // 2, (part_of + 1) * chunks // 2)
            def _(chunk):
                columns = pl.ds(pl.multiple_of(chunk * LANES, LANES), LANES)
                gs[:, columns] = tap_sum(
                    pg[section, :, columns].astype(F32), section, columns, False
                ) * mask_rows(0, part)

        for start in range(0, part, NORM_ROWS):
            rows = slice(start, start + NORM_ROWS)
            masked = gs[rows]
            normed = norm[section, rows]
            first = jnp.mean(masked, axis=-1, keepdims=True)
            second = jnp.mean(masked * normed, axis=-1, keepdims=True)
            grad = inv[section, rows][:, :1] * (masked - first - normed * second)
            up[section, rows] = (up[section + 1, rows].astype(F32) + grad).astype(BF)
        gin_start(section, False)
        if section == 0:
            gin_start(section, True)

    slots = [0, 0]
    for index, (kind, section, step) in enumerate(STAGES):
        for plane, table in ((0, INNER_0), (1, INNER_1)):
            if table[index]:
                start = slots[plane]

                @pl.when(inner & (x == plane))
                def _():
                    run_events(table[index], plane, False, start)

                slots[plane] += sum(event % 4 < 3 for event in table[index])
        pl.when(inner)(lambda: forward_stage(kind, section, step))
    @pl.when(inner)
    def _():
        for section in reversed(range(n_sec)):
            backward(section)

    sums = jnp.zeros((kg.shape[1], 2 * LANES), F32)
    for number in range(n_mp):
        from_seg, from_mp = 2 * (number // 4) + y, number % 4 + 2
        same = (seg == from_seg) & (mp == from_mp)

        @pl.when(same)
        def _():
            pltpu.make_async_copy(kg_sum.at[0, 0], kg_land.at[number], kg_recv.at[number]).wait()

        @pl.when(jnp.logical_not(same))
        def _():
            pltpu.make_async_remote_copy(
                src_ref=kg_sum.at[0, 0], dst_ref=kg_land.at[number],
                send_sem=kg_send.at[0], recv_sem=kg_recv.at[number],
                device_id=(seg, mp), device_id_type=MESH,
            ).wait_recv()

        sums = sums + kg_land[number]
    scale = (2 * part * n_mp) ** (-0.5)
    even, odd = sums[:taps, :own], sums[:taps, 2 * LANES - own :]
    kg_out[:, 0, :] = jnp.where(y == 0, even, odd) * scale

    result_wait(a, out_whole, out_send, out_recv)
    result_wait(up, gin_whole, gin_send, gin_recv)

    for piece in range(PIECES):
        own_copy(0, piece).wait_send()
    for index in range(2):
        pl.when(away)(lambda: x_move(index, True).wait_send())
    for plane, table in ((0, CORNER_0), (1, CORNER_1)):
        pl.when(corner & (x == plane))(lambda: finish_events((table,), plane, True))
    for plane, table in ((0, INNER_0), (1, INNER_1)):
        pl.when(inner & (x == plane))(lambda: finish_events(table, plane, False))

    @pl.when(inner)
    def _():
        for piece in range(PIECES):
            own_copy(1, piece).wait_send()
        for by in range(1, n_sec):
            k_move(by, seg).wait_send()
        for section in range(n_sec):
            halo_sent(pm, section, 0)
            halo_sent(pg, section, 1)
            halo_sent(pg, section, 2)
            result_sent(*out_what(section))
            result_sent(*gin_what(section))
            kg_pair(section).wait_send()
            for index in range(n_mp // 2):
                same = (seg == section) & (mp == 2 * index + c)
                pl.when(jnp.logical_not(same))(lambda: kg_copy(section, index, True).wait_send())


def spread_call(frames_in, section_weights, conv_kernels, valid_length, out_cotangent):
    frames, width = frames_in.shape
    taps = conv_kernels.shape[1]
    n_sec, n_mp = lax.axis_size("segment"), lax.axis_size("mp")
    own = width // n_mp
    part = frames // 2
    vmem = pl.BlockSpec(memory_space=pltpu.VMEM)
    smem = pl.BlockSpec(memory_space=pltpu.SMEM)
    whole = pl.BlockSpec(memory_space=pl.ANY)
    tap_rows = -(-taps // 8) * 8
    dma = pltpu.SemaphoreType.DMA
    out, gin, grad = pl.pallas_call(
        spread,
        out_shape=(
            jax.ShapeDtypeStruct((1, frames, width), BF),
            jax.ShapeDtypeStruct((1, frames, width), BF),
            jax.ShapeDtypeStruct((taps, 1, own), F32),
        ),
        in_specs=[whole, whole, whole, smem, whole],
        out_specs=(whole, whole, vmem),
        scratch_shapes=[
            pltpu.VMEM((n_sec, width, width), BF),
            pltpu.VMEM((n_sec + 1, part, width), BF),
            pltpu.VMEM((n_sec + 1, part, width), BF),
            pltpu.VMEM((n_sec, part, width), F32),
            pltpu.VMEM((n_sec, part, LANES), F32),
            pltpu.VMEM((n_sec, part + 2 * PAD, width), BF),
            pltpu.VMEM((n_sec, part + 2 * PAD, width), BF),
            pltpu.VMEM((n_sec, part, width), BF),
            pltpu.VMEM((n_sec, part, width), F32),
            pltpu.VMEM((part, width), F32),
            pltpu.VMEM((n_sec, taps, width), BF),
            pltpu.VMEM((n_sec, taps, width), F32),
            pltpu.VMEM((n_sec, tap_rows, width), F32),
            pltpu.VMEM((n_sec, tap_rows, width), F32),
            pltpu.VMEM((n_sec, n_mp // 2, tap_rows, 2 * LANES), F32),
            pltpu.VMEM((n_mp, tap_rows, 2 * LANES), F32),
            dma((2,)), dma((2,)), dma((2,)), dma((n_sec - 1,)), dma((n_sec,)),
            dma((2 * PIECES,)), dma((SENDS,)),
            dma((PIECES * n_sec * n_mp,)), dma((PIECES * n_sec * n_mp,)), dma((PIECES * n_sec * n_mp,)),
            dma((6 * n_sec,)), dma((6 * n_sec,)),
            dma((n_sec,)), dma((2,)), dma((n_sec,)), dma((2,)),
            dma((n_sec,)), dma((n_sec,)), dma((4 * n_sec,)), dma((n_mp,)),
        ],
        compiler_params=pltpu.CompilerParams(
            collective_id=1, has_side_effects=True, vmem_limit_bytes=60 * 2**20
        ),
    )(frames_in, section_weights[0], conv_kernels[0], valid_length, out_cotangent)
    return out, gin, grad.transpose(1, 0, 2)


def cascade(
    relay, x_any, w_any, k_any, vl_ref, cot_any,
    out_whole, gin_whole, kg_out,
    cur, up, norm, inv, pm, pg, act, slope, gs, out_ref, gin_ref, w_ref, k_bf, k_ref, kg_ref, kg_land,
    halo_send, halo_recv, in_send, in_recv, up_send, up_recv,
    local_sem, w_send, w_recv, end_send, end_recv, kg_send, kg_recv, turn_sem,
):
    frames, width = x_any.shape
    taps = k_ref.shape[0]
    seg, mp = lax.axis_index("segment"), lax.axis_index("mp")
    n_seg, n_mp = lax.axis_size("segment"), lax.axis_size("mp")
    chunks = width // LANES
    blocks = frames // ROWS
    tiles = width // WIDE

    barrier = pltpu.get_barrier_semaphore()
    steps_mp = range(1, n_mp) if relay else (1, n_mp - 1)
    for axis, index, count, steps in (
        ("segment", seg, n_seg, (1, n_seg - 1)), ("mp", mp, n_mp, steps_mp)
    ):
        for by in steps:
            pl.semaphore_signal(
                barrier, inc=1, device_id={axis: lax.rem(index + by, count)}, device_id_type=MESH
            )
    own = width // n_mp
    w_rows = pl.ds(pl.multiple_of(mp * own, own), own) if relay else pl.ds(0, width)
    w_copy = pltpu.make_async_copy(w_any, w_ref.at[w_rows], local_sem.at[0])
    x_copy = pltpu.make_async_copy(x_any, cur, local_sem.at[1])
    cot_copy = pltpu.make_async_copy(cot_any, up, local_sem.at[2])
    k_copy = pltpu.make_async_copy(k_any, k_bf, local_sem.at[3])
    out_copy = pltpu.make_async_copy(out_ref, out_whole.at[0], local_sem.at[4])
    gin_copy = pltpu.make_async_copy(gin_ref, gin_whole.at[0], local_sem.at[5])
    w_copy.start()
    k_copy.start()

    @pl.when(seg == 0)
    def _():
        x_copy.start()

    @pl.when(seg == n_seg - 1)
    def _():
        cot_copy.start()

    pl.semaphore_wait(barrier, 2 + len(steps_mp))

    row, column = lax.div(mp, 2), lax.rem(mp, 2)
    n_row = n_mp // 2

    half = own // 2

    def block_copy(block, way, count=own):
        rows = pl.ds(pl.multiple_of(block * own, own), count)
        target = (mp + 2, mp - 2, mp + 1 - 2 * column)[way]
        return pltpu.make_async_remote_copy(
            src_ref=w_ref.at[rows], dst_ref=w_ref.at[rows],
            send_sem=w_send.at[way, block], recv_sem=w_recv.at[block],
            device_id={"mp": target}, device_id_type=MESH,
        )

    def end_copy(way):
        block = (0 if way == 0 else n_mp - 2) + 1 - column
        rows = pl.ds(pl.multiple_of(block * own + half, half), half)
        return pltpu.make_async_remote_copy(
            src_ref=w_ref.at[rows], dst_ref=w_ref.at[rows],
            send_sem=end_send.at[way], recv_sem=end_recv.at[way],
            device_id={"mp": mp + 2 if way == 0 else mp - 2}, device_id_type=MESH,
        )

    def each_block(distance, act_on, arrive):
        if distance == 0:
            pl.when(row < n_row - 1)(lambda: act_on(mp, 0))
            pl.when(row > 0)(lambda: act_on(mp, 1))
            act_on(mp, 2)
            return
        low, high = mp - 2 * distance, mp + 2 * distance

        @pl.when(row >= distance)
        def _():
            arrive(low)
            pl.when(row < n_row - 1)(lambda: act_on(low, 0))
            pl.when(row == distance)(lambda: act_on(low, 2, half))
            pl.when(row > distance)(lambda: act_on(low, 2))

        @pl.when(row + distance < n_row)
        def _():
            arrive(high)
            pl.when(row > 0)(lambda: act_on(high, 1))
            pl.when(row + distance == n_row - 1)(lambda: act_on(high, 2, half))
            pl.when(row + distance < n_row - 1)(lambda: act_on(high, 2))

    def pass_on(distance):
        each_block(
            distance,
            lambda *what: block_copy(*what).start(),
            lambda block: block_copy(block, 0).wait_recv(),
        )
        if distance == 1:
            for way, end in ((0, 0), (1, n_row - 1)):

                @pl.when(row == end)
                def _():
                    block_copy(2 * end + 1 - column, 2).wait_recv()
                    end_copy(way).start()

    def passed():
        for distance in range(n_row):
            each_block(
                distance,
                lambda *what: block_copy(*what).wait_send(),
                lambda block: None,
            )
        pl.when(row < n_row - 1)(lambda: end_copy(0).wait_send())
        pl.when(row > 0)(lambda: end_copy(1).wait_send())

    def gather_rest(first):
        if relay:
            for distance in range(first, n_row):
                pass_on(distance)

            @pl.when(row > 0)
            def _():
                end_copy(0).wait_recv()
                pl.when(row < n_row - 1)(lambda: end_copy(0).start())

            @pl.when(row < n_row - 1)
            def _():
                end_copy(1).wait_recv()
                pl.when(row > 0)(lambda: end_copy(1).start())

            for index in range(n_row):
                block = index * 2 + 1 - column
                if index in (0, n_row - 1):
                    pl.when(row != index)(lambda: block_copy(block, 2, half).wait_recv())
                else:
                    block_copy(block, 2).wait_recv()

    def kg_copy(target, sender):
        start = 384 * lax.div(target, 2) + 128 * lax.rem(target, 2)
        window = pl.ds(pl.multiple_of(start, LANES), 2 * LANES)
        return pltpu.make_async_remote_copy(
            src_ref=kg_ref.at[:, window], dst_ref=kg_land.at[sender],
            send_sem=kg_send.at[target], recv_sem=kg_recv.at[sender],
            device_id={"mp": target}, device_id_type=MESH,
        )

    w_copy.wait()
    if relay:

        @pl.when(seg != 1)
        def _():
            pass_on(0)

    k_copy.wait()
    k_ref[...] = k_bf[...].astype(F32)
    kg_ref[...] = jnp.zeros(kg_ref.shape, F32)

    def halo_copy(pad_ref, first, to_right):
        rows_from = pl.ds(frames, PAD) if to_right else pl.ds(PAD, PAD)
        rows_to = pl.ds(0, PAD) if to_right else pl.ds(frames + PAD, PAD)
        target = lax.rem(mp + (1 if to_right else n_mp - 1), n_mp)
        slot = first + (0 if to_right else 1)
        return pltpu.make_async_remote_copy(
            src_ref=pad_ref.at[rows_from], dst_ref=pad_ref.at[rows_to],
            send_sem=halo_send.at[slot], recv_sem=halo_recv.at[slot],
            device_id={"mp": target}, device_id_type=MESH,
        )

    def halo_start(pad_ref, first):
        @pl.when(mp < n_mp - 1)
        def _():
            halo_copy(pad_ref, first, True).start()

        @pl.when(mp > 0)
        def _():
            halo_copy(pad_ref, first, False).start()

    def halo_wait(pad_ref, first):
        @pl.when(mp > 0)
        def _():
            halo_copy(pad_ref, first, True).wait_recv()

        @pl.when(mp < n_mp - 1)
        def _():
            halo_copy(pad_ref, first, False).wait_recv()

    def halo_sent(pad_ref, first):
        @pl.when(mp < n_mp - 1)
        def _():
            halo_copy(pad_ref, first, True).wait_send()

        @pl.when(mp > 0)
        def _():
            halo_copy(pad_ref, first, False).wait_send()

    def halo_clear(pad_ref):
        @pl.when(mp == 0)
        def _():
            pad_ref[0:PAD, :] = jnp.zeros((PAD, width), BF)

        @pl.when(mp == n_mp - 1)
        def _():
            pad_ref[frames + PAD : frames + 2 * PAD, :] = jnp.zeros((PAD, width), BF)

    def in_copy(tile):
        columns = pl.ds(tile * WIDE, WIDE)
        return pltpu.make_async_remote_copy(
            src_ref=out_ref.at[:, columns], dst_ref=cur.at[:, columns],
            send_sem=in_send.at[tile], recv_sem=in_recv.at[tile],
            device_id={"segment": lax.rem(seg + 1, n_seg)}, device_id_type=MESH,
        )

    def up_copy(block):
        rows = pl.ds(block * ROWS, ROWS)
        return pltpu.make_async_remote_copy(
            src_ref=gin_ref.at[rows], dst_ref=up.at[rows],
            send_sem=up_send.at[block], recv_sem=up_recv.at[block],
            device_id={"segment": lax.rem(seg + n_seg - 1, n_seg)}, device_id_type=MESH,
        )

    def mask_rows(start, count):
        position = mp * frames + start + lax.broadcasted_iota(jnp.int32, (count, LANES), 0)
        return (position < vl_ref[0]).astype(F32)

    def back_product():
        for tile in range(tiles):
            columns = slice(tile * WIDE, (tile + 1) * WIDE)
            gs[:, columns] = lax.dot_general(
                up[...], w_ref[columns, :], (((1,), (1,)), ((), ())), preferred_element_type=F32
            )

    halo_clear(pm)
    halo_clear(pg)

    @pl.when(seg == n_seg - 1)
    def _():
        gather_rest(1)
        cot_copy.wait()
        back_product()

    @pl.when(seg == 0)
    def _():
        x_copy.wait()

    @pl.when(seg == 1)
    def _():
        if relay:
            pl.semaphore_wait(turn_sem, 1)
            pass_on(0)

    @pl.when((seg > 1) & (seg < n_seg - 1))
    def _():
        gather_rest(1)

    @pl.when(seg > 0)
    def _():
        for tile in range(tiles):
            in_copy(tile).wait_recv()

    def norm_rows(block):
        start = pl.multiple_of(block * ROWS, ROWS)
        rows = pl.ds(start, ROWS)
        values = cur[rows, :].astype(F32)
        center = values - jnp.mean(values, axis=-1, keepdims=True)
        inverse = lax.rsqrt(jnp.mean(center * center, axis=-1, keepdims=True) + EPSILON)
        normed = center * inverse
        norm[rows, :] = normed
        inv[rows, :] = jnp.broadcast_to(inverse, (ROWS, LANES))
        pm[pl.ds(pl.multiple_of(PAD + start, ROWS), ROWS), :] = (
            normed * mask_rows(start, ROWS)[:, :1]
        ).astype(BF)

    norm_rows(0)
    norm_rows(blocks - 1)
    halo_start(pm, 0)

    @pl.loop(1, blocks - 1)
    def _(block):
        norm_rows(block)

    if relay:

        @pl.when(seg < 2)
        def _():
            pass_on(1)

    halo_wait(pm, 0)

    def shifted(padded):
        total = padded.shape[0]
        return [padded if r == 0 else pltpu.roll(padded, total - r, 0) for r in range(8)]

    def tap_sum(padded, columns, forward):
        total = padded.shape[0]
        running = jnp.zeros((frames, LANES), F32)
        for r in range(8):
            moved = padded if r == 0 else pltpu.roll(padded, total - r, 0)
            for base in range(0, 2 * PAD, 8):
                offset = base + r
                if 1 <= offset <= taps:
                    tap = offset - 1 if forward else taps - offset
                    running = running + k_ref[tap : tap + 1, columns] * moved[base : base + frames]
        return running

    @pl.loop(0, chunks)
    def _(chunk):
        columns = pl.ds(pl.multiple_of(chunk * LANES, LANES), LANES)
        conv = tap_sum(pm[:, columns].astype(F32), columns, True)
        gate = jax.nn.sigmoid(conv)
        act[:, columns] = (conv * gate).astype(BF)
        slope[:, columns] = gate * (1.0 + conv * (1.0 - gate))

    if relay:

        @pl.when(seg < 2)
        def _():
            pass_on(2)

        @pl.when(seg == 0)
        def _():
            pl.semaphore_signal(
                turn_sem, inc=1, device_id={"segment": seg + 1}, device_id_type=MESH
            )

        @pl.when(seg < 2)
        def _():
            gather_rest(3)

    for tile in range(tiles):
        columns = slice(tile * WIDE, (tile + 1) * WIDE)
        product = jnp.dot(act[...], w_ref[:, columns], preferred_element_type=F32)
        out_ref[:, columns] = (cur[:, columns].astype(F32) + product).astype(BF)

        @pl.when(seg < n_seg - 1)
        def _():
            in_copy(tile).start()

    out_copy.start()

    @pl.when(seg < n_seg - 1)
    def _():
        for block in range(blocks):
            up_copy(block).wait_recv()
        back_product()

    def grad_rows(block):
        start = pl.multiple_of(block * ROWS, ROWS)
        rows = pl.ds(start, ROWS)
        pg[pl.ds(pl.multiple_of(PAD + start, ROWS), ROWS), :] = (
            gs[rows, :] * slope[rows, :]
        ).astype(BF)

    grad_rows(0)
    grad_rows(blocks - 1)
    halo_start(pg, 2)

    @pl.loop(1, blocks - 1)
    def _(block):
        grad_rows(block)

    kg_start = 384 * row + 128 * column
    kg_window = pl.ds(pl.multiple_of(kg_start, LANES), 2 * LANES)

    def tap_grads():
        @pl.loop(0, chunks)
        def _(chunk):
            columns = pl.ds(pl.multiple_of(chunk * LANES, LANES), LANES)
            padded = pm[:, columns].astype(F32)
            grad = pg[PAD : PAD + frames, columns].astype(F32)
            total = padded.shape[0]
            for r in range(8):
                moved = padded if r == 0 else pltpu.roll(padded, total - r, 0)
                for base in range(0, 2 * PAD, 8):
                    tap = base + r - 1
                    if 0 <= tap < taps:
                        kg_ref[tap : tap + 1, columns] = jnp.sum(
                            grad * moved[base : base + frames], axis=0, keepdims=True
                        )

        if relay:
            for by in range(1, n_mp):
                kg_copy(lax.rem(mp + by, n_mp), mp).start()

    @pl.when(seg == 0)
    def _():
        tap_grads()

    halo_wait(pg, 2)

    @pl.loop(0, chunks)
    def _(chunk):
        columns = pl.ds(pl.multiple_of(chunk * LANES, LANES), LANES)
        gs[:, columns] = tap_sum(pg[:, columns].astype(F32), columns, False) * mask_rows(0, frames)

    @pl.loop(0, blocks)
    def _(block):
        rows = pl.ds(pl.multiple_of(block * ROWS, ROWS), ROWS)
        masked = gs[rows, :]
        normed = norm[rows, :]
        first = jnp.mean(masked, axis=-1, keepdims=True)
        second = jnp.mean(masked * normed, axis=-1, keepdims=True)
        grad = inv[rows, :][:, :1] * (masked - first - normed * second)
        gin_ref[rows, :] = (up[rows, :].astype(F32) + grad).astype(BF)

        @pl.when(seg > 0)
        def _():
            up_copy(block).start()

    gin_copy.start()

    @pl.when(seg > 0)
    def _():
        tap_grads()

    if relay:
        total = kg_ref[:, kg_window]
        for by in range(1, n_mp):
            sender = lax.rem(mp + n_mp - by, n_mp)
            kg_copy(mp, sender).wait_recv()
            total = total + kg_land[sender]
        scale = (frames * n_mp) ** (-0.5)
        even, odd = total[:taps, :own], total[:taps, 2 * LANES - own :]
        kg_out[0] = jnp.where(column == 0, even, odd) * scale
        for by in range(1, n_mp):
            kg_copy(lax.rem(mp + by, n_mp), mp).wait_send()
        passed()
    else:
        kg_out[0] = kg_ref[:taps, :]

    out_copy.wait()
    gin_copy.wait()
    halo_sent(pm, 0)
    halo_sent(pg, 2)

    @pl.when(seg < n_seg - 1)
    def _():
        for tile in range(tiles):
            in_copy(tile).wait_send()

    @pl.when(seg > 0)
    def _():
        for block in range(blocks):
            up_copy(block).wait_send()


def on_device(frames_in, section_weights, conv_kernels, valid_length, out_cotangent):
    frames, width = frames_in.shape
    taps = conv_kernels.shape[1]
    n_mp = lax.axis_size("mp")
    own = width // n_mp
    if width == 1536 and n_mp == 8 and frames == 128:
        return spread_call(frames_in, section_weights, conv_kernels, valid_length, out_cotangent)
    relay = False
    weight = section_weights[0]
    if not relay:
        weight = lax.all_gather(weight, "mp", axis=0, tiled=True)
    vmem = pl.BlockSpec(memory_space=pltpu.VMEM)
    smem = pl.BlockSpec(memory_space=pltpu.SMEM)
    whole = pl.BlockSpec(memory_space=pl.ANY)
    padded = (frames + 2 * PAD, width)
    tap_rows = -(-taps // 8) * 8
    dma = pltpu.SemaphoreType.DMA
    out, gin, grad = pl.pallas_call(
        functools.partial(cascade, relay),
        out_shape=(
            jax.ShapeDtypeStruct((1, frames, width), BF),
            jax.ShapeDtypeStruct((1, frames, width), BF),
            jax.ShapeDtypeStruct((1, taps, own if relay else width), F32),
        ),
        in_specs=[whole, whole, whole, smem, whole],
        out_specs=(whole, whole, vmem),
        scratch_shapes=[
            pltpu.VMEM((frames, width), BF),
            pltpu.VMEM((frames, width), BF),
            pltpu.VMEM((frames, width), F32),
            pltpu.VMEM((frames, LANES), F32),
            pltpu.VMEM(padded, BF),
            pltpu.VMEM(padded, BF),
            pltpu.VMEM((frames, width), BF),
            pltpu.VMEM((frames, width), F32),
            pltpu.VMEM((frames, width), F32),
            pltpu.VMEM((frames, width), BF),
            pltpu.VMEM((frames, width), BF),
            pltpu.VMEM((width, width), BF),
            pltpu.VMEM((taps, width), BF),
            pltpu.VMEM((taps, width), F32),
            pltpu.VMEM((tap_rows, width), F32),
            pltpu.VMEM((n_mp if relay else 1, tap_rows, 2 * LANES), F32),
            dma((4,)), dma((4,)),
            dma((width // WIDE,)), dma((width // WIDE,)),
            dma((frames // ROWS,)), dma((frames // ROWS,)),
            dma((6,)),
            dma((3, n_mp)), dma((n_mp,)), dma((2,)), dma((2,)), dma((n_mp,)), dma((n_mp,)),
            pltpu.SemaphoreType.REGULAR,
        ],
        compiler_params=pltpu.CompilerParams(
            collective_id=0, has_side_effects=True, vmem_limit_bytes=60 * 2**20
        ),
    )(frames_in, weight, conv_kernels[0], valid_length, out_cotangent)
    if not relay:
        grad = lax.psum_scatter(grad, "mp", scatter_dimension=2, tiled=True)
        grad = grad * (frames * n_mp) ** (-0.5)
    return (out, gin, grad)


def solution(mesh):
    in_specs = (
        P("mp", None),
        P("segment", "mp", None),
        P("segment", None, None),
        P(),
        P("mp", None),
    )
    out_specs = (P("segment", "mp", None), P("segment", "mp", None), P("segment", None, "mp"))
    return jax.shard_map(
        on_device, mesh=mesh, in_specs=in_specs, out_specs=out_specs, check_vma=False
    )
```
